32 devices in a mesh: seq: 4 (over z), expert: 8 (over y, x, core).
Axes of the slice: x: 2, y: 2, z: 4, core: 2. Of those that a mesh axis runs over, the one named last changes fastest.
Arguments:
- tokens: bfloat16 [8, 1024, 768], P('expert', 'seq'), may hold values from -6 to 6
- cotangent: bfloat16 [8, 1024, 768], P('expert', 'seq'), may hold values from -6 to 6
- segments: int32 [8, 1024], P('expert'), may hold values from 0 to 3, never falling along the last dimension, each value on 1 to 512 neighbouring positions
- buckets: int32 [1024], replicated, may hold values from 0 to 31, as said below
- routes: int32 [8, 1024, 2], P('expert', 'seq'), may hold values from 0 to 15, all different within a row; in each aligned block of 256 rows (0 to 255, 256 to 511, ..., all dimensions but the last counted through in order) at most 48 rows name the same one
- attend_in: bfloat16 [2, 768, 2304], P(None, ('seq', 'expert')), may hold values from -0.21875 to 0.21875
- attend_out: bfloat16 [2, 768, 768], P(None, ('seq', 'expert')), may hold values from -1.75 to 1.75
- router_weight: bfloat16 [2, 768, 16], P(None, ('seq', 'expert')), may hold values from -0.4375 to 0.4375
- gain_attend: bfloat16 [2, 768], P(None, ('seq', 'expert')), may hold values from 0.5 to 1.5
- gain_expert: bfloat16 [2, 768], P(None, ('seq', 'expert')), may hold values from 0.5 to 1.5
- bias_table: bfloat16 [2, 384], P(None, ('seq', 'expert')), may hold values from -4 to 4
- expert_in: bfloat16 [2, 16, 768, 3072], P(None, 'expert', None, 'seq'), may hold values from -0.21875 to 0.21875
- expert_out: bfloat16 [2, 16, 3072, 768], P(None, 'expert', 'seq'), may hold values from -0.109375 to 0.109375
Outputs:
- block_out: bfloat16 [8, 1024, 768], P('expert', 'seq')
- tokens_grad: bfloat16 [8, 1024, 768], P('expert', 'seq')
- attend_in_grad: float32 [2, 768, 2304], P(None, ('seq', 'expert'))
- attend_out_grad: float32 [2, 768, 768], P(None, ('seq', 'expert'))
- router_grad: float32 [2, 768, 16], P(None, ('seq', 'expert'))
- gain_attend_grad: float32 [2, 768], P(None, ('seq', 'expert'))
- gain_expert_grad: float32 [2, 768], P(None, ('seq', 'expert'))
- table_grad: float32 [2, 384], P(None, ('seq', 'expert'))
- expert_in_grad: float32 [2, 16, 768, 3072], P(None, 'expert', None, 'seq')
- expert_out_grad: float32 [2, 16, 3072, 768], P(None, 'expert', 'seq')
The draws below stay inside these ranges and needn't reach their ends.
Inputs may be any that keep to these rules, and one draw needn't show every extreme that they name: `routes`: in each aligned block of 256 positions of a sequence (the rows of one device) no expert is named more than 48 times; the two experts of a position differ. `segments`: document numbers never fall along a sequence; a document spans at most 512 positions. `buckets`: equal to the distance below 16, never falling as the distance grows.
All inputs are finite; a program needn't handle non-finite values.
Results may differ from the reference program's by a relative error of at most 0.024.
Values may be sent and summed in bfloat16 or wider, within the bound.
No kernel may reach another device: no remote copies, remote signals or barrier semaphores. Data moves between devices by JAX's collectives and lax.ppermute only.
A program may use at most 320 MiB of HBM per device.

```python
import math
from functools import partial
import jax
import jax.numpy as jnp
import numpy as np
from jax import lax

D = 768
H = 12
HD = 64
FF = 3072
BUCKETS = 32
LAYERS = 2
LEN = 1024
TOK_DEV = 256
SEQS = 8
EXPERTS = 16
CAP = 48


def draw_buckets(key, part):
    exact_span = BUCKETS // 2
    shuffled = jax.random.permutation(key, LEN - exact_span - 1)
    edge_points = shuffled[:BUCKETS - exact_span - 1] + exact_span + 1
    distance = jnp.arange(LEN, dtype=jnp.int32)
    passed_edges = jnp.sum((edge_points[None, :] <= distance[:, None]).astype(jnp.int32), axis=1)
    return jnp.where(distance < exact_span, distance, exact_span + passed_edges).astype(jnp.int32)


def with_spikes(entries, rng, source, target, shards_of, factor):
    def block_of(dim):
        return (jnp.arange(entries.shape[dim]) // (entries.shape[dim] // shards_of)).reshape((-1,) + (1,) * (entries.ndim - 1 - dim))

    first = jax.random.permutation(rng, shards_of)[block_of(target)]
    far = (block_of(target) + shards_of // 2) % shards_of
    return jnp.where((block_of(source) == first) | (block_of(source) == far), factor * entries, entries)


def levels(stream_key, shape, cuts, least, top_value):
    loudness = 1.0
    for axis_at, shards_of in cuts:
        steps = jax.random.uniform(jax.random.fold_in(jax.random.fold_in(stream_key, 6), axis_at), (shards_of,), jnp.float32, least / len(cuts), top_value / len(cuts))
        loudness = loudness * jnp.repeat(jnp.exp(steps), shape[axis_at] // shards_of).reshape((-1,) + (1,) * (len(shape) - 1 - axis_at))
    return loudness


def length_profile(number_of, total, reach, slope):
    portions = [(1 << 20) // math.isqrt(rank ** slope) + 1 for rank in range(2, number_of + 1)]
    rest, given = total - reach - (number_of - 1), [1] * (number_of - 1)
    while rest > 0:
        free = [i for i in range(number_of - 1) if given[i] < reach]
        mass, left = sum([portions[i] for i in free]), rest
        for i in free:
            extra = min(reach - given[i], max(1, left * portions[i] // mass), rest)
            given[i] = given[i] + extra
            rest = rest - extra
    return np.array([reach] + given)


def uneven_parts(key, count, total, reach, skew):
    if count == 2:
        one = jax.random.randint(key, (), max(1, total - reach), min(reach, total - 1) + 1)
        return jnp.stack([one, total - one])
    tallies = jnp.asarray(length_profile(count, total, reach, skew), jnp.int32)
    pairs = (count - 1) // 2
    source_of, receiver = tallies[1:1 + 2 * pairs:2], tallies[2:2 + 2 * pairs:2]
    room = jnp.minimum(source_of - 1, reach - receiver)
    moved = jax.random.randint(jax.random.fold_in(key, 1), (pairs,), 0, 1 << 20) % (room + 1)
    tallies = tallies.at[1:1 + 2 * pairs:2].set(source_of - moved).at[2:2 + 2 * pairs:2].set(receiver + moved)
    return tallies[jax.random.permutation(jax.random.fold_in(key, 2), count)]


def routed_block(rng, own, number, rows, amount, top, bound, skew):
    sequence = jax.random.permutation(rng, amount)
    heavy_load, usual = load_shares(amount, rows * top, bound, skew, True), load_shares(amount, rows * top, bound, skew, False)
    places = jnp.arange(amount)

    def named(tallies, turn):
        used = int((tallies > 0).sum())
        fixed = max(1, used // 4)
        shifted = fixed + (places - fixed + turn * (used - fixed)) % max(1, amount - fixed)
        return jnp.zeros((amount,), jnp.int32).at[sequence[jnp.where(places < fixed, places, shifted)]].set(jnp.asarray(tallies, jnp.int32))

    tallies = jnp.where(number % 4 == 0, named(heavy_load, number // 4), named(usual, number - number // 4 - 1))
    mixed = jax.random.permutation(jax.random.fold_in(own, 3), amount)
    source_of, sink = mixed[0:amount // 2 * 2:2], mixed[1:amount // 2 * 2:2]
    slack = jnp.minimum(tallies[source_of] - 1, bound - tallies[sink]) // 2
    slack = jnp.where((source_of == sequence[0]) | (sink == sequence[0]) | (tallies[sink] == 0), 0, jnp.maximum(slack, 0))
    shifted = jax.random.randint(jax.random.fold_in(own, 4), (amount // 2,), 0, 1 << 20) % (slack + 1)
    tallies = tallies.at[source_of].add(-shifted).at[sink].add(shifted)
    items = jnp.searchsorted(jnp.cumsum(tallies), jnp.arange(rows * top), side="right").astype(jnp.int32)
    grid = items.reshape(top, rows).T
    grid = grid[jax.random.permutation(jax.random.fold_in(own, 1), rows)]
    turn = jax.random.randint(jax.random.fold_in(own, 2), (rows, 1), 0, top)
    return jnp.take_along_axis(grid, (jnp.arange(top)[None, :] + turn) % top, axis=1)


def load_shares(amount, total, bound, skew, full):
    loads = [(1 << 20) // math.isqrt(standing ** skew) + 1 for standing in range(1, amount + 1)]
    largest = bound if full else min(bound, max(-(-total // amount), total * loads[0] // sum(loads)))
    least = 1 if total - largest >= amount - 1 else 0
    given, surplus = [largest] + [least] * (amount - 1), total - largest - least * (amount - 1)
    while surplus > 0:
        free = [i for i in range(1, amount) if given[i] < largest] or [i for i in range(1, amount) if given[i] < bound]
        pool, remaining = sum([loads[i] for i in free]), surplus
        for i in free:
            extra = min(bound - given[i], max(1, remaining * loads[i] // pool), surplus)
            given[i] = given[i] + extra
            surplus = surplus - extra
    return np.array(given)


def centred(own_key, extent, deviation, most, split=(), kind=jnp.bfloat16):
    level = levels(own_key, extent, split, -0.22, 0.18) if split else 1.0
    values = jax.random.normal(own_key, extent, jnp.float32) * deviation * level
    return jnp.minimum(jnp.maximum(values, -most), most).astype(kind)


def heavy_noise(rng, dims, width, bound, shards, heavy, kind=jnp.bfloat16):
    values = width * jax.random.normal(rng, dims, jnp.float32)
    if shards:
        values = values * levels(rng, dims, shards, -0.22, 0.18)
    return jnp.clip(with_spikes(values, jax.random.fold_in(rng, 3), *heavy), -bound, bound).astype(kind)


def setup_inputs(seed: int = 0) -> dict:
    streams_of = jax.random.split(jax.random.key(seed), 14)
    tokens = heavy_noise(streams_of[0], (SEQS, LEN, D), 1.0, 6.0, ((0, 8), (1, 4)), (0, 2, 8, 2.0))
    cotangent = centred(streams_of[1], (SEQS, LEN, D), 1.0, 6.0, ((0, 8), (1, 4)))
    segments = jax.vmap(lambda own: jnp.searchsorted(jnp.cumsum(uneven_parts(own, 4, LEN, LEN // 2, 0)), jnp.arange(LEN), side="right"))(jax.random.split(streams_of[2], SEQS)).reshape((SEQS, LEN)).astype(jnp.int32)
    buckets = draw_buckets(jax.random.fold_in(streams_of[13], 71), 0)
    routes_keys = jax.random.split(jax.random.fold_in(streams_of[4], 1), SEQS * LEN // TOK_DEV)
    routes_turns = jax.random.permutation(jax.random.fold_in(streams_of[4], 3), SEQS * LEN // TOK_DEV)
    routes = jax.vmap(lambda own, number: routed_block(jax.random.fold_in(streams_of[4], 2), own, number, TOK_DEV, EXPERTS, 2, CAP, 2))(routes_keys, routes_turns).reshape((SEQS, LEN, 2))
    attend_in = centred(streams_of[5], (LAYERS, D, 3 * D), D ** -0.5, 0.21875, ((1, 32),))
    attend_out = centred(streams_of[6], (LAYERS, D, D), (D // 64) ** -0.5, 1.75, ((1, 32),))
    router_weight = centred(streams_of[7], (LAYERS, D, EXPERTS), (D // 4) ** -0.5, 0.4375, ((1, 32),))
    gain_attend = jnp.clip(1.0 + 0.1 * jax.random.normal(streams_of[8], (LAYERS, D), jnp.float32), 0.5, 1.5).astype(jnp.bfloat16)
    gain_expert = jnp.clip(1.0 + 0.1 * jax.random.normal(streams_of[9], (LAYERS, D), jnp.float32), 0.5, 1.5).astype(jnp.bfloat16)
    bias_table = centred(streams_of[10], (LAYERS, H * BUCKETS), 1.0, 4.0, ((1, 32),))
    expert_in = centred(streams_of[11], (LAYERS, EXPERTS, D, FF), D ** -0.5, 0.21875, ((1, 8), (3, 4)))
    expert_out = centred(streams_of[12], (LAYERS, EXPERTS, FF, D), FF ** -0.5, 0.109375, ((1, 8), (2, 4)))
    return {"tokens": tokens, "cotangent": cotangent, "segments": segments, "buckets": buckets, "routes": routes, "attend_in": attend_in, "attend_out": attend_out, "router_weight": router_weight, "gain_attend": gain_attend, "gain_expert": gain_expert, "bias_table": bias_table, "expert_in": expert_in, "expert_out": expert_out}


norm_eps = 1e-06
masked_score = -1000000000.0

@jax.custom_vjp
def low(v):
    return lax.optimization_barrier(v.astype(jnp.bfloat16)).astype(jnp.float32)

@jax.custom_vjp
def low_back(v):
    return v

def low_keep(v):
    return (low(v), None)

def low_pass(kept, grad):
    return (grad,)

def back_keep(v):
    return (v, None)

def back_low(kept, grad):
    return (low(grad),)
low.defvjp(low_keep, low_pass)
low_back.defvjp(back_keep, back_low)

def exact_dot(left, right):
    return jnp.dot(left, right, precision=lax.Precision.HIGHEST, preferred_element_type=jnp.float32)

def rms_norm(stream, gain_vec):
    inverse = lax.rsqrt(lax.optimization_barrier(jnp.mean(stream * stream, axis=-1, keepdims=True)) + norm_eps)
    return stream * inverse * gain_vec

def slot_places(route_rows, experts):
    flat_routes = route_rows.reshape(-1)
    onehot = (flat_routes[:, None] == jnp.arange(experts, dtype=jnp.int32)[None, :]).astype(jnp.int32)
    before = jnp.cumsum(onehot, axis=0) - onehot
    position = lax.optimization_barrier(jnp.sum(before * onehot, axis=1))
    return (position * experts + flat_routes).reshape(route_rows.shape)

def attend_sequence(normed, seg_row, buckets, w_attend_in, w_attend_out, bias_rows):
    qkv_rows = low(low_back(exact_dot(normed, w_attend_in)))
    queries = qkv_rows[:, :D].reshape(LEN, H, HD)
    key_rows = qkv_rows[:, D:2 * D].reshape(LEN, H, HD)
    value_rows = qkv_rows[:, 2 * D:].reshape(LEN, H, HD)
    places = jnp.arange(LEN, dtype=jnp.int32)
    distance = places[:, None] - places[None, :]
    allowed = (distance >= 0) & (seg_row[:, None] == seg_row[None, :])
    bias_grid = bias_rows[:, buckets[jnp.clip(distance, 0, LEN - 1)]]
    raw_scores = jnp.einsum('qhd,khd->hqk', queries, key_rows, precision=lax.Precision.HIGHEST)
    scores = low_back(raw_scores * (1.0 / math.sqrt(HD)) + bias_grid)
    scores = jnp.where(allowed[None], scores, masked_score)
    soft_weights = low(jax.nn.softmax(scores, axis=-1))
    mixed_heads = jnp.einsum('hqk,khd->qhd', soft_weights, value_rows, precision=lax.Precision.HIGHEST).reshape(LEN, D)
    mixed_heads = low(low_back(mixed_heads))
    return low_back(exact_dot(mixed_heads, w_attend_out))

def expert_apply(inputs_expert):
    slot_rows, first_w, second_w = inputs_expert
    pre_act = low_back(exact_dot(slot_rows, first_w))
    hidden = low(jax.nn.gelu(pre_act))
    return low(low_back(exact_dot(hidden, second_w)))

def layer_step(stream, segments, buckets, routes, slot_place, w_attend_in, w_attend_out, w_router, gain_first, gain_second, bias_rows, first_all, second_all):
    normed = low(rms_norm(stream, gain_first))

    def one_sequence(seq_inputs):
        return attend_sequence(seq_inputs[0], seq_inputs[1], buckets, w_attend_in, w_attend_out, bias_rows)
    attended = lax.map(jax.checkpoint(one_sequence), (normed, segments))
    stream_mid = stream + attended
    normed_mid = low(rms_norm(stream_mid, gain_second))
    logits = exact_dot(normed_mid, w_router)
    route_hot = routes[..., None] == jnp.arange(EXPERTS, dtype=jnp.int32)
    chosen = lax.optimization_barrier(jnp.sum(jnp.where(route_hot, logits[:, :, None, :], 0.0), axis=-1))
    gate_weights = jax.nn.softmax(chosen, axis=-1)
    blocks = normed_mid.reshape(-1, TOK_DEV, D)
    block_count = blocks.shape[0]
    paired = jnp.repeat(blocks, 2, axis=1)
    empty = jnp.zeros((block_count, CAP * EXPERTS, D), jnp.float32)
    buffer = jax.vmap(lambda empty_rows, where_rows, tok_rows: empty_rows.at[where_rows].set(tok_rows))(empty, slot_place.reshape(block_count, -1), paired)
    buffer = low_back(buffer)
    per_expert = jnp.transpose(buffer.reshape(block_count * CAP, EXPERTS, D), (1, 0, 2))
    results = lax.map(jax.checkpoint(expert_apply), (per_expert, first_all, second_all))
    results = jnp.transpose(results, (1, 0, 2)).reshape(block_count, CAP * EXPERTS, D)
    picked = jax.vmap(lambda rows_of, places_of: rows_of[places_of])(results, slot_place)
    mixture = lax.optimization_barrier(jnp.sum(gate_weights.reshape(block_count, TOK_DEV, 2, 1) * picked, axis=2))
    return stream_mid + mixture.reshape(stream.shape)

def reference(tokens, cotangent, segments, buckets, routes, attend_in, attend_out, router_weight, gain_attend, gain_expert, bias_table, expert_in, expert_out):
    slot_place = jax.vmap(partial(slot_places, experts=EXPERTS))(routes.reshape(-1, TOK_DEV, 2))

    def forward(stream, w_attend_in, w_attend_out, w_router, gain_first, gain_second, bias_all, first_all, second_all):
        for layer_idx in range(LAYERS):
            stream = layer_step(stream, segments, buckets, routes, slot_place, w_attend_in[layer_idx], w_attend_out[layer_idx], w_router[layer_idx], gain_first[layer_idx], gain_second[layer_idx], bias_all[layer_idx].reshape(H, BUCKETS), first_all[layer_idx], second_all[layer_idx])
        return stream
    result, pull = jax.vjp(forward, tokens.astype(jnp.float32), attend_in.astype(jnp.float32), attend_out.astype(jnp.float32), router_weight.astype(jnp.float32), gain_attend.astype(jnp.float32), gain_expert.astype(jnp.float32), bias_table.astype(jnp.float32), expert_in.astype(jnp.float32), expert_out.astype(jnp.float32))
    grads = pull(cotangent.astype(jnp.float32))
    return (result.astype(jnp.bfloat16), grads[0].astype(jnp.bfloat16), grads[1], grads[2], grads[3], grads[4], grads[5], grads[6], grads[7], grads[8])
```

```python
from functools import partial
import math

import jax
import jax.numpy as jnp
from jax import lax
from jax.experimental import pallas as pl
from jax.experimental.pallas import tpu as pltpu
from jax.sharding import PartitionSpec as P

HD = 64
BLK = 256
BACK = 3
CHUNKS = 2
NORM_EPS = 1e-06
MASKED = -1000000000.0
BF = jnp.bfloat16
F32 = jnp.float32


def fdot(left, right, dims=((1,), (0,))):
    return lax.dot_general(left, right, (dims, ((), ())), preferred_element_type=F32)


def exact_dot(left, right):
    return jnp.dot(left, right, precision=lax.Precision.HIGHEST, preferred_element_type=F32)


def toeplitz_rows(rev_ref, head, back, length):
    start = length - BLK * back
    line = jnp.concatenate(
        [rev_ref[head : head + 1, start : start + BLK], rev_ref[head : head + 1, start - BLK : start]],
        axis=1,
    )
    rows = jnp.broadcast_to(line, (8, 2 * BLK))
    row_id = lax.broadcasted_iota(jnp.int32, rows.shape, 0)
    for bit in (1, 2, 4):
        rows = jnp.where((row_id & bit) != 0, pltpu.roll(rows, bit, 1), rows)
    size = 8
    while size < BLK:
        rows = jnp.concatenate([rows, pltpu.roll(rows, size, 1)], axis=0)
        size *= 2
    return rows[:, :BLK]


def toeplitz_fold(grid):
    rows = jnp.concatenate([grid, jnp.zeros_like(grid)], axis=1)
    width = 2 * BLK
    size = BLK // 2
    while size >= 8:
        rows = rows[:size] + pltpu.roll(rows[size:], width - size, 1)
        size //= 2
    row_id = lax.broadcasted_iota(jnp.int32, rows.shape, 0)
    for bit in (1, 2, 4):
        rows = jnp.where((row_id & bit) != 0, pltpu.roll(rows, width - bit, 1), rows)
    return jnp.sum(rows, axis=0, keepdims=True)


def key_span(query_block):
    return list(range(max(0, query_block - BACK + 1), query_block + 1))


def allowed_mask(segcol_ref, segrow_ref, query_block):
    span = key_span(query_block)
    first = span[0] * BLK
    own = segcol_ref[query_block * BLK : (query_block + 1) * BLK, :]
    theirs = segrow_ref[:, first : (query_block + 1) * BLK]
    same = own == theirs
    shape = (BLK, len(span) * BLK)
    rows = lax.broadcasted_iota(jnp.int32, shape, 0) + query_block * BLK
    cols = lax.broadcasted_iota(jnp.int32, shape, 1) + first
    return same & (cols <= rows)


def head_cols(part, head, width):
    return slice(part * width + head * HD, part * width + (head + 1) * HD)


def block_of(refs, per_chunk, block, cols):
    inner = block % per_chunk
    return refs[block // per_chunk][inner * BLK : (inner + 1) * BLK, cols]


def attend_fwd_kernel(chunk, per_chunk, heads, length, rev_ref, segcol_ref, segrow_ref, *rest):
    qkv_refs, out_ref, grid_ref = rest[: chunk + 1], rest[chunk + 1], rest[chunk + 2]
    width = heads * HD
    backs = min(BACK, (chunk + 1) * per_chunk)
    for head in range(heads):
        for back in range(backs):
            grid_ref[head * BACK + back] = toeplitz_rows(rev_ref, head, back, length)
    for inner in range(per_chunk):
        query_block = chunk * per_chunk + inner
        span = key_span(query_block)
        allowed = allowed_mask(segcol_ref, segrow_ref, query_block)
        for head in range(heads):
            query = block_of(qkv_refs, per_chunk, query_block, head_cols(0, head, width))
            scores = jnp.concatenate(
                [
                    fdot(query, block_of(qkv_refs, per_chunk, kb, head_cols(1, head, width)), ((1,), (1,)))
                    * (1.0 / math.sqrt(HD))
                    + grid_ref[head * BACK + query_block - kb]
                    for kb in span
                ],
                axis=1,
            )
            scores = jnp.where(allowed, scores, MASKED)
            top = jnp.max(scores, axis=1, keepdims=True)
            weights = jnp.exp(scores - top)
            weights = weights * (1.0 / jnp.sum(weights, axis=1, keepdims=True))
            probs = weights.astype(BF)
            mixed = sum(
                fdot(
                    probs[:, pos * BLK : (pos + 1) * BLK],
                    block_of(qkv_refs, per_chunk, kb, head_cols(2, head, width)),
                )
                for pos, kb in enumerate(span)
            )
            out_ref[inner * BLK : (inner + 1) * BLK, head * HD : (head + 1) * HD] = mixed.astype(BF)


def attend_bwd_kernel(
    chunk, per_chunk, heads, length, has_acc, rev_ref, segcol_ref, segrow_ref, dmix_ref, *rest
):
    rest = list(rest)
    qkv_refs = [rest.pop(0) for _ in range(chunk + 1)]
    acc_in = [rest.pop(0) for _ in range(chunk + 1)] if has_acc else None
    dqkv_ref = rest.pop(0)
    fold_ref = rest.pop(0)
    acc_out = [rest.pop(0) for _ in range(chunk)]
    grid_ref, dgrid_ref, own_acc = rest
    width = heads * HD
    backs = min(BACK, (chunk + 1) * per_chunk)
    accs = acc_out + [own_acc]
    for pos, acc in enumerate(accs):
        acc[...] = acc_in[pos][...] if has_acc else jnp.zeros_like(acc)
    dgrid_ref[...] = jnp.zeros_like(dgrid_ref)
    for head in range(heads):
        for back in range(backs):
            grid_ref[head * BACK + back] = toeplitz_rows(rev_ref, head, back, length)
    scale = 1.0 / math.sqrt(HD)
    for inner in range(per_chunk):
        query_block = chunk * per_chunk + inner
        own_rows = slice(inner * BLK, (inner + 1) * BLK)
        span = key_span(query_block)
        allowed = allowed_mask(segcol_ref, segrow_ref, query_block)
        for head in range(heads):
            query = block_of(qkv_refs, per_chunk, query_block, head_cols(0, head, width))
            keys = [block_of(qkv_refs, per_chunk, kb, head_cols(1, head, width)) for kb in span]
            values = [block_of(qkv_refs, per_chunk, kb, head_cols(2, head, width)) for kb in span]
            d_mixed = dmix_ref[own_rows, head * HD : (head + 1) * HD]
            scores = jnp.concatenate(
                [
                    fdot(query, key, ((1,), (1,))) * scale + grid_ref[head * BACK + query_block - kb]
                    for key, kb in zip(keys, span)
                ],
                axis=1,
            )
            scores = jnp.where(allowed, scores, MASKED)
            top = jnp.max(scores, axis=1, keepdims=True)
            weights = jnp.exp(scores - top)
            weights = weights * (1.0 / jnp.sum(weights, axis=1, keepdims=True))
            d_soft = jnp.concatenate([fdot(d_mixed, value, ((1,), (1,))) for value in values], axis=1)
            inner_sum = jnp.sum(d_soft * weights, axis=1, keepdims=True)
            d_scores = (weights * (d_soft - inner_sum)).astype(BF)
            probs = weights.astype(BF)
            d_query = jnp.zeros((BLK, HD), F32)
            for pos, kb in enumerate(span):
                cols = slice(pos * BLK, (pos + 1) * BLK)
                piece = d_scores[:, cols]
                d_query = d_query + fdot(piece, keys[pos])
                dgrid_ref[head * BACK + query_block - kb] += piece.astype(F32)
                acc = accs[kb // per_chunk]
                rows = slice((kb % per_chunk) * BLK, (kb % per_chunk + 1) * BLK)
                acc[rows, head_cols(0, head, width)] += fdot(piece, query, ((0,), (0,))) * scale
                acc[rows, head_cols(1, head, width)] += fdot(probs[:, cols], d_mixed, ((0,), (0,)))
            dqkv_ref[own_rows, head_cols(0, head, width)] = (d_query * scale).astype(BF)
    dqkv_ref[:, width : 3 * width] = own_acc[...].astype(BF)
    for slot in range(heads * BACK):
        fold_ref[slot : slot + 1, :] = toeplitz_fold(dgrid_ref[slot])


VM = pl.BlockSpec(memory_space=pltpu.VMEM)


def attend_forward(chunk, rev_bias, segcol, segrow, qkv_list):
    rows, width3 = qkv_list[0].shape
    heads = width3 // (3 * HD)
    length = segrow.shape[1]
    return pl.pallas_call(
        partial(attend_fwd_kernel, chunk, rows // BLK, heads, length),
        out_shape=jax.ShapeDtypeStruct((rows, heads * HD), BF),
        in_specs=[VM] * (3 + chunk + 1),
        out_specs=VM,
        scratch_shapes=[pltpu.VMEM((heads * BACK, BLK, BLK), F32)],
        cost_estimate=pl.CostEstimate(flops=int(2e9), bytes_accessed=int(4e6), transcendentals=int(2e6)),
        name="attend_fwd",
    )(rev_bias, segcol, segrow, *qkv_list[: chunk + 1])


def attend_backward(chunk, rev_bias, segcol, segrow, d_mixed, qkv_list, acc_list):
    rows, width3 = qkv_list[0].shape
    heads = width3 // (3 * HD)
    length = segrow.shape[1]
    acc_shape = (rows, 2 * heads * HD)
    has_acc = acc_list is not None
    args = [rev_bias, segcol, segrow, d_mixed, *qkv_list[: chunk + 1]]
    if has_acc:
        args += list(acc_list)
    outs = pl.pallas_call(
        partial(attend_bwd_kernel, chunk, rows // BLK, heads, length, has_acc),
        out_shape=[
            jax.ShapeDtypeStruct((rows, width3), BF),
            jax.ShapeDtypeStruct((heads * BACK, 2 * BLK), F32),
        ]
        + [jax.ShapeDtypeStruct(acc_shape, F32)] * chunk,
        in_specs=[VM] * len(args),
        out_specs=[VM] * (2 + chunk),
        scratch_shapes=[
            pltpu.VMEM((heads * BACK, BLK, BLK), F32),
            pltpu.VMEM((heads * BACK, BLK, BLK), F32),
            pltpu.VMEM(acc_shape, F32),
        ],
        cost_estimate=pl.CostEstimate(flops=int(5e9), bytes_accessed=int(8e6), transcendentals=int(2e6)),
        name="attend_bwd",
    )(*args)
    return outs[0], outs[1], list(outs[2:])


def dispatch_kernel(experts_dev, cap, weighted, code_ref, *rest):
    if weighted:
        gate_ref, x_ref, *outs = rest
    else:
        x_ref, *outs = rest
    slots = experts_dev * cap * 2
    slot_id = lax.broadcasted_iota(jnp.int32, (slots, BLK), 0)
    first = slot_id == code_ref[0, 0:1, :]
    second = slot_id == code_ref[0, 1:2, :]
    pick = jnp.where(first | second, 1.0, 0.0).astype(BF)
    rows = fdot(pick, x_ref[...].astype(BF))
    if weighted:
        gate = jnp.sum(
            jnp.where(first, gate_ref[0, 0:1, :], 0.0) + jnp.where(second, gate_ref[0, 1:2, :], 0.0),
            axis=1,
            keepdims=True,
        )
        rows = rows * gate
    rows = rows.astype(BF)
    half = slots // 2
    for local, out in enumerate(outs):
        for dest in range(experts_dev):
            out[dest, 0] = rows[local * half + dest * cap : local * half + (dest + 1) * cap]


def dispatch(x, code_row, gate_row, experts_dev, cap):
    tokens, width = x.shape
    blocks = tokens // BLK
    if cap % 16 != 0:
        slots = jnp.arange(2 * experts_dev * cap, dtype=jnp.int32)
        match = code_row[:, :, None, :] == slots[None, None, :, None]
        if gate_row is None:
            pick = jnp.sum(match.astype(F32), axis=1)
        else:
            pick = jnp.sum(jnp.where(match, gate_row[:, :, None, :], 0.0), axis=1)
        rows = jnp.einsum("bst,btd->bsd", pick, x.reshape(blocks, BLK, width).astype(F32),
                          precision=lax.Precision.HIGHEST).astype(BF)
        rows = rows.reshape(blocks, 2, experts_dev, cap, width)
        return tuple(jnp.transpose(rows[:, loc], (1, 0, 2, 3)) for loc in range(2))
    code_spec = pl.BlockSpec((1, 2, BLK), lambda b: (b, 0, 0))
    args, specs = [code_row], [code_spec]
    if gate_row is not None:
        args.append(gate_row)
        specs.append(code_spec)
    args.append(x)
    specs.append(pl.BlockSpec((BLK, width), lambda b: (b, 0)))
    shape = (experts_dev, blocks, cap, width)
    return tuple(
        pl.pallas_call(
            partial(dispatch_kernel, experts_dev, cap, gate_row is not None),
            grid=(blocks,),
            out_shape=[jax.ShapeDtypeStruct(shape, BF)] * 2,
            in_specs=specs,
            out_specs=[pl.BlockSpec((experts_dev, 1, cap, width), lambda b: (0, b, 0, 0))] * 2,
            cost_estimate=pl.CostEstimate(
                flops=int(2 * blocks * 768 * BLK * width), bytes_accessed=int(4e6), transcendentals=0
            ),
            name="dispatch",
        )(*args)
    )


def gather_rows(ref, experts_dev, cap):
    return jnp.concatenate([ref[dest, 0] for dest in range(experts_dev)], axis=0)


def combine_kernel(experts_dev, cap, weighted, code_ref, *rest):
    if weighted:
        gate_ref, r0_ref, r1_ref, out_ref = rest
    else:
        r0_ref, r1_ref, out_ref = rest
    half = experts_dev * cap
    slot_id = lax.broadcasted_iota(jnp.int32, (BLK, 2 * half), 1)
    g0 = gate_ref[:, 0:1] if weighted else 1.0
    g1 = gate_ref[:, 1:2] if weighted else 1.0
    pick = jnp.where(slot_id == code_ref[:, 0:1], g0, 0.0) + jnp.where(
        slot_id == code_ref[:, 1:2], g1, 0.0
    )
    pick = pick.astype(BF)
    total = fdot(pick[:, :half], gather_rows(r0_ref, experts_dev, cap)) + fdot(
        pick[:, half:], gather_rows(r1_ref, experts_dev, cap)
    )
    out_ref[...] = total.astype(out_ref.dtype)


def combine(rows_pair, code_col, gates, experts_dev, cap, out_dtype):
    tokens = code_col.shape[0]
    blocks = tokens // BLK
    width = rows_pair[0].shape[-1]
    if cap % 16 != 0:
        slots = jnp.arange(2 * experts_dev * cap, dtype=jnp.int32)
        match = code_col[:, :, None] == slots
        weight = jnp.where(match, 1.0 if gates is None else gates[:, :, None], 0.0).sum(axis=1)
        rows = jnp.concatenate(
            [jnp.transpose(r, (1, 0, 2, 3)).reshape(blocks, -1, width) for r in rows_pair], axis=1
        )
        out = jnp.einsum("bts,bsd->btd", weight.reshape(blocks, BLK, -1), rows.astype(F32),
                         precision=lax.Precision.HIGHEST)
        return out.reshape(tokens, width).astype(out_dtype)
    row_spec = pl.BlockSpec((experts_dev, 1, cap, width), lambda b: (0, b, 0, 0))
    col_spec = pl.BlockSpec((BLK, 2), lambda b: (b, 0))
    args, specs = [code_col], [col_spec]
    if gates is not None:
        args.append(gates)
        specs.append(col_spec)
    return pl.pallas_call(
        partial(combine_kernel, experts_dev, cap, gates is not None),
        grid=(blocks,),
        out_shape=jax.ShapeDtypeStruct((tokens, width), out_dtype),
        in_specs=specs + [row_spec] * 2,
        out_specs=pl.BlockSpec((BLK, width), lambda b: (b, 0)),
        cost_estimate=pl.CostEstimate(
            flops=int(2 * blocks * 768 * BLK * width), bytes_accessed=int(4e6), transcendentals=0
        ),
        name="combine",
    )(*args, *rows_pair)


def gate_grad_kernel(experts_dev, cap, code_ref, g_ref, r0_ref, r1_ref, out_ref):
    half = experts_dev * cap
    upstream = g_ref[...].astype(BF)
    dots = jnp.concatenate(
        [fdot(upstream, gather_rows(r, experts_dev, cap), ((1,), (1,))) for r in (r0_ref, r1_ref)],
        axis=1,
    )
    slot_id = lax.broadcasted_iota(jnp.int32, (BLK, 2 * half), 1)
    for k in range(2):
        out_ref[:, k : k + 1] = jnp.sum(
            jnp.where(slot_id == code_ref[:, k : k + 1], dots, 0.0), axis=1, keepdims=True
        )


def gate_grad(g2, rows_pair, code_col, experts_dev, cap):
    tokens, width = g2.shape
    blocks = tokens // BLK
    if cap % 16 != 0:
        slots = jnp.arange(2 * experts_dev * cap, dtype=jnp.int32)
        match = code_col[:, :, None] == slots
        rows = jnp.concatenate(
            [jnp.transpose(r, (1, 0, 2, 3)).reshape(blocks, -1, width) for r in rows_pair], axis=1
        )
        dots = jnp.einsum("btd,bsd->bts", g2.reshape(blocks, BLK, width), rows.astype(F32),
                          precision=lax.Precision.HIGHEST)
        return jnp.sum(jnp.where(match, dots.reshape(tokens, 1, -1), 0.0), axis=2)
    row_spec = pl.BlockSpec((experts_dev, 1, cap, width), lambda b: (0, b, 0, 0))
    col_spec = pl.BlockSpec((BLK, 2), lambda b: (b, 0))
    return pl.pallas_call(
        partial(gate_grad_kernel, experts_dev, cap),
        grid=(blocks,),
        out_shape=jax.ShapeDtypeStruct((tokens, 2), F32),
        in_specs=[col_spec, pl.BlockSpec((BLK, width), lambda b: (b, 0)), row_spec, row_spec],
        out_specs=col_spec,
        cost_estimate=pl.CostEstimate(
            flops=int(2 * blocks * 768 * BLK * width), bytes_accessed=int(4e6), transcendentals=0
        ),
        name="gate_grad",
    )(code_col, g2, *rows_pair)


def norm_forward(stream, gain):
    inverse = lax.rsqrt(jnp.mean(stream * stream, axis=-1, keepdims=True) + NORM_EPS)
    return (stream * inverse * gain).astype(BF), inverse


def norm_backward(stream, inverse, gain, upstream):
    scaled = upstream * gain
    inner_mean = jnp.mean(scaled * stream, axis=-1, keepdims=True)
    d_stream = inverse * scaled - stream * (inverse * inverse * inverse) * inner_mean
    return d_stream, jnp.sum(upstream * stream * inverse, axis=0)


def slot_codes(routes, experts, experts_dev, cap):
    blocks = routes.shape[0] // BLK
    flat = routes.reshape(blocks, BLK * 2)
    onehot = (flat[:, :, None] == jnp.arange(experts, dtype=jnp.int32)).astype(F32)
    steps = jnp.arange(BLK * 2, dtype=jnp.int32)
    before = (steps[:, None] > steps[None, :]).astype(F32)
    count = jnp.einsum("ij,bje->bie", before, onehot, preferred_element_type=F32)
    place = jnp.sum(count * onehot, axis=2).astype(jnp.int32)
    code = (flat % 2) * (experts_dev * cap) + (flat // 2) * cap + place
    return code.reshape(blocks * BLK, 2)


def spread(x, axis_name):
    return lax.all_to_all(x, axis_name, split_axis=0, concat_axis=0, tiled=True)


def body(
    tokens,
    cotangent,
    segments,
    buckets,
    routes,
    attend_in,
    attend_out,
    router_weight,
    gain_attend,
    gain_expert,
    bias_table,
    expert_in,
    expert_out,
):
    zs = lax.axis_size("seq")
    es = lax.axis_size("expert")
    z_id = lax.axis_index("seq")
    own_rows, width = tokens.shape[1:]
    length = segments.shape[1]
    layers, shard_rows = attend_in.shape[:2]
    experts = router_weight.shape[2]
    cap = 3 * own_rows // experts
    heads_all = width // HD
    heads = heads_all // zs
    hw = heads * HD
    bucket_count = bias_table.shape[1] * zs * es // heads_all
    chunks = CHUNKS
    rows_c = length // chunks

    def split(x):
        return [x[c * rows_c : (c + 1) * rows_c] for c in range(chunks)]

    route_rows = routes[0].astype(BF).reshape(-1, width) if (own_rows * 2) % width == 0 else None
    if route_rows is None:
        flat_routes = routes[0].astype(BF).reshape(-1)
        pad = -flat_routes.shape[0] % (16 * width)
        route_rows = jnp.pad(flat_routes, (0, pad)).reshape(-1, width)
    packed = lax.all_gather(jnp.concatenate([tokens[0], route_rows], axis=0), "seq", axis=0)
    stream_full = packed[:, :own_rows].reshape(length, width)
    routes_full = (
        packed[:, own_rows:].reshape(zs, -1)[:, : own_rows * 2].reshape(length, 2).astype(jnp.int32)
    )

    small = jnp.concatenate(
        [
            gain_attend.reshape(-1),
            gain_expert.reshape(-1),
            bias_table.reshape(-1),
            router_weight.reshape(-1),
        ]
    )
    small = lax.all_gather(small, ("seq", "expert"), axis=0)
    sizes = [layers * shard_rows, layers * shard_rows, layers * bias_table.shape[1]]
    at = 0
    parts = []
    for size in sizes:
        parts.append(small[:, at : at + size])
        at += size
    gains_a = jnp.transpose(parts[0].reshape(-1, layers, shard_rows), (1, 0, 2)).reshape(layers, width)
    gains_e = jnp.transpose(parts[1].reshape(-1, layers, shard_rows), (1, 0, 2)).reshape(layers, width)
    bias_all = jnp.transpose(
        parts[2].reshape(-1, layers, bias_table.shape[1]), (1, 0, 2)
    ).reshape(layers, heads_all, bucket_count)
    routers = jnp.transpose(
        small[:, at:].reshape(-1, layers, shard_rows, experts), (1, 0, 2, 3)
    ).reshape(layers, width, experts)
    gains_a = gains_a.astype(F32)
    gains_e = gains_e.astype(F32)

    w_in_list, w_out_list = [], []
    for layer in range(layers):
        piece = attend_in[layer].reshape(shard_rows, 3, zs, hw)
        piece = jnp.transpose(piece, (2, 0, 1, 3)).reshape(zs, shard_rows, 3 * hw)
        piece = spread(piece, "seq")
        piece = lax.all_gather(piece, "expert", axis=1, tiled=True)
        w_in_list.append(piece.reshape(width, 3 * hw))
        w_out_list.append(lax.all_gather(attend_out[layer], ("seq", "expert"), axis=0, tiled=True))

    upstream_full = lax.all_gather(cotangent[0], "seq", axis=0, tiled=True)

    steps = length - jnp.arange(length + BLK, dtype=jnp.int32)
    rev_buckets = jnp.concatenate(
        [buckets[length - 1 :], buckets[::-1], jnp.broadcast_to(buckets[:1], (BLK - 1,))]
    )
    rev_hot = (rev_buckets[:, None] == jnp.arange(bucket_count, dtype=jnp.int32)).astype(F32)
    segrow = segments
    segcol = segments.reshape(length, 1)

    code_full = slot_codes(routes_full, experts, es, cap)
    code_col = split(code_full)
    code_row_full = jnp.transpose(code_full.reshape(-1, BLK, 2), (0, 2, 1))
    blocks_c = rows_c // BLK
    code_row = [code_row_full[c * blocks_c : (c + 1) * blocks_c] for c in range(chunks)]
    route_hot = split(routes_full[..., None] == jnp.arange(experts, dtype=jnp.int32))

    def exchange(pair):
        return [
            spread(r.reshape(es, -1, width), "expert").reshape(-1, width) for r in pair
        ]

    def exchange_back(pair):
        return [
            spread(r.reshape(es, -1, width), "expert").reshape(es, blocks_c, cap, width) for r in pair
        ]

    stream = split(stream_full.astype(F32))
    saved = []
    block_out = None
    for layer in range(layers):
        w_in, w_out = w_in_list[layer], w_out_list[layer]
        local_bias = lax.dynamic_slice_in_dim(bias_all[layer], z_id * heads, heads, 0)
        rev_bias = fdot(local_bias, rev_hot.astype(BF), ((1,), (1,)))
        w_out_heads = w_out.reshape(zs, hw, width)
        keep = dict(stream=stream, rev_bias=rev_bias, chunks=[])
        qkv = []
        mids, partials = [], []
        for c in range(chunks):
            normed, inv_a = norm_forward(stream[c], gains_a[layer])
            qkv.append(fdot(normed, w_in).astype(BF))
            mixed = attend_forward(c, rev_bias, segcol, segrow, qkv)
            mixed_all = lax.all_gather(mixed, "seq", axis=0)
            proj = jnp.einsum("ztd,zde->te", mixed_all, w_out_heads, preferred_element_type=F32)
            mid = stream[c] + proj
            normed_mid, inv_e = norm_forward(mid, gains_e[layer])
            logits = fdot(normed_mid, routers[layer])
            chosen = jnp.sum(jnp.where(route_hot[c], logits[:, None, :], 0.0), axis=-1)
            gates = jax.nn.softmax(chosen, axis=-1)
            rows = exchange(dispatch(normed_mid, code_row[c], None, es, cap))
            inner, hidden, result = [], [], []
            for loc in range(2):
                pre = fdot(rows[loc], expert_in[layer, loc])
                hid = jax.nn.gelu(pre).astype(BF)
                inner.append(pre)
                hidden.append(hid)
                result.append(fdot(hid, expert_out[layer, loc]).astype(BF))
            back = exchange_back(result)
            partials.append(combine(back, code_col[c], gates, es, cap, BF))
            mids.append(mid)
            keep["chunks"].append(
                dict(normed=normed, inv_a=inv_a, mixed=mixed, mid=mid, normed_mid=normed_mid,
                     inv_e=inv_e, gates=gates, rows=rows, inner=inner, hidden=hidden, back=back)
            )
        keep["qkv"] = qkv
        saved.append(keep)
        if layer + 1 < layers:
            stream = [mids[c] + lax.psum(partials[c], "seq").astype(F32) for c in range(chunks)]
        else:
            delta = lax.psum_scatter(
                jnp.concatenate(partials, axis=0), "seq", scatter_dimension=0, tiled=True
            )
            mid_own = lax.dynamic_slice_in_dim(
                jnp.concatenate(mids, axis=0), z_id * own_rows, own_rows, 0
            )
            block_out = (mid_own + delta.astype(F32)).astype(BF)

    upstream = split(upstream_full.astype(F32))
    in_grads, out_grads = [None] * layers, [None] * layers
    first_grads, second_grads = [None] * layers, [None] * layers
    small_grads = [None] * layers
    tokens_grad = None
    for layer in reversed(range(layers)):
        keep = saved[layer]
        w_in, w_out = w_in_list[layer], w_out_list[layer]
        w_out_own = lax.dynamic_slice_in_dim(w_out, z_id * hw, hw, 0)
        d_mids, d_parts = [None] * chunks, [None] * chunks
        total_in = total_out = total_router = total_ga = total_ge = total_fold = None
        g_first = [None, None]
        g_second = [None, None]
        acc = None

        def plus(left, right):
            return right if left is None else left + right

        for c in reversed(range(chunks)):
            k = keep["chunks"][c]
            g2 = upstream[c]
            gates = k["gates"]
            gate_row = jnp.transpose(gates.reshape(blocks_c, BLK, 2), (0, 2, 1))
            d_res = exchange(dispatch(g2, code_row[c], gate_row, es, cap))
            d_rows = []
            for loc in range(2):
                d_hid = fdot(d_res[loc], expert_out[layer, loc], ((1,), (1,)))
                _, pull = jax.vjp(jax.nn.gelu, k["inner"][loc])
                d_inner = pull(d_hid)[0].astype(BF)
                d_rows.append(fdot(d_inner, expert_in[layer, loc], ((1,), (1,))).astype(BF))
                g_second[loc] = plus(g_second[loc], fdot(k["hidden"][loc], d_res[loc], ((0,), (0,))))
                g_first[loc] = plus(g_first[loc], fdot(k["rows"][loc], d_inner, ((0,), (0,))))
            d_back = exchange_back(d_rows)
            d_gates = gate_grad(g2, k["back"], code_col[c], es, cap)
            d_chosen = gates * (d_gates - jnp.sum(gates * d_gates, axis=-1, keepdims=True))
            d_logits = jnp.sum(jnp.where(route_hot[c], d_chosen[..., None], 0.0), axis=1)
            total_router = plus(
                total_router, exact_dot(k["normed_mid"].astype(F32).T, d_logits)
            )
            partial_d = combine(d_back, code_col[c], None, es, cap, F32) + exact_dot(
                d_logits, routers[layer].astype(F32).T
            )
            d_normed_mid = lax.psum(partial_d.astype(BF), "seq").astype(F32)
            d_stream, ge = norm_backward(k["mid"], k["inv_e"], gains_e[layer], d_normed_mid)
            total_ge = plus(total_ge, ge)
            d_mid = g2 + d_stream
            d_proj = d_mid.astype(BF)
            total_out = plus(total_out, fdot(k["mixed"], d_proj, ((0,), (0,))))
            d_mixed = fdot(d_proj, w_out_own, ((1,), (1,))).astype(BF)
            d_qkv, fold, acc = attend_backward(
                c, keep["rev_bias"], segcol, segrow, d_mixed, keep["qkv"], acc
            )
            total_fold = plus(total_fold, fold)
            total_in = plus(total_in, fdot(k["normed"], d_qkv, ((0,), (0,))))
            d_parts[c] = fdot(d_qkv, w_in, ((1,), (1,))).astype(BF)
            d_mids[c] = d_mid
            if layer > 0:
                d_normed = lax.psum(d_parts[c], "seq").astype(F32)
                d_in, ga = norm_backward(keep["stream"][c], k["inv_a"], gains_a[layer], d_normed)
                total_ga = plus(total_ga, ga)
                upstream[c] = d_in + d_mid
        own = (jnp.arange(zs) == z_id).astype(F32)[:, None]
        if layer == 0:
            d_normed = lax.psum_scatter(
                jnp.concatenate(d_parts, axis=0), "seq", scatter_dimension=0, tiled=True
            ).astype(F32)

            def mine(items):
                return lax.dynamic_slice_in_dim(
                    jnp.concatenate(items, axis=0), z_id * own_rows, own_rows, 0
                )

            stream_own = mine(keep["stream"])
            inv_own = mine([keep["chunks"][c]["inv_a"] for c in range(chunks)])
            d_in, ga = norm_backward(stream_own, inv_own, gains_a[layer], d_normed)
            tokens_grad = (d_in + mine(d_mids)).astype(BF)
            gain_a_part = ga.reshape(zs, -1)
        else:
            gain_a_part = total_ga.reshape(zs, -1) * own
        gain_e_part = total_ge.reshape(zs, -1) * own
        fold = total_fold.reshape(heads, BACK, 2 * BLK)
        hot = jnp.stack(
            [
                jnp.concatenate(
                    [
                        rev_hot[length - BLK * back : length - BLK * (back - 1)],
                        rev_hot[length - BLK * (back + 1) : length - BLK * back],
                    ],
                    axis=0,
                )
                for back in range(BACK)
            ]
        )
        table = exact_dot(fold.reshape(heads, -1), hot.reshape(-1, bucket_count))
        table_part = table.reshape(1, -1) * own
        router_part = total_router.reshape(zs, es, shard_rows * experts)
        small_grads[layer] = jnp.concatenate(
            [
                router_part,
                gain_a_part.reshape(zs, es, -1),
                gain_e_part.reshape(zs, es, -1),
                table_part.reshape(zs, es, -1),
            ],
            axis=-1,
        )
        dense = jnp.concatenate(
            [
                jnp.transpose(total_in.reshape(zs, es, shard_rows, 3 * hw), (1, 2, 0, 3)).reshape(
                    es, shard_rows, zs * 3 * hw
                ),
                total_out.reshape(es, shard_rows, width),
            ],
            axis=2,
        ).astype(BF)
        dense = jnp.sum(spread(dense, "expert").astype(F32), axis=0)
        out_grads[layer] = dense[:, zs * 3 * hw :]
        piece = jnp.transpose(dense[:, : zs * 3 * hw].reshape(shard_rows, zs, 3 * hw), (1, 0, 2))
        piece = spread(piece.astype(BF), "seq").astype(F32)
        piece = jnp.transpose(piece.reshape(zs, shard_rows, 3, hw), (1, 2, 0, 3))
        in_grads[layer] = piece.reshape(shard_rows, 3 * width)
        first_grads[layer] = jnp.stack(g_first)
        second_grads[layer] = jnp.stack(g_second)

    packed_small = jnp.stack(small_grads, axis=2)
    packed_small = jnp.transpose(packed_small, (1, 0, 2, 3))
    packed_small = jnp.sum(spread(packed_small, "expert"), axis=0)
    packed_small = jnp.sum(spread(packed_small, "seq"), axis=0)
    r_size = shard_rows * experts
    router_grad = packed_small[:, :r_size].reshape(layers, shard_rows, experts)
    ga_grad = packed_small[:, r_size : r_size + shard_rows]
    ge_grad = packed_small[:, r_size + shard_rows : r_size + 2 * shard_rows]
    table_grad = packed_small[:, r_size + 2 * shard_rows :]
    return (
        block_out[None],
        tokens_grad[None],
        jnp.stack(in_grads),
        jnp.stack(out_grads),
        router_grad,
        ga_grad,
        ge_grad,
        table_grad,
        jnp.stack(first_grads),
        jnp.stack(second_grads),
    )


def solution(mesh):
    both = ("seq", "expert")
    return jax.shard_map(
        body,
        mesh=mesh,
        in_specs=(
            P("expert", "seq", None),
            P("expert", "seq", None),
            P("expert", None),
            P(),
            P("expert", "seq", None),
            P(None, both, None),
            P(None, both, None),
            P(None, both, None),
            P(None, both),
            P(None, both),
            P(None, both),
            P(None, "expert", None, "seq"),
            P(None, "expert", "seq", None),
        ),
        out_specs=(
            P("expert", "seq", None),
            P("expert", "seq", None),
            P(None, both, None),
            P(None, both, None),
            P(None, both, None),
            P(None, both),
            P(None, both),
            P(None, both),
            P(None, "expert", None, "seq"),
            P(None, "expert", "seq", None),
        ),
        check_vma=False,
    )
```

```python
from functools import partial
import math

import jax
import jax.numpy as jnp
from jax import lax
from jax.experimental import pallas as pl
from jax.experimental.pallas import tpu as pltpu
from jax.sharding import PartitionSpec as P

HD = 64
BLK = 256
BACK = 3
CHUNKS = 2
NORM_EPS = 1e-06
MASKED = -1000000000.0
BF = jnp.bfloat16
F32 = jnp.float32


def fdot(left, right, dims=((1,), (0,))):
    return lax.dot_general(left, right, (dims, ((), ())), preferred_element_type=F32)


def exact_dot(left, right):
    return jnp.dot(left, right, precision=lax.Precision.HIGHEST, preferred_element_type=F32)


def toeplitz_rows(rev_ref, head, back, length):
    start = length - BLK * back
    line = jnp.concatenate(
        [rev_ref[head : head + 1, start : start + BLK], rev_ref[head : head + 1, start - BLK : start]],
        axis=1,
    )
    rows = jnp.broadcast_to(line, (8, 2 * BLK))
    row_id = lax.broadcasted_iota(jnp.int32, rows.shape, 0)
    for bit in (1, 2, 4):
        rows = jnp.where((row_id & bit) != 0, pltpu.roll(rows, bit, 1), rows)
    size = 8
    while size < BLK:
        rows = jnp.concatenate([rows, pltpu.roll(rows, size, 1)], axis=0)
        size *= 2
    return rows[:, :BLK]


def toeplitz_fold(grid):
    rows = jnp.concatenate([grid, jnp.zeros_like(grid)], axis=1)
    width = 2 * BLK
    size = BLK // 2
    while size >= 8:
        rows = rows[:size] + pltpu.roll(rows[size:], width - size, 1)
        size //= 2
    row_id = lax.broadcasted_iota(jnp.int32, rows.shape, 0)
    for bit in (1, 2, 4):
        rows = jnp.where((row_id & bit) != 0, pltpu.roll(rows, width - bit, 1), rows)
    return jnp.sum(rows, axis=0, keepdims=True)


def key_span(query_block):
    return list(range(max(0, query_block - BACK + 1), query_block + 1))


def allowed_mask(segcol_ref, segrow_ref, query_block):
    span = key_span(query_block)
    first = span[0] * BLK
    own = segcol_ref[query_block * BLK : (query_block + 1) * BLK, :]
    theirs = segrow_ref[:, first : (query_block + 1) * BLK]
    same = own == theirs
    shape = (BLK, len(span) * BLK)
    rows = lax.broadcasted_iota(jnp.int32, shape, 0) + query_block * BLK
    cols = lax.broadcasted_iota(jnp.int32, shape, 1) + first
    return same & (cols <= rows)


def head_cols(part, head, width):
    return slice(part * width + head * HD, part * width + (head + 1) * HD)


def block_of(refs, per_chunk, block, cols):
    inner = block % per_chunk
    return refs[block // per_chunk][inner * BLK : (inner + 1) * BLK, cols]


def attend_fwd_kernel(chunk, per_chunk, heads, length, rev_ref, segcol_ref, segrow_ref, *rest):
    qkv_refs, out_ref, grid_ref = rest[: chunk + 1], rest[chunk + 1], rest[chunk + 2]
    width = heads * HD
    backs = min(BACK, (chunk + 1) * per_chunk)
    for head in range(heads):
        for back in range(backs):
            grid_ref[head * BACK + back] = toeplitz_rows(rev_ref, head, back, length)
    for inner in range(per_chunk):
        query_block = chunk * per_chunk + inner
        span = key_span(query_block)
        allowed = allowed_mask(segcol_ref, segrow_ref, query_block)
        for head in range(heads):
            query = block_of(qkv_refs, per_chunk, query_block, head_cols(0, head, width))
            scores = jnp.concatenate(
                [
                    fdot(query, block_of(qkv_refs, per_chunk, kb, head_cols(1, head, width)), ((1,), (1,)))
                    * (1.0 / math.sqrt(HD))
                    + grid_ref[head * BACK + query_block - kb]
                    for kb in span
                ],
                axis=1,
            )
            scores = jnp.where(allowed, scores, MASKED)
            top = jnp.max(scores, axis=1, keepdims=True)
            weights = jnp.exp(scores - top)
            weights = weights * (1.0 / jnp.sum(weights, axis=1, keepdims=True))
            probs = weights.astype(BF)
            mixed = sum(
                fdot(
                    probs[:, pos * BLK : (pos + 1) * BLK],
                    block_of(qkv_refs, per_chunk, kb, head_cols(2, head, width)),
                )
                for pos, kb in enumerate(span)
            )
            out_ref[inner * BLK : (inner + 1) * BLK, head * HD : (head + 1) * HD] = mixed.astype(BF)


def attend_bwd_kernel(
    chunk, per_chunk, heads, length, has_acc, rev_ref, segcol_ref, segrow_ref, dmix_ref, *rest
):
    rest = list(rest)
    qkv_refs = [rest.pop(0) for _ in range(chunk + 1)]
    acc_in = [rest.pop(0) for _ in range(chunk + 1)] if has_acc else None
    dqkv_ref = rest.pop(0)
    fold_ref = rest.pop(0)
    acc_out = [rest.pop(0) for _ in range(chunk)]
    grid_ref, dgrid_ref, own_acc = rest
    width = heads * HD
    backs = min(BACK, (chunk + 1) * per_chunk)
    accs = acc_out + [own_acc]
    for pos, acc in enumerate(accs):
        acc[...] = acc_in[pos][...] if has_acc else jnp.zeros_like(acc)
    dgrid_ref[...] = jnp.zeros_like(dgrid_ref)
    for head in range(heads):
        for back in range(backs):
            grid_ref[head * BACK + back] = toeplitz_rows(rev_ref, head, back, length)
    scale = 1.0 / math.sqrt(HD)
    for inner in range(per_chunk):
        query_block = chunk * per_chunk + inner
        own_rows = slice(inner * BLK, (inner + 1) * BLK)
        span = key_span(query_block)
        allowed = allowed_mask(segcol_ref, segrow_ref, query_block)
        for head in range(heads):
            query = block_of(qkv_refs, per_chunk, query_block, head_cols(0, head, width))
            keys = [block_of(qkv_refs, per_chunk, kb, head_cols(1, head, width)) for kb in span]
            values = [block_of(qkv_refs, per_chunk, kb, head_cols(2, head, width)) for kb in span]
            d_mixed = dmix_ref[own_rows, head * HD : (head + 1) * HD]
            scores = jnp.concatenate(
                [
                    fdot(query, key, ((1,), (1,))) * scale + grid_ref[head * BACK + query_block - kb]
                    for key, kb in zip(keys, span)
                ],
                axis=1,
            )
            scores = jnp.where(allowed, scores, MASKED)
            top = jnp.max(scores, axis=1, keepdims=True)
            weights = jnp.exp(scores - top)
            weights = weights * (1.0 / jnp.sum(weights, axis=1, keepdims=True))
            d_soft = jnp.concatenate([fdot(d_mixed, value, ((1,), (1,))) for value in values], axis=1)
            inner_sum = jnp.sum(d_soft * weights, axis=1, keepdims=True)
            d_scores = (weights * (d_soft - inner_sum)).astype(BF)
            probs = weights.astype(BF)
            d_query = jnp.zeros((BLK, HD), F32)
            for pos, kb in enumerate(span):
                cols = slice(pos * BLK, (pos + 1) * BLK)
                piece = d_scores[:, cols]
                d_query = d_query + fdot(piece, keys[pos])
                dgrid_ref[head * BACK + query_block - kb] += piece.astype(F32)
                acc = accs[kb // per_chunk]
                rows = slice((kb % per_chunk) * BLK, (kb % per_chunk + 1) * BLK)
                acc[rows, head_cols(0, head, width)] += fdot(piece, query, ((0,), (0,))) * scale
                acc[rows, head_cols(1, head, width)] += fdot(probs[:, cols], d_mixed, ((0,), (0,)))
            dqkv_ref[own_rows, head_cols(0, head, width)] = (d_query * scale).astype(BF)
    dqkv_ref[:, width : 3 * width] = own_acc[...].astype(BF)
    for slot in range(heads * BACK):
        fold_ref[slot : slot + 1, :] = toeplitz_fold(dgrid_ref[slot])


VM = pl.BlockSpec(memory_space=pltpu.VMEM)


def attend_forward(chunk, rev_bias, segcol, segrow, qkv_list):
    rows, width3 = qkv_list[0].shape
    heads = width3 // (3 * HD)
    length = segrow.shape[1]
    return pl.pallas_call(
        partial(attend_fwd_kernel, chunk, rows // BLK, heads, length),
        out_shape=jax.ShapeDtypeStruct((rows, heads * HD), BF),
        in_specs=[VM] * (3 + chunk + 1),
        out_specs=VM,
        scratch_shapes=[pltpu.VMEM((heads * BACK, BLK, BLK), F32)],
        cost_estimate=pl.CostEstimate(flops=int(2e9), bytes_accessed=int(4e6), transcendentals=int(2e6)),
        name="attend_fwd",
    )(rev_bias, segcol, segrow, *qkv_list[: chunk + 1])


def attend_backward(chunk, rev_bias, segcol, segrow, d_mixed, qkv_list, acc_list):
    rows, width3 = qkv_list[0].shape
    heads = width3 // (3 * HD)
    length = segrow.shape[1]
    acc_shape = (rows, 2 * heads * HD)
    has_acc = acc_list is not None
    args = [rev_bias, segcol, segrow, d_mixed, *qkv_list[: chunk + 1]]
    if has_acc:
        args += list(acc_list)
    outs = pl.pallas_call(
        partial(attend_bwd_kernel, chunk, rows // BLK, heads, length, has_acc),
        out_shape=[
            jax.ShapeDtypeStruct((rows, width3), BF),
            jax.ShapeDtypeStruct((heads * BACK, 2 * BLK), F32),
        ]
        + [jax.ShapeDtypeStruct(acc_shape, F32)] * chunk,
        in_specs=[VM] * len(args),
        out_specs=[VM] * (2 + chunk),
        scratch_shapes=[
            pltpu.VMEM((heads * BACK, BLK, BLK), F32),
            pltpu.VMEM((heads * BACK, BLK, BLK), F32),
            pltpu.VMEM(acc_shape, F32),
        ],
        cost_estimate=pl.CostEstimate(flops=int(5e9), bytes_accessed=int(8e6), transcendentals=int(2e6)),
        name="attend_bwd",
    )(*args)
    return outs[0], outs[1], list(outs[2:])


def dispatch_kernel(experts_dev, cap, weighted, code_ref, *rest):
    if weighted:
        gate_ref, x_ref, *outs = rest
    else:
        x_ref, *outs = rest
    slots = experts_dev * cap * 2
    slot_id = lax.broadcasted_iota(jnp.int32, (slots, BLK), 0)
    first = slot_id == code_ref[0, 0:1, :]
    second = slot_id == code_ref[0, 1:2, :]
    pick = jnp.where(first | second, 1.0, 0.0).astype(BF)
    rows = fdot(pick, x_ref[...].astype(BF))
    if weighted:
        gate = jnp.sum(
            jnp.where(first, gate_ref[0, 0:1, :], 0.0) + jnp.where(second, gate_ref[0, 1:2, :], 0.0),
            axis=1,
            keepdims=True,
        )
        rows = rows * gate
    rows = rows.astype(BF)
    half = slots // 2
    for local, out in enumerate(outs):
        for dest in range(experts_dev):
            out[dest, 0] = rows[local * half + dest * cap : local * half + (dest + 1) * cap]


def dispatch(x, code_row, gate_row, experts_dev, cap):
    tokens, width = x.shape
    blocks = tokens // BLK
    if cap % 16 != 0:
        slots = jnp.arange(2 * experts_dev * cap, dtype=jnp.int32)
        match = code_row[:, :, None, :] == slots[None, None, :, None]
        if gate_row is None:
            pick = jnp.sum(match.astype(F32), axis=1)
        else:
            pick = jnp.sum(jnp.where(match, gate_row[:, :, None, :], 0.0), axis=1)
        rows = jnp.einsum("bst,btd->bsd", pick, x.reshape(blocks, BLK, width).astype(F32),
                          precision=lax.Precision.HIGHEST).astype(BF)
        rows = rows.reshape(blocks, 2, experts_dev, cap, width)
        return tuple(jnp.transpose(rows[:, loc], (1, 0, 2, 3)) for loc in range(2))
    code_spec = pl.BlockSpec((1, 2, BLK), lambda b: (b, 0, 0))
    args, specs = [code_row], [code_spec]
    if gate_row is not None:
        args.append(gate_row)
        specs.append(code_spec)
    args.append(x)
    specs.append(pl.BlockSpec((BLK, width), lambda b: (b, 0)))
    shape = (experts_dev, blocks, cap, width)
    return tuple(
        pl.pallas_call(
            partial(dispatch_kernel, experts_dev, cap, gate_row is not None),
            grid=(blocks,),
            out_shape=[jax.ShapeDtypeStruct(shape, BF)] * 2,
            in_specs=specs,
            out_specs=[pl.BlockSpec((experts_dev, 1, cap, width), lambda b: (0, b, 0, 0))] * 2,
            cost_estimate=pl.CostEstimate(
                flops=int(2 * blocks * 768 * BLK * width), bytes_accessed=int(4e6), transcendentals=0
            ),
            name="dispatch",
        )(*args)
    )


def gather_rows(ref, experts_dev, cap):
    return jnp.concatenate([ref[dest, 0] for dest in range(experts_dev)], axis=0)


def combine_kernel(experts_dev, cap, weighted, code_ref, *rest):
    if weighted:
        gate_ref, r0_ref, r1_ref, out_ref = rest
    else:
        r0_ref, r1_ref, out_ref = rest
    half = experts_dev * cap
    slot_id = lax.broadcasted_iota(jnp.int32, (BLK, 2 * half), 1)
    g0 = gate_ref[:, 0:1] if weighted else 1.0
    g1 = gate_ref[:, 1:2] if weighted else 1.0
    pick = jnp.where(slot_id == code_ref[:, 0:1], g0, 0.0) + jnp.where(
        slot_id == code_ref[:, 1:2], g1, 0.0
    )
    pick = pick.astype(BF)
    total = fdot(pick[:, :half], gather_rows(r0_ref, experts_dev, cap)) + fdot(
        pick[:, half:], gather_rows(r1_ref, experts_dev, cap)
    )
    out_ref[...] = total.astype(out_ref.dtype)


def combine(rows_pair, code_col, gates, experts_dev, cap, out_dtype):
    tokens = code_col.shape[0]
    blocks = tokens // BLK
    width = rows_pair[0].shape[-1]
    if cap % 16 != 0:
        slots = jnp.arange(2 * experts_dev * cap, dtype=jnp.int32)
        match = code_col[:, :, None] == slots
        weight = jnp.where(match, 1.0 if gates is None else gates[:, :, None], 0.0).sum(axis=1)
        rows = jnp.concatenate(
            [jnp.transpose(r, (1, 0, 2, 3)).reshape(blocks, -1, width) for r in rows_pair], axis=1
        )
        out = jnp.einsum("bts,bsd->btd", weight.reshape(blocks, BLK, -1), rows.astype(F32),
                         precision=lax.Precision.HIGHEST)
        return out.reshape(tokens, width).astype(out_dtype)
    row_spec = pl.BlockSpec((experts_dev, 1, cap, width), lambda b: (0, b, 0, 0))
    col_spec = pl.BlockSpec((BLK, 2), lambda b: (b, 0))
    args, specs = [code_col], [col_spec]
    if gates is not None:
        args.append(gates)
        specs.append(col_spec)
    return pl.pallas_call(
        partial(combine_kernel, experts_dev, cap, gates is not None),
        grid=(blocks,),
        out_shape=jax.ShapeDtypeStruct((tokens, width), out_dtype),
        in_specs=specs + [row_spec] * 2,
        out_specs=pl.BlockSpec((BLK, width), lambda b: (b, 0)),
        cost_estimate=pl.CostEstimate(
            flops=int(2 * blocks * 768 * BLK * width), bytes_accessed=int(4e6), transcendentals=0
        ),
        name="combine",
    )(*args, *rows_pair)


def gate_grad_kernel(experts_dev, cap, code_ref, g_ref, r0_ref, r1_ref, out_ref):
    half = experts_dev * cap
    upstream = g_ref[...].astype(BF)
    dots = jnp.concatenate(
        [fdot(upstream, gather_rows(r, experts_dev, cap), ((1,), (1,))) for r in (r0_ref, r1_ref)],
        axis=1,
    )
    slot_id = lax.broadcasted_iota(jnp.int32, (BLK, 2 * half), 1)
    for k in range(2):
        out_ref[:, k : k + 1] = jnp.sum(
            jnp.where(slot_id == code_ref[:, k : k + 1], dots, 0.0), axis=1, keepdims=True
        )


def gate_grad(g2, rows_pair, code_col, experts_dev, cap):
    tokens, width = g2.shape
    blocks = tokens // BLK
    if cap % 16 != 0:
        slots = jnp.arange(2 * experts_dev * cap, dtype=jnp.int32)
        match = code_col[:, :, None] == slots
        rows = jnp.concatenate(
            [jnp.transpose(r, (1, 0, 2, 3)).reshape(blocks, -1, width) for r in rows_pair], axis=1
        )
        dots = jnp.einsum("btd,bsd->bts", g2.reshape(blocks, BLK, width), rows.astype(F32),
                          precision=lax.Precision.HIGHEST)
        return jnp.sum(jnp.where(match, dots.reshape(tokens, 1, -1), 0.0), axis=2)
    row_spec = pl.BlockSpec((experts_dev, 1, cap, width), lambda b: (0, b, 0, 0))
    col_spec = pl.BlockSpec((BLK, 2), lambda b: (b, 0))
    return pl.pallas_call(
        partial(gate_grad_kernel, experts_dev, cap),
        grid=(blocks,),
        out_shape=jax.ShapeDtypeStruct((tokens, 2), F32),
        in_specs=[col_spec, pl.BlockSpec((BLK, width), lambda b: (b, 0)), row_spec, row_spec],
        out_specs=col_spec,
        cost_estimate=pl.CostEstimate(
            flops=int(2 * blocks * 768 * BLK * width), bytes_accessed=int(4e6), transcendentals=0
        ),
        name="gate_grad",
    )(code_col, g2, *rows_pair)


def dispatch_parts_kernel(devices, cap, weighted, code_ref, *rest):
    if weighted:
        gate_ref, x_ref, out = rest
    else:
        x_ref, out = rest
    slots = devices * cap * 2
    slot_id = lax.broadcasted_iota(jnp.int32, (slots, BLK), 0)
    first = slot_id == code_ref[0, 0:1, :]
    second = slot_id == code_ref[0, 1:2, :]
    pick = jnp.where(first | second, 1.0, 0.0).astype(BF)
    rows = fdot(pick, x_ref[...].astype(BF))
    if weighted:
        gate = jnp.sum(
            jnp.where(first, gate_ref[0, 0:1, :], 0.0) + jnp.where(second, gate_ref[0, 1:2, :], 0.0),
            axis=1,
            keepdims=True,
        )
        rows = rows * gate
    rows = rows.astype(BF)
    for part in range(devices):
        for local in range(2):
            at = (local * devices + part) * cap
            out[part, local] = rows[at : at + cap]


def dispatch_parts(x, code_row, gate_row, devices, cap):
    tokens, width = x.shape
    blocks = tokens // BLK
    code_spec = pl.BlockSpec((1, 2, BLK), lambda b: (b, 0, 0))
    args, specs = [code_row], [code_spec]
    if gate_row is not None:
        args.append(gate_row)
        specs.append(code_spec)
    args.append(x)
    specs.append(pl.BlockSpec((BLK, width), lambda b: (b, 0)))
    return pl.pallas_call(
        partial(dispatch_parts_kernel, devices, cap, gate_row is not None),
        grid=(blocks,),
        out_shape=jax.ShapeDtypeStruct((devices, 2, blocks * cap, width), BF),
        in_specs=specs,
        out_specs=pl.BlockSpec((devices, 2, cap, width), lambda b: (0, 0, b, 0)),
        cost_estimate=pl.CostEstimate(
            flops=int(2 * blocks * 768 * BLK * width), bytes_accessed=int(4e6), transcendentals=0
        ),
        name="dispatch",
    )(*args)


def slot_rows(ref):
    pieces = [ref[part, local] for local in range(2) for part in range(ref.shape[0])]
    return jnp.concatenate(pieces, axis=0)


def combine_parts_kernel(devices, cap, weighted, code_ref, *rest):
    if weighted:
        gate_ref, *rest = rest
    parts, out_ref = rest
    slot_id = lax.broadcasted_iota(jnp.int32, (BLK, 2 * devices * cap), 1)
    g0 = gate_ref[:, 0:1] if weighted else 1.0
    g1 = gate_ref[:, 1:2] if weighted else 1.0
    pick = jnp.where(slot_id == code_ref[:, 0:1], g0, 0.0) + jnp.where(
        slot_id == code_ref[:, 1:2], g1, 0.0
    )
    out_ref[...] = fdot(pick.astype(BF), slot_rows(parts)).astype(out_ref.dtype)


def combine_parts(parts, code_col, gates, devices, cap, out_dtype):
    tokens = code_col.shape[0]
    width = parts.shape[-1]
    blocks = tokens // BLK
    row_spec = pl.BlockSpec((devices, 2, cap, width), lambda b: (0, 0, b, 0))
    col_spec = pl.BlockSpec((BLK, 2), lambda b: (b, 0))
    args, specs = [code_col], [col_spec]
    if gates is not None:
        args.append(gates)
        specs.append(col_spec)
    return pl.pallas_call(
        partial(combine_parts_kernel, devices, cap, gates is not None),
        grid=(blocks,),
        out_shape=jax.ShapeDtypeStruct((tokens, width), out_dtype),
        in_specs=specs + [row_spec],
        out_specs=pl.BlockSpec((BLK, width), lambda b: (b, 0)),
        cost_estimate=pl.CostEstimate(
            flops=int(2 * blocks * 768 * BLK * width), bytes_accessed=int(4e6), transcendentals=0
        ),
        name="combine",
    )(*args, parts)


def gate_grad_parts_kernel(devices, cap, code_ref, g_ref, *rest):
    parts, out_ref = rest
    dots = fdot(g_ref[...].astype(BF), slot_rows(parts), ((1,), (1,)))
    slot_id = lax.broadcasted_iota(jnp.int32, (BLK, 2 * devices * cap), 1)
    for k in range(2):
        out_ref[:, k : k + 1] = jnp.sum(
            jnp.where(slot_id == code_ref[:, k : k + 1], dots, 0.0), axis=1, keepdims=True
        )


def gate_grad_parts(g2, parts, code_col, devices, cap):
    tokens, width = g2.shape
    blocks = tokens // BLK
    row_spec = pl.BlockSpec((devices, 2, cap, width), lambda b: (0, 0, b, 0))
    col_spec = pl.BlockSpec((BLK, 2), lambda b: (b, 0))
    return pl.pallas_call(
        partial(gate_grad_parts_kernel, devices, cap),
        grid=(blocks,),
        out_shape=jax.ShapeDtypeStruct((tokens, 2), F32),
        in_specs=[col_spec, pl.BlockSpec((BLK, width), lambda b: (b, 0))] + [row_spec],
        out_specs=col_spec,
        cost_estimate=pl.CostEstimate(
            flops=int(2 * blocks * 768 * BLK * width), bytes_accessed=int(4e6), transcendentals=0
        ),
        name="gate_grad",
    )(code_col, g2, parts)


GELU_A = 0.7978845608028654
GELU_B = 0.044715


def expert_fwd_kernel(parts, first_ref, second_ref, inner_ref, hidden_ref, out):
    rows = jnp.concatenate([parts[part, 0] for part in range(parts.shape[0])], axis=0)
    inner = fdot(rows, first_ref[0, 0])
    inner_ref[0] = inner.astype(inner_ref.dtype)
    wave = jnp.tanh(GELU_A * (inner + GELU_B * (inner * inner * inner)))
    hidden = (0.5 * inner * (1.0 + wave)).astype(BF)
    hidden_ref[0] = hidden
    result = fdot(hidden, second_ref[0, 0]).astype(BF)
    size = parts.shape[2]
    for part in range(parts.shape[0]):
        out[part, 0] = result[part * size : (part + 1) * size]


def expert_forward(parts, first, second, layer):
    devices, _, size, width = parts.shape
    hid = first.shape[3]
    part_spec = pl.BlockSpec((devices, 1, size, width), lambda l: (0, l, 0, 0))
    outs = pl.pallas_call(
        expert_fwd_kernel,
        grid=(2,),
        out_shape=[
            jax.ShapeDtypeStruct((2, devices * size, hid), F32),
            jax.ShapeDtypeStruct((2, devices * size, hid), BF),
        ]
        + [jax.ShapeDtypeStruct((devices, 2, size, width), BF)],
        in_specs=[part_spec]
        + [
            pl.BlockSpec((1, 1, width, hid), lambda l: (layer, l, 0, 0)),
            pl.BlockSpec((1, 1, hid, width), lambda l: (layer, l, 0, 0)),
        ],
        out_specs=[
            pl.BlockSpec((1, devices * size, hid), lambda l: (l, 0, 0)),
            pl.BlockSpec((1, devices * size, hid), lambda l: (l, 0, 0)),
        ]
        + [part_spec],
        cost_estimate=pl.CostEstimate(
            flops=int(8 * devices * size * width * hid), bytes_accessed=int(20e6), transcendentals=0
        ),
        name="expert_fwd",
    )(parts, first, second)
    return outs


def expert_bwd_kernel(parts, inner_ref, first_ref, second_ref, dinner_ref, out):
    rows = jnp.concatenate([parts[part, 0] for part in range(parts.shape[0])], axis=0)
    d_hidden = fdot(rows, second_ref[0, 0], ((1,), (1,)))
    inner = inner_ref[0]
    square = inner * inner
    wave = jnp.tanh(GELU_A * inner * (1.0 + GELU_B * square))
    slope = 0.5 * (1.0 + wave) + (0.5 * GELU_A) * inner * (1.0 - wave * wave) * (
        1.0 + (3.0 * GELU_B) * square
    )
    d_inner = (d_hidden * slope).astype(BF)
    dinner_ref[0] = d_inner
    d_rows = fdot(d_inner, first_ref[0, 0], ((1,), (1,))).astype(BF)
    size = parts.shape[2]
    for part in range(parts.shape[0]):
        out[part, 0] = d_rows[part * size : (part + 1) * size]


def expert_backward(parts, inner, first, second, layer):
    devices, _, size, width = parts.shape
    hid = first.shape[3]
    part_spec = pl.BlockSpec((devices, 1, size, width), lambda l: (0, l, 0, 0))
    outs = pl.pallas_call(
        expert_bwd_kernel,
        grid=(2,),
        out_shape=[
            jax.ShapeDtypeStruct((2, devices * size, hid), BF),
        ]
        + [jax.ShapeDtypeStruct((devices, 2, size, width), BF)],
        in_specs=[part_spec]
        + [
            pl.BlockSpec((1, devices * size, hid), lambda l: (l, 0, 0)),
            pl.BlockSpec((1, 1, width, hid), lambda l: (layer, l, 0, 0)),
            pl.BlockSpec((1, 1, hid, width), lambda l: (layer, l, 0, 0)),
        ],
        out_specs=[
            pl.BlockSpec((1, devices * size, hid), lambda l: (l, 0, 0)),
        ]
        + [part_spec],
        cost_estimate=pl.CostEstimate(
            flops=int(8 * devices * size * width * hid), bytes_accessed=int(20e6), transcendentals=0
        ),
        name="expert_bwd",
    )(parts, inner, first, second)
    return outs


def spread(x, axis_name):
    return lax.all_to_all(x, axis_name, split_axis=0, concat_axis=0, tiled=True)


def swap(x, axis_name, step):
    size = lax.axis_size(axis_name)
    return lax.ppermute(x, axis_name, [(i, i ^ step) for i in range(size)])


def spread_gather(x, axis_name):
    size = lax.axis_size(axis_name)
    return spread(jnp.broadcast_to(x[None], (size,) + x.shape), axis_name)


def reduce_rows(x):
    zs, z_id = lax.axis_size("seq"), lax.axis_index("seq")
    pieces = x.reshape(zs, -1, x.shape[1])
    total = lax.dynamic_index_in_dim(pieces, z_id, 0, keepdims=False).astype(F32)
    for step in range(1, zs):
        piece = lax.dynamic_index_in_dim(pieces, z_id ^ step, 0, keepdims=False)
        total = total + swap(piece, "seq", step).astype(F32)
    return total


def sum_rows(x):
    zs, z_id = lax.axis_size("seq"), lax.axis_index("seq")
    steps = [1 << bit for bit in range(zs.bit_length() - 1)]
    total = x
    for step in steps:
        half = total.shape[0] // 2
        upper = (z_id & step) != 0
        low, high = total[:half], total[half:]
        got = swap(jnp.where(upper, low, high), "seq", step)
        total = (jnp.where(upper, high, low).astype(F32) + got.astype(F32)).astype(BF)
    for step in reversed(steps):
        upper = (z_id & step) != 0
        got = swap(total, "seq", step)
        total = jnp.concatenate(
            [jnp.where(upper, got, total), jnp.where(upper, total, got)], axis=0
        )
    return total.astype(F32)


def split_dense_kernel(zs, es, rows, in_ref, out_ref, in_send, out_send):
    for dest in range(es):
        pieces = [
            in_ref[(plane * es + dest) * rows : (plane * es + dest + 1) * rows] for plane in range(zs)
        ]
        in_send[dest] = jnp.concatenate(pieces, axis=0).astype(BF)
        out_send[dest] = out_ref[dest * rows : (dest + 1) * rows].astype(BF)


def split_dense(total_in, total_out, zs, es, rows):
    wide, width = total_in.shape[1], total_out.shape[1]
    if rows % 8 != 0:
        in_send = jnp.transpose(total_in.reshape(zs, es, rows, wide), (1, 0, 2, 3))
        return (
            in_send.reshape(es, zs * rows, wide).astype(BF),
            total_out.reshape(es, rows, width).astype(BF),
        )
    return pl.pallas_call(
        partial(split_dense_kernel, zs, es, rows),
        out_shape=[
            jax.ShapeDtypeStruct((es, zs * rows, wide), BF),
            jax.ShapeDtypeStruct((es, rows, width), BF),
        ],
        in_specs=[VM] * 2,
        out_specs=[VM] * 2,
        cost_estimate=pl.CostEstimate(flops=int(1e6), bytes_accessed=int(4e6), transcendentals=0),
        name="split_dense",
    )(total_in, total_out)


def norm_forward(stream, gain):
    inverse = lax.rsqrt(jnp.mean(stream * stream, axis=-1, keepdims=True) + NORM_EPS)
    return (stream * inverse * gain).astype(BF), inverse


def norm_backward(stream, inverse, gain, upstream):
    scaled = upstream * gain
    inner_mean = jnp.mean(scaled * stream, axis=-1, keepdims=True)
    d_stream = inverse * scaled - stream * (inverse * inverse * inverse) * inner_mean
    return d_stream, jnp.sum(upstream * stream * inverse, axis=0)


def slot_codes(routes, experts, experts_dev, cap):
    blocks = routes.shape[0] // BLK
    flat = routes.reshape(blocks, BLK * 2)
    onehot = (flat[:, :, None] == jnp.arange(experts, dtype=jnp.int32)).astype(F32)
    steps = jnp.arange(BLK * 2, dtype=jnp.int32)
    before = (steps[:, None] > steps[None, :]).astype(F32)
    count = jnp.einsum("ij,bje->bie", before, onehot, preferred_element_type=F32)
    place = jnp.sum(count * onehot, axis=2).astype(jnp.int32)
    code = (flat % 2) * (experts_dev * cap) + (flat // 2) * cap + place
    return code.reshape(blocks * BLK, 2)


def body(
    tokens,
    cotangent,
    segments,
    buckets,
    routes,
    attend_in,
    attend_out,
    router_weight,
    gain_attend,
    gain_expert,
    bias_table,
    expert_in,
    expert_out,
):
    zs = lax.axis_size("seq")
    es = lax.axis_size("expert")
    z_id = lax.axis_index("seq")
    own_rows, width = tokens.shape[1:]
    length = segments.shape[1]
    layers, shard_rows = attend_in.shape[:2]
    experts = router_weight.shape[2]
    cap = 3 * own_rows // experts
    heads_all = width // HD
    heads = heads_all // zs
    hw = heads * HD
    bucket_count = bias_table.shape[1] * zs * es // heads_all
    chunks = CHUNKS
    rows_c = length // chunks

    def split(x):
        return [x[c * rows_c : (c + 1) * rows_c] for c in range(chunks)]

    route_rows = routes[0].astype(BF).reshape(-1, width) if (own_rows * 2) % width == 0 else None
    if route_rows is None:
        flat_routes = routes[0].astype(BF).reshape(-1)
        pad = -flat_routes.shape[0] % (16 * width)
        route_rows = jnp.pad(flat_routes, (0, pad)).reshape(-1, width)
    packed = lax.all_gather(jnp.concatenate([tokens[0], route_rows], axis=0), "seq", axis=0)
    stream_full = packed[:, :own_rows].reshape(length, width)
    routes_full = (
        packed[:, own_rows:].reshape(zs, -1)[:, : own_rows * 2].reshape(length, 2).astype(jnp.int32)
    )

    small = jnp.concatenate(
        [
            gain_attend.reshape(-1),
            gain_expert.reshape(-1),
            bias_table.reshape(-1),
            router_weight.reshape(-1),
        ]
    )
    small = spread_gather(spread_gather(small, "expert"), "seq").reshape(zs * es, -1)
    sizes = [layers * shard_rows, layers * shard_rows, layers * bias_table.shape[1]]
    at = 0
    parts = []
    for size in sizes:
        parts.append(small[:, at : at + size])
        at += size
    gains_a = jnp.transpose(parts[0].reshape(-1, layers, shard_rows), (1, 0, 2)).reshape(layers, width)
    gains_e = jnp.transpose(parts[1].reshape(-1, layers, shard_rows), (1, 0, 2)).reshape(layers, width)
    bias_all = jnp.transpose(
        parts[2].reshape(-1, layers, bias_table.shape[1]), (1, 0, 2)
    ).reshape(layers, heads_all, bucket_count)
    routers = jnp.transpose(
        small[:, at:].reshape(-1, layers, shard_rows, experts), (1, 0, 2, 3)
    ).reshape(layers, width, experts)
    gains_a = gains_a.astype(F32)
    gains_e = gains_e.astype(F32)

    piece = attend_in.reshape(layers, shard_rows, 3, zs, hw)
    piece = jnp.transpose(piece, (3, 0, 1, 2, 4)).reshape(zs, layers, shard_rows, 3 * hw)
    piece = spread(piece, "seq")
    piece = lax.all_gather(piece, "expert", axis=0)
    piece = jnp.transpose(piece, (2, 1, 0, 3, 4)).reshape(layers, width, 3 * hw)
    w_in_list = [piece[layer] for layer in range(layers)]
    w_out_list = [
        lax.all_gather(attend_out[layer], ("seq", "expert"), axis=0, tiled=True)
        for layer in range(layers)
    ]

    steps = length - jnp.arange(length + BLK, dtype=jnp.int32)
    rev_buckets = jnp.concatenate(
        [buckets[length - 1 :], buckets[::-1], jnp.broadcast_to(buckets[:1], (BLK - 1,))]
    )
    rev_hot = (rev_buckets[:, None] == jnp.arange(bucket_count, dtype=jnp.int32)).astype(F32)
    segrow = segments
    segcol = segments.reshape(length, 1)

    fast = cap % 16 == 0
    code_full = slot_codes(routes_full, experts, es, cap)
    code_col = split(code_full)
    code_row_full = jnp.transpose(code_full.reshape(-1, BLK, 2), (0, 2, 1))
    blocks_c = rows_c // BLK
    code_row = [code_row_full[c * blocks_c : (c + 1) * blocks_c] for c in range(chunks)]
    route_hot = split(routes_full[..., None] == jnp.arange(experts, dtype=jnp.int32))

    def exchange(pair):
        return [
            spread(r.reshape(es, -1, width), "expert").reshape(-1, width) for r in pair
        ]

    def exchange_back(pair):
        return [
            spread(r.reshape(es, -1, width), "expert").reshape(es, blocks_c, cap, width) for r in pair
        ]

    stream = split(stream_full.astype(F32))
    saved = []
    block_out = None
    for layer in range(layers):
        w_in, w_out = w_in_list[layer], w_out_list[layer]
        local_bias = lax.dynamic_slice_in_dim(bias_all[layer], z_id * heads, heads, 0)
        rev_bias = fdot(local_bias, rev_hot.astype(BF), ((1,), (1,)))
        w_out_flip = [
            lax.dynamic_slice_in_dim(w_out, (z_id ^ step) * hw, hw, 0) for step in range(zs)
        ]
        keep = dict(stream=stream, rev_bias=rev_bias, chunks=[])
        qkv = []
        mids, partials = [], []
        for c in range(chunks):
            normed, inv_a = norm_forward(stream[c], gains_a[layer])
            qkv.append(fdot(normed, w_in).astype(BF))
            mixed = attend_forward(c, rev_bias, segcol, segrow, qkv)
            if layer == 0 and c == 0:
                held = lax.optimization_barrier((cotangent, mixed[:8, :128]))[0]
                upstream_full = lax.all_gather(held[0], "seq", axis=0, tiled=True)
            mid = stream[c]
            for step in range(zs):
                got = mixed if step == 0 else swap(mixed, "seq", step)
                mid = mid + fdot(got, w_out_flip[step])
            normed_mid, inv_e = norm_forward(mid, gains_e[layer])
            logits = fdot(normed_mid, routers[layer])
            chosen = jnp.sum(jnp.where(route_hot[c], logits[:, None, :], 0.0), axis=-1)
            gates = jax.nn.softmax(chosen, axis=-1)
            if fast:
                rows = spread(dispatch_parts(normed_mid, code_row[c], None, es, cap), "expert")
                inner, hidden, result = expert_forward(rows, expert_in, expert_out, layer)
                back = spread(result, "expert")
                partials.append(combine_parts(back, code_col[c], gates, es, cap, BF))
            else:
                rows = exchange(dispatch(normed_mid, code_row[c], None, es, cap))
                inner, hidden, result = [], [], []
                for loc in range(2):
                    pre = fdot(rows[loc], expert_in[layer, loc])
                    hid = jax.nn.gelu(pre).astype(BF)
                    inner.append(pre)
                    hidden.append(hid)
                    result.append(fdot(hid, expert_out[layer, loc]).astype(BF))
                back = exchange_back(result)
                partials.append(combine(back, code_col[c], gates, es, cap, BF))
            mids.append(mid)
            keep["chunks"].append(
                dict(normed=normed, inv_a=inv_a, mixed=mixed, mid=mid, normed_mid=normed_mid,
                     inv_e=inv_e, gates=gates, rows=rows, inner=inner, hidden=hidden, back=back)
            )
        keep["qkv"] = qkv
        saved.append(keep)
        if layer + 1 < layers:
            stream = [mids[c] + sum_rows(partials[c]) for c in range(chunks)]
        else:
            delta = reduce_rows(jnp.concatenate(partials, axis=0))
            mid_own = lax.dynamic_slice_in_dim(
                jnp.concatenate(mids, axis=0), z_id * own_rows, own_rows, 0
            )
            block_out = (mid_own + delta.astype(F32)).astype(BF)

    upstream = split(upstream_full.astype(F32))
    in_grads, out_grads = [None] * layers, [None] * layers
    first_grads, second_grads = [None] * layers, [None] * layers
    small_grads = [None] * layers
    tokens_grad = None
    for layer in reversed(range(layers)):
        keep = saved[layer]
        w_in, w_out = w_in_list[layer], w_out_list[layer]
        w_out_own = lax.dynamic_slice_in_dim(w_out, z_id * hw, hw, 0)
        d_mids, d_parts = [None] * chunks, [None] * chunks
        total_in = total_out = total_router = total_ga = total_ge = total_fold = None
        g_first = [None, None]
        g_second = [None, None]
        acc = None

        def plus(left, right):
            return right if left is None else left + right

        for c in reversed(range(chunks)):
            k = keep["chunks"][c]
            g2 = upstream[c]
            gates = k["gates"]
            gate_row = jnp.transpose(gates.reshape(blocks_c, BLK, 2), (0, 2, 1))
            if fast:
                d_res = spread(dispatch_parts(g2, code_row[c], gate_row, es, cap), "expert")
                d_inner, d_rows = expert_backward(d_res, k["inner"], expert_in, expert_out, layer)
                d_back = spread(d_rows, "expert")
                for loc in range(2):
                    d_loc = d_res[:, loc].reshape(-1, width)
                    r_loc = k["rows"][:, loc].reshape(-1, width)
                    g_second[loc] = plus(g_second[loc], fdot(k["hidden"][loc], d_loc, ((0,), (0,))))
                    g_first[loc] = plus(g_first[loc], fdot(r_loc, d_inner[loc], ((0,), (0,))))
                d_gates = gate_grad_parts(g2, k["back"], code_col[c], es, cap)
                d_moved = combine_parts(d_back, code_col[c], None, es, cap, F32)
            else:
                d_res = exchange(dispatch(g2, code_row[c], gate_row, es, cap))
                d_rows = []
                for loc in range(2):
                    d_hid = fdot(d_res[loc], expert_out[layer, loc], ((1,), (1,)))
                    _, pull = jax.vjp(jax.nn.gelu, k["inner"][loc])
                    d_inner = pull(d_hid)[0].astype(BF)
                    d_rows.append(fdot(d_inner, expert_in[layer, loc], ((1,), (1,))).astype(BF))
                    g_second[loc] = plus(
                        g_second[loc], fdot(k["hidden"][loc], d_res[loc], ((0,), (0,)))
                    )
                    g_first[loc] = plus(g_first[loc], fdot(k["rows"][loc], d_inner, ((0,), (0,))))
                d_back = exchange_back(d_rows)
                d_gates = gate_grad(g2, k["back"], code_col[c], es, cap)
                d_moved = combine(d_back, code_col[c], None, es, cap, F32)
            d_chosen = gates * (d_gates - jnp.sum(gates * d_gates, axis=-1, keepdims=True))
            d_logits = jnp.sum(jnp.where(route_hot[c], d_chosen[..., None], 0.0), axis=1)
            total_router = plus(
                total_router, exact_dot(k["normed_mid"].astype(F32).T, d_logits)
            )
            partial_d = d_moved + exact_dot(d_logits, routers[layer].astype(F32).T)
            d_normed_mid = sum_rows(partial_d.astype(BF))
            d_stream, ge = norm_backward(k["mid"], k["inv_e"], gains_e[layer], d_normed_mid)
            total_ge = plus(total_ge, ge)
            d_mid = g2 + d_stream
            d_proj = d_mid.astype(BF)
            total_out = plus(total_out, fdot(k["mixed"], d_proj, ((0,), (0,))))
            d_mixed = fdot(d_proj, w_out_own, ((1,), (1,))).astype(BF)
            d_qkv, fold, acc = attend_backward(
                c, keep["rev_bias"], segcol, segrow, d_mixed, keep["qkv"], acc
            )
            total_fold = plus(total_fold, fold)
            total_in = plus(total_in, fdot(k["normed"], d_qkv, ((0,), (0,))))
            d_parts[c] = fdot(d_qkv, w_in, ((1,), (1,))).astype(BF)
            d_mids[c] = d_mid
            if layer > 0:
                d_normed = sum_rows(d_parts[c])
                d_in, ga = norm_backward(keep["stream"][c], k["inv_a"], gains_a[layer], d_normed)
                total_ga = plus(total_ga, ga)
                upstream[c] = d_in + d_mid
        own = (jnp.arange(zs) == z_id).astype(F32)[:, None]
        if layer == 0:
            d_normed = reduce_rows(jnp.concatenate(d_parts, axis=0))

            def mine(items):
                return lax.dynamic_slice_in_dim(
                    jnp.concatenate(items, axis=0), z_id * own_rows, own_rows, 0
                )

            stream_own = mine(keep["stream"])
            inv_own = mine([keep["chunks"][c]["inv_a"] for c in range(chunks)])
            d_in, ga = norm_backward(stream_own, inv_own, gains_a[layer], d_normed)
            tokens_grad = (d_in + mine(d_mids)).astype(BF)
            gain_a_part = ga.reshape(zs, -1)
        else:
            gain_a_part = total_ga.reshape(zs, -1) * own
        gain_e_part = total_ge.reshape(zs, -1) * own
        fold = total_fold.reshape(heads, BACK, 2 * BLK)
        hot = jnp.stack(
            [
                jnp.concatenate(
                    [
                        rev_hot[length - BLK * back : length - BLK * (back - 1)],
                        rev_hot[length - BLK * (back + 1) : length - BLK * back],
                    ],
                    axis=0,
                )
                for back in range(BACK)
            ]
        )
        table = exact_dot(fold.reshape(heads, -1), hot.reshape(-1, bucket_count))
        table_part = table.reshape(1, -1) * own
        router_part = total_router.reshape(zs, es, shard_rows * experts)
        small_grads[layer] = jnp.concatenate(
            [
                router_part,
                gain_a_part.reshape(zs, es, -1),
                gain_e_part.reshape(zs, es, -1),
                table_part.reshape(zs, es, -1),
            ],
            axis=-1,
        )
        in_send, out_send = split_dense(total_in, total_out, zs, es, shard_rows)
        piece = jnp.sum(spread(in_send, "expert").astype(F32), axis=0)
        out_grads[layer] = jnp.sum(spread(out_send, "expert").astype(F32), axis=0)
        piece = spread(piece.reshape(zs, shard_rows, 3 * hw).astype(BF), "seq").astype(F32)
        piece = jnp.transpose(piece.reshape(zs, shard_rows, 3, hw), (1, 2, 0, 3))
        in_grads[layer] = piece.reshape(shard_rows, 3 * width)
        first_grads[layer] = jnp.stack(g_first)
        second_grads[layer] = jnp.stack(g_second)

    packed_small = jnp.stack(small_grads, axis=2)
    packed_small = jnp.transpose(packed_small, (1, 0, 2, 3))
    packed_small = jnp.sum(spread(packed_small, "expert"), axis=0)
    packed_small = jnp.sum(spread(packed_small, "seq"), axis=0)
    r_size = shard_rows * experts
    router_grad = packed_small[:, :r_size].reshape(layers, shard_rows, experts)
    ga_grad = packed_small[:, r_size : r_size + shard_rows]
    ge_grad = packed_small[:, r_size + shard_rows : r_size + 2 * shard_rows]
    table_grad = packed_small[:, r_size + 2 * shard_rows :]
    return (
        block_out[None],
        tokens_grad[None],
        jnp.stack(in_grads),
        jnp.stack(out_grads),
        router_grad,
        ga_grad,
        ge_grad,
        table_grad,
        jnp.stack(first_grads),
        jnp.stack(second_grads),
    )


def solution(mesh):
    both = ("seq", "expert")
    return jax.shard_map(
        body,
        mesh=mesh,
        in_specs=(
            P("expert", "seq", None),
            P("expert", "seq", None),
            P("expert", None),
            P(),
            P("expert", "seq", None),
            P(None, both, None),
            P(None, both, None),
            P(None, both, None),
            P(None, both),
            P(None, both),
            P(None, both),
            P(None, "expert", None, "seq"),
            P(None, "expert", "seq", None),
        ),
        out_specs=(
            P("expert", "seq", None),
            P("expert", "seq", None),
            P(None, both, None),
            P(None, both, None),
            P(None, both, None),
            P(None, both),
            P(None, both),
            P(None, both),
            P(None, "expert", None, "seq"),
            P(None, "expert", "seq", None),
        ),
        check_vma=False,
    )
```

```python
from functools import partial
import math

import jax
import jax.numpy as jnp
from jax import lax
from jax.experimental import pallas as pl
from jax.experimental.pallas import tpu as pltpu
from jax.sharding import PartitionSpec as P

HD = 64
BLK = 256
BACK = 3
CHUNKS = 2
NORM_EPS = 1e-06
MASKED = -1000000000.0
BF = jnp.bfloat16
F32 = jnp.float32


def fdot(left, right, dims=((1,), (0,))):
    return lax.dot_general(left, right, (dims, ((), ())), preferred_element_type=F32)


def exact_dot(left, right):
    return jnp.dot(left, right, precision=lax.Precision.HIGHEST, preferred_element_type=F32)


def toeplitz_rows(rev_ref, head, back, length):
    start = length - BLK * back
    line = jnp.concatenate(
        [rev_ref[head : head + 1, start : start + BLK], rev_ref[head : head + 1, start - BLK : start]],
        axis=1,
    )
    rows = jnp.broadcast_to(line, (8, 2 * BLK))
    row_id = lax.broadcasted_iota(jnp.int32, rows.shape, 0)
    for bit in (1, 2, 4):
        rows = jnp.where((row_id & bit) != 0, pltpu.roll(rows, bit, 1), rows)
    size = 8
    while size < BLK:
        rows = jnp.concatenate([rows, pltpu.roll(rows, size, 1)], axis=0)
        size *= 2
    return rows[:, :BLK]


def toeplitz_fold(grid):
    rows = jnp.concatenate([grid, jnp.zeros_like(grid)], axis=1)
    width = 2 * BLK
    size = BLK // 2
    while size >= 8:
        rows = rows[:size] + pltpu.roll(rows[size:], width - size, 1)
        size //= 2
    row_id = lax.broadcasted_iota(jnp.int32, rows.shape, 0)
    for bit in (1, 2, 4):
        rows = jnp.where((row_id & bit) != 0, pltpu.roll(rows, width - bit, 1), rows)
    return jnp.sum(rows, axis=0, keepdims=True)


def key_span(query_block):
    return list(range(max(0, query_block - BACK + 1), query_block + 1))


def allowed_mask(segcol_ref, segrow_ref, query_block):
    span = key_span(query_block)
    first = span[0] * BLK
    own = segcol_ref[query_block * BLK : (query_block + 1) * BLK, :]
    theirs = segrow_ref[:, first : (query_block + 1) * BLK]
    same = own == theirs
    shape = (BLK, len(span) * BLK)
    rows = lax.broadcasted_iota(jnp.int32, shape, 0) + query_block * BLK
    cols = lax.broadcasted_iota(jnp.int32, shape, 1) + first
    return same & (cols <= rows)


def head_cols(part, head, width):
    return slice(part * width + head * HD, part * width + (head + 1) * HD)


def block_of(refs, per_chunk, block, cols):
    inner = block % per_chunk
    return refs[block // per_chunk][inner * BLK : (inner + 1) * BLK, cols]


def attend_fwd_kernel(chunk, per_chunk, heads, length, rev_ref, segcol_ref, segrow_ref, *rest):
    qkv_refs, out_ref, grid_ref = rest[: chunk + 1], rest[chunk + 1], rest[chunk + 2]
    width = heads * HD
    backs = min(BACK, (chunk + 1) * per_chunk)
    for head in range(heads):
        for back in range(backs):
            grid_ref[head * BACK + back] = toeplitz_rows(rev_ref, head, back, length)
    for inner in range(per_chunk):
        query_block = chunk * per_chunk + inner
        span = key_span(query_block)
        allowed = allowed_mask(segcol_ref, segrow_ref, query_block)
        for head in range(heads):
            query = block_of(qkv_refs, per_chunk, query_block, head_cols(0, head, width))
            scores = jnp.concatenate(
                [
                    fdot(query, block_of(qkv_refs, per_chunk, kb, head_cols(1, head, width)), ((1,), (1,)))
                    * (1.0 / math.sqrt(HD))
                    + grid_ref[head * BACK + query_block - kb]
                    for kb in span
                ],
                axis=1,
            )
            scores = jnp.where(allowed, scores, MASKED)
            top = jnp.max(scores, axis=1, keepdims=True)
            weights = jnp.exp(scores - top)
            weights = weights * (1.0 / jnp.sum(weights, axis=1, keepdims=True))
            probs = weights.astype(BF)
            mixed = sum(
                fdot(
                    probs[:, pos * BLK : (pos + 1) * BLK],
                    block_of(qkv_refs, per_chunk, kb, head_cols(2, head, width)),
                )
                for pos, kb in enumerate(span)
            )
            out_ref[inner * BLK : (inner + 1) * BLK, head * HD : (head + 1) * HD] = mixed.astype(BF)


def attend_bwd_kernel(
    chunk, per_chunk, heads, length, has_acc, rev_ref, segcol_ref, segrow_ref, dmix_ref, *rest
):
    rest = list(rest)
    qkv_refs = [rest.pop(0) for _ in range(chunk + 1)]
    acc_in = [rest.pop(0) for _ in range(chunk + 1)] if has_acc else None
    dqkv_ref = rest.pop(0)
    fold_ref = rest.pop(0)
    acc_out = [rest.pop(0) for _ in range(chunk)]
    grid_ref, dgrid_ref, own_acc = rest
    width = heads * HD
    backs = min(BACK, (chunk + 1) * per_chunk)
    accs = acc_out + [own_acc]
    for pos, acc in enumerate(accs):
        acc[...] = acc_in[pos][...] if has_acc else jnp.zeros_like(acc)
    dgrid_ref[...] = jnp.zeros_like(dgrid_ref)
    for head in range(heads):
        for back in range(backs):
            grid_ref[head * BACK + back] = toeplitz_rows(rev_ref, head, back, length)
    scale = 1.0 / math.sqrt(HD)
    for inner in range(per_chunk):
        query_block = chunk * per_chunk + inner
        own_rows = slice(inner * BLK, (inner + 1) * BLK)
        span = key_span(query_block)
        allowed = allowed_mask(segcol_ref, segrow_ref, query_block)
        for head in range(heads):
            query = block_of(qkv_refs, per_chunk, query_block, head_cols(0, head, width))
            keys = [block_of(qkv_refs, per_chunk, kb, head_cols(1, head, width)) for kb in span]
            values = [block_of(qkv_refs, per_chunk, kb, head_cols(2, head, width)) for kb in span]
            d_mixed = dmix_ref[own_rows, head * HD : (head + 1) * HD]
            scores = jnp.concatenate(
                [
                    fdot(query, key, ((1,), (1,))) * scale + grid_ref[head * BACK + query_block - kb]
                    for key, kb in zip(keys, span)
                ],
                axis=1,
            )
            scores = jnp.where(allowed, scores, MASKED)
            top = jnp.max(scores, axis=1, keepdims=True)
            weights = jnp.exp(scores - top)
            weights = weights * (1.0 / jnp.sum(weights, axis=1, keepdims=True))
            d_soft = jnp.concatenate([fdot(d_mixed, value, ((1,), (1,))) for value in values], axis=1)
            inner_sum = jnp.sum(d_soft * weights, axis=1, keepdims=True)
            d_scores = (weights * (d_soft - inner_sum)).astype(BF)
            probs = weights.astype(BF)
            d_query = jnp.zeros((BLK, HD), F32)
            for pos, kb in enumerate(span):
                cols = slice(pos * BLK, (pos + 1) * BLK)
                piece = d_scores[:, cols]
                d_query = d_query + fdot(piece, keys[pos])
                dgrid_ref[head * BACK + query_block - kb] += piece.astype(F32)
                acc = accs[kb // per_chunk]
                rows = slice((kb % per_chunk) * BLK, (kb % per_chunk + 1) * BLK)
                acc[rows, head_cols(0, head, width)] += fdot(piece, query, ((0,), (0,))) * scale
                acc[rows, head_cols(1, head, width)] += fdot(probs[:, cols], d_mixed, ((0,), (0,)))
            dqkv_ref[own_rows, head_cols(0, head, width)] = (d_query * scale).astype(BF)
    dqkv_ref[:, width : 3 * width] = own_acc[...].astype(BF)
    for slot in range(heads * BACK):
        fold_ref[slot : slot + 1, :] = toeplitz_fold(dgrid_ref[slot])


VM = pl.BlockSpec(memory_space=pltpu.VMEM)


def attend_forward(chunk, rev_bias, segcol, segrow, qkv_list):
    rows, width3 = qkv_list[0].shape
    heads = width3 // (3 * HD)
    length = segrow.shape[1]
    return pl.pallas_call(
        partial(attend_fwd_kernel, chunk, rows // BLK, heads, length),
        out_shape=jax.ShapeDtypeStruct((rows, heads * HD), BF),
        in_specs=[VM] * (3 + chunk + 1),
        out_specs=VM,
        scratch_shapes=[pltpu.VMEM((heads * BACK, BLK, BLK), F32)],
        cost_estimate=pl.CostEstimate(flops=int(2e9), bytes_accessed=int(4e6), transcendentals=int(2e6)),
        name="attend_fwd",
    )(rev_bias, segcol, segrow, *qkv_list[: chunk + 1])


def attend_backward(chunk, rev_bias, segcol, segrow, d_mixed, qkv_list, acc_list):
    rows, width3 = qkv_list[0].shape
    heads = width3 // (3 * HD)
    length = segrow.shape[1]
    acc_shape = (rows, 2 * heads * HD)
    has_acc = acc_list is not None
    args = [rev_bias, segcol, segrow, d_mixed, *qkv_list[: chunk + 1]]
    if has_acc:
        args += list(acc_list)
    outs = pl.pallas_call(
        partial(attend_bwd_kernel, chunk, rows // BLK, heads, length, has_acc),
        out_shape=[
            jax.ShapeDtypeStruct((rows, width3), BF),
            jax.ShapeDtypeStruct((heads * BACK, 2 * BLK), F32),
        ]
        + [jax.ShapeDtypeStruct(acc_shape, F32)] * chunk,
        in_specs=[VM] * len(args),
        out_specs=[VM] * (2 + chunk),
        scratch_shapes=[
            pltpu.VMEM((heads * BACK, BLK, BLK), F32),
            pltpu.VMEM((heads * BACK, BLK, BLK), F32),
            pltpu.VMEM(acc_shape, F32),
        ],
        cost_estimate=pl.CostEstimate(flops=int(5e9), bytes_accessed=int(8e6), transcendentals=int(2e6)),
        name="attend_bwd",
    )(*args)
    return outs[0], outs[1], list(outs[2:])


def dispatch_kernel(experts_dev, cap, weighted, code_ref, *rest):
    if weighted:
        gate_ref, x_ref, *outs = rest
    else:
        x_ref, *outs = rest
    slots = experts_dev * cap * 2
    slot_id = lax.broadcasted_iota(jnp.int32, (slots, BLK), 0)
    first = slot_id == code_ref[0, 0:1, :]
    second = slot_id == code_ref[0, 1:2, :]
    pick = jnp.where(first | second, 1.0, 0.0).astype(BF)
    rows = fdot(pick, x_ref[...].astype(BF))
    if weighted:
        gate = jnp.sum(
            jnp.where(first, gate_ref[0, 0:1, :], 0.0) + jnp.where(second, gate_ref[0, 1:2, :], 0.0),
            axis=1,
            keepdims=True,
        )
        rows = rows * gate
    rows = rows.astype(BF)
    half = slots // 2
    for local, out in enumerate(outs):
        for dest in range(experts_dev):
            out[dest, 0] = rows[local * half + dest * cap : local * half + (dest + 1) * cap]


def dispatch(x, code_row, gate_row, experts_dev, cap):
    tokens, width = x.shape
    blocks = tokens // BLK
    if cap % 16 != 0:
        slots = jnp.arange(2 * experts_dev * cap, dtype=jnp.int32)
        match = code_row[:, :, None, :] == slots[None, None, :, None]
        if gate_row is None:
            pick = jnp.sum(match.astype(F32), axis=1)
        else:
            pick = jnp.sum(jnp.where(match, gate_row[:, :, None, :], 0.0), axis=1)
        rows = jnp.einsum("bst,btd->bsd", pick, x.reshape(blocks, BLK, width).astype(F32),
                          precision=lax.Precision.HIGHEST).astype(BF)
        rows = rows.reshape(blocks, 2, experts_dev, cap, width)
        return tuple(jnp.transpose(rows[:, loc], (1, 0, 2, 3)) for loc in range(2))
    code_spec = pl.BlockSpec((1, 2, BLK), lambda b: (b, 0, 0))
    args, specs = [code_row], [code_spec]
    if gate_row is not None:
        args.append(gate_row)
        specs.append(code_spec)
    args.append(x)
    specs.append(pl.BlockSpec((BLK, width), lambda b: (b, 0)))
    shape = (experts_dev, blocks, cap, width)
    return tuple(
        pl.pallas_call(
            partial(dispatch_kernel, experts_dev, cap, gate_row is not None),
            grid=(blocks,),
            out_shape=[jax.ShapeDtypeStruct(shape, BF)] * 2,
            in_specs=specs,
            out_specs=[pl.BlockSpec((experts_dev, 1, cap, width), lambda b: (0, b, 0, 0))] * 2,
            cost_estimate=pl.CostEstimate(
                flops=int(2 * blocks * 768 * BLK * width), bytes_accessed=int(4e6), transcendentals=0
            ),
            name="dispatch",
        )(*args)
    )


def gather_rows(ref, experts_dev, cap):
    return jnp.concatenate([ref[dest, 0] for dest in range(experts_dev)], axis=0)


def combine_kernel(experts_dev, cap, weighted, code_ref, *rest):
    if weighted:
        gate_ref, r0_ref, r1_ref, out_ref = rest
    else:
        r0_ref, r1_ref, out_ref = rest
    half = experts_dev * cap
    slot_id = lax.broadcasted_iota(jnp.int32, (BLK, 2 * half), 1)
    g0 = gate_ref[:, 0:1] if weighted else 1.0
    g1 = gate_ref[:, 1:2] if weighted else 1.0
    pick = jnp.where(slot_id == code_ref[:, 0:1], g0, 0.0) + jnp.where(
        slot_id == code_ref[:, 1:2], g1, 0.0
    )
    pick = pick.astype(BF)
    total = fdot(pick[:, :half], gather_rows(r0_ref, experts_dev, cap)) + fdot(
        pick[:, half:], gather_rows(r1_ref, experts_dev, cap)
    )
    out_ref[...] = total.astype(out_ref.dtype)


def combine(rows_pair, code_col, gates, experts_dev, cap, out_dtype):
    tokens = code_col.shape[0]
    blocks = tokens // BLK
    width = rows_pair[0].shape[-1]
    if cap % 16 != 0:
        slots = jnp.arange(2 * experts_dev * cap, dtype=jnp.int32)
        match = code_col[:, :, None] == slots
        weight = jnp.where(match, 1.0 if gates is None else gates[:, :, None], 0.0).sum(axis=1)
        rows = jnp.concatenate(
            [jnp.transpose(r, (1, 0, 2, 3)).reshape(blocks, -1, width) for r in rows_pair], axis=1
        )
        out = jnp.einsum("bts,bsd->btd", weight.reshape(blocks, BLK, -1), rows.astype(F32),
                         precision=lax.Precision.HIGHEST)
        return out.reshape(tokens, width).astype(out_dtype)
    row_spec = pl.BlockSpec((experts_dev, 1, cap, width), lambda b: (0, b, 0, 0))
    col_spec = pl.BlockSpec((BLK, 2), lambda b: (b, 0))
    args, specs = [code_col], [col_spec]
    if gates is not None:
        args.append(gates)
        specs.append(col_spec)
    return pl.pallas_call(
        partial(combine_kernel, experts_dev, cap, gates is not None),
        grid=(blocks,),
        out_shape=jax.ShapeDtypeStruct((tokens, width), out_dtype),
        in_specs=specs + [row_spec] * 2,
        out_specs=pl.BlockSpec((BLK, width), lambda b: (b, 0)),
        cost_estimate=pl.CostEstimate(
            flops=int(2 * blocks * 768 * BLK * width), bytes_accessed=int(4e6), transcendentals=0
        ),
        name="combine",
    )(*args, *rows_pair)


def gate_grad_kernel(experts_dev, cap, code_ref, g_ref, r0_ref, r1_ref, out_ref):
    half = experts_dev * cap
    upstream = g_ref[...].astype(BF)
    dots = jnp.concatenate(
        [fdot(upstream, gather_rows(r, experts_dev, cap), ((1,), (1,))) for r in (r0_ref, r1_ref)],
        axis=1,
    )
    slot_id = lax.broadcasted_iota(jnp.int32, (BLK, 2 * half), 1)
    for k in range(2):
        out_ref[:, k : k + 1] = jnp.sum(
            jnp.where(slot_id == code_ref[:, k : k + 1], dots, 0.0), axis=1, keepdims=True
        )


def gate_grad(g2, rows_pair, code_col, experts_dev, cap):
    tokens, width = g2.shape
    blocks = tokens // BLK
    if cap % 16 != 0:
        slots = jnp.arange(2 * experts_dev * cap, dtype=jnp.int32)
        match = code_col[:, :, None] == slots
        rows = jnp.concatenate(
            [jnp.transpose(r, (1, 0, 2, 3)).reshape(blocks, -1, width) for r in rows_pair], axis=1
        )
        dots = jnp.einsum("btd,bsd->bts", g2.reshape(blocks, BLK, width), rows.astype(F32),
                          precision=lax.Precision.HIGHEST)
        return jnp.sum(jnp.where(match, dots.reshape(tokens, 1, -1), 0.0), axis=2)
    row_spec = pl.BlockSpec((experts_dev, 1, cap, width), lambda b: (0, b, 0, 0))
    col_spec = pl.BlockSpec((BLK, 2), lambda b: (b, 0))
    return pl.pallas_call(
        partial(gate_grad_kernel, experts_dev, cap),
        grid=(blocks,),
        out_shape=jax.ShapeDtypeStruct((tokens, 2), F32),
        in_specs=[col_spec, pl.BlockSpec((BLK, width), lambda b: (b, 0)), row_spec, row_spec],
        out_specs=col_spec,
        cost_estimate=pl.CostEstimate(
            flops=int(2 * blocks * 768 * BLK * width), bytes_accessed=int(4e6), transcendentals=0
        ),
        name="gate_grad",
    )(code_col, g2, *rows_pair)


def dispatch_parts_kernel(devices, cap, weighted, code_ref, *rest):
    if weighted:
        gate_ref, x_ref, *outs = rest
    else:
        x_ref, *outs = rest
    slots = devices * cap * 2
    slot_id = lax.broadcasted_iota(jnp.int32, (slots, BLK), 0)
    first = slot_id == code_ref[0, 0:1, :]
    second = slot_id == code_ref[0, 1:2, :]
    pick = jnp.where(first | second, 1.0, 0.0).astype(BF)
    rows = fdot(pick, x_ref[...].astype(BF))
    if weighted:
        gate = jnp.sum(
            jnp.where(first, gate_ref[0, 0:1, :], 0.0) + jnp.where(second, gate_ref[0, 1:2, :], 0.0),
            axis=1,
            keepdims=True,
        )
        rows = rows * gate
    rows = rows.astype(BF)
    for part, out in enumerate(outs):
        for local in range(2):
            at = (local * devices + part) * cap
            out[local] = rows[at : at + cap]


def dispatch_parts(x, code_row, gate_row, devices, cap):
    tokens, width = x.shape
    blocks = tokens // BLK
    code_spec = pl.BlockSpec((1, 2, BLK), lambda b: (b, 0, 0))
    args, specs = [code_row], [code_spec]
    if gate_row is not None:
        args.append(gate_row)
        specs.append(code_spec)
    args.append(x)
    specs.append(pl.BlockSpec((BLK, width), lambda b: (b, 0)))
    return pl.pallas_call(
        partial(dispatch_parts_kernel, devices, cap, gate_row is not None),
        grid=(blocks,),
        out_shape=[jax.ShapeDtypeStruct((2, blocks * cap, width), BF)] * devices,
        in_specs=specs,
        out_specs=[pl.BlockSpec((2, cap, width), lambda b: (0, b, 0))] * devices,
        cost_estimate=pl.CostEstimate(
            flops=int(2 * blocks * 768 * BLK * width), bytes_accessed=int(4e6), transcendentals=0
        ),
        name="dispatch",
    )(*args)


def slot_rows(refs):
    return jnp.concatenate([ref[local] for local in range(2) for ref in refs], axis=0)


def combine_parts_kernel(devices, cap, weighted, code_ref, *rest):
    if weighted:
        gate_ref, *rest = rest
    parts, out_ref = rest[:devices], rest[devices]
    slot_id = lax.broadcasted_iota(jnp.int32, (BLK, 2 * devices * cap), 1)
    g0 = gate_ref[:, 0:1] if weighted else 1.0
    g1 = gate_ref[:, 1:2] if weighted else 1.0
    pick = jnp.where(slot_id == code_ref[:, 0:1], g0, 0.0) + jnp.where(
        slot_id == code_ref[:, 1:2], g1, 0.0
    )
    out_ref[...] = fdot(pick.astype(BF), slot_rows(parts)).astype(out_ref.dtype)


def combine_parts(parts, code_col, gates, devices, cap, out_dtype):
    tokens = code_col.shape[0]
    width = parts[0].shape[-1]
    blocks = tokens // BLK
    row_spec = pl.BlockSpec((2, cap, width), lambda b: (0, b, 0))
    col_spec = pl.BlockSpec((BLK, 2), lambda b: (b, 0))
    args, specs = [code_col], [col_spec]
    if gates is not None:
        args.append(gates)
        specs.append(col_spec)
    return pl.pallas_call(
        partial(combine_parts_kernel, devices, cap, gates is not None),
        grid=(blocks,),
        out_shape=jax.ShapeDtypeStruct((tokens, width), out_dtype),
        in_specs=specs + [row_spec] * devices,
        out_specs=pl.BlockSpec((BLK, width), lambda b: (b, 0)),
        cost_estimate=pl.CostEstimate(
            flops=int(2 * blocks * 768 * BLK * width), bytes_accessed=int(4e6), transcendentals=0
        ),
        name="combine",
    )(*args, *parts)


def gate_grad_parts_kernel(devices, cap, code_ref, route_ref, gate_ref, g_ref, *rest):
    parts, out_ref = rest[:devices], rest[devices]
    dots = fdot(g_ref[...].astype(BF), slot_rows(parts), ((1,), (1,)))
    slot_id = lax.broadcasted_iota(jnp.int32, (BLK, 2 * devices * cap), 1)
    d_gates = [
        jnp.sum(jnp.where(slot_id == code_ref[:, k : k + 1], dots, 0.0), axis=1, keepdims=True)
        for k in range(2)
    ]
    gates = [gate_ref[:, k : k + 1] for k in range(2)]
    centre = gates[0] * d_gates[0] + gates[1] * d_gates[1]
    expert_id = lax.broadcasted_iota(jnp.int32, out_ref.shape, 1)
    total = jnp.zeros(out_ref.shape, F32)
    for k in range(2):
        d_chosen = gates[k] * (d_gates[k] - centre)
        total = total + jnp.where(expert_id == route_ref[:, k : k + 1], d_chosen, 0.0)
    out_ref[...] = total


def logit_grad_parts(g2, parts, code_col, routes, gates, experts, devices, cap):
    tokens, width = g2.shape
    blocks = tokens // BLK
    row_spec = pl.BlockSpec((2, cap, width), lambda b: (0, b, 0))
    col_spec = pl.BlockSpec((BLK, 2), lambda b: (b, 0))
    return pl.pallas_call(
        partial(gate_grad_parts_kernel, devices, cap),
        grid=(blocks,),
        out_shape=jax.ShapeDtypeStruct((tokens, experts), F32),
        in_specs=[col_spec] * 3 + [pl.BlockSpec((BLK, width), lambda b: (b, 0))]
        + [row_spec] * devices,
        out_specs=pl.BlockSpec((BLK, experts), lambda b: (b, 0)),
        cost_estimate=pl.CostEstimate(
            flops=int(2 * blocks * 768 * BLK * width), bytes_accessed=int(4e6), transcendentals=0
        ),
        name="logit_grad",
    )(code_col, routes, gates, g2, *parts)


def return_grad_kernel(devices, cap, code_ref, dlog_ref, router_ref, *rest):
    parts, out_ref = rest[:devices], rest[devices]
    slot_id = lax.broadcasted_iota(jnp.int32, (BLK, 2 * devices * cap), 1)
    chosen = (slot_id == code_ref[:, 0:1]) | (slot_id == code_ref[:, 1:2])
    total = fdot(jnp.where(chosen, 1.0, 0.0).astype(BF), slot_rows(parts))
    router_term = lax.dot_general(
        dlog_ref[...],
        router_ref[...].astype(F32),
        (((1,), (1,)), ((), ())),
        precision=lax.Precision.HIGHEST,
        preferred_element_type=F32,
    )
    out_ref[...] = (total + router_term).astype(out_ref.dtype)


def return_grad(parts, code_col, d_logits, router, devices, cap):
    tokens = code_col.shape[0]
    width = parts[0].shape[-1]
    experts = router.shape[1]
    blocks = tokens // BLK
    return pl.pallas_call(
        partial(return_grad_kernel, devices, cap),
        grid=(blocks,),
        out_shape=jax.ShapeDtypeStruct((tokens, width), BF),
        in_specs=[
            pl.BlockSpec((BLK, 2), lambda b: (b, 0)),
            pl.BlockSpec((BLK, experts), lambda b: (b, 0)),
            pl.BlockSpec((width, experts), lambda b: (0, 0)),
        ]
        + [pl.BlockSpec((2, cap, width), lambda b: (0, b, 0))] * devices,
        out_specs=pl.BlockSpec((BLK, width), lambda b: (b, 0)),
        cost_estimate=pl.CostEstimate(
            flops=int(2 * blocks * 768 * BLK * width), bytes_accessed=int(4e6), transcendentals=0
        ),
        name="return_grad",
    )(code_col, d_logits, router, *parts)


def mix_kernel(zs, z_ref, route_ref, stream_ref, gain_ref, router_ref, w_ref, *rest):
    mixed = rest[:zs]
    mid_ref, normed_ref, gate_ref = rest[zs:]
    z_id = z_ref[0]
    hw = mixed[0].shape[1]
    mid = stream_ref[...]
    for step in range(zs):
        rows = pl.ds(pl.multiple_of((z_id ^ step) * hw, 64), hw)
        mid = mid + fdot(mixed[step][...], w_ref[rows, :])
    mid_ref[...] = mid
    inverse = lax.rsqrt(jnp.mean(mid * mid, axis=1, keepdims=True) + NORM_EPS)
    normed = (mid * inverse * gain_ref[...]).astype(BF)
    normed_ref[...] = normed
    logits = fdot(normed, router_ref[...])
    expert_id = lax.broadcasted_iota(jnp.int32, logits.shape, 1)
    first, second = [
        jnp.sum(jnp.where(expert_id == route_ref[:, k : k + 1], logits, 0.0), axis=1, keepdims=True)
        for k in range(2)
    ]
    top = jnp.maximum(first, second)
    first, second = jnp.exp(first - top), jnp.exp(second - top)
    total = first + second
    gate_ref[:, 0:1] = first / total
    gate_ref[:, 1:2] = second / total


def mix_forward(z_id, routes, stream, gain, router, w_out, mixed_list):
    tokens, width = stream.shape
    zs = len(mixed_list)
    hw = mixed_list[0].shape[1]
    experts = router.shape[1]
    row = lambda cols: pl.BlockSpec((BLK, cols), lambda b: (b, 0))
    full = lambda shape: pl.BlockSpec(shape, lambda b: (0, 0))
    return pl.pallas_call(
        partial(mix_kernel, zs),
        grid=(tokens // BLK,),
        out_shape=[
            jax.ShapeDtypeStruct((tokens, width), F32),
            jax.ShapeDtypeStruct((tokens, width), BF),
            jax.ShapeDtypeStruct((tokens, 2), F32),
        ],
        in_specs=[
            pl.BlockSpec(memory_space=pltpu.SMEM),
            row(2),
            row(width),
            full((1, width)),
            full((width, experts)),
            full((width, width)),
        ]
        + [row(hw)] * zs,
        out_specs=[row(width), row(width), row(2)],
        cost_estimate=pl.CostEstimate(
            flops=int(2 * tokens * width * width), bytes_accessed=int(6e6), transcendentals=0
        ),
        name="mix_fwd",
    )(z_id.reshape(1), routes, stream, gain.reshape(1, -1), router, w_out, *mixed_list)


def mix_bwd_kernel(z_ref, g_ref, mid_ref, dn_ref, gain_ref, w_ref, dmid_ref, dproj_ref, dmix_ref, gain_out):
    hw = dmix_ref.shape[1]
    mid = mid_ref[...]
    upstream = dn_ref[...].astype(F32)
    inverse = lax.rsqrt(jnp.mean(mid * mid, axis=1, keepdims=True) + NORM_EPS)
    scaled = upstream * gain_ref[...]
    inner_mean = jnp.mean(scaled * mid, axis=1, keepdims=True)
    d_mid = g_ref[...] + inverse * scaled - mid * (inverse * inverse * inverse) * inner_mean
    dmid_ref[...] = d_mid
    d_proj = d_mid.astype(BF)
    dproj_ref[...] = d_proj
    rows = pl.ds(pl.multiple_of(z_ref[0] * hw, 64), hw)
    dmix_ref[...] = fdot(d_proj, w_ref[rows, :], ((1,), (1,))).astype(BF)
    part = jnp.sum(upstream * mid * inverse, axis=0, keepdims=True)

    @pl.when(pl.program_id(0) == 0)
    def _():
        gain_out[...] = jnp.zeros_like(gain_out)

    gain_out[...] += part


def mix_backward(z_id, g2, mid, d_normed, gain, w_out, hw):
    tokens, width = mid.shape
    row = lambda cols: pl.BlockSpec((BLK, cols), lambda b: (b, 0))
    full = lambda shape: pl.BlockSpec(shape, lambda b: (0, 0))
    return pl.pallas_call(
        mix_bwd_kernel,
        grid=(tokens // BLK,),
        out_shape=[
            jax.ShapeDtypeStruct((tokens, width), F32),
            jax.ShapeDtypeStruct((tokens, width), BF),
            jax.ShapeDtypeStruct((tokens, hw), BF),
            jax.ShapeDtypeStruct((1, width), F32),
        ],
        in_specs=[
            pl.BlockSpec(memory_space=pltpu.SMEM),
            row(width),
            row(width),
            row(width),
            full((1, width)),
            full((width, width)),
        ],
        out_specs=[row(width), row(width), row(hw), full((1, width))],
        cost_estimate=pl.CostEstimate(
            flops=int(2 * tokens * width * hw), bytes_accessed=int(8e6), transcendentals=0
        ),
        name="mix_bwd",
    )(z_id.reshape(1), g2, mid, d_normed, gain.reshape(1, -1), w_out)


GELU_A = 0.7978845608028654
GELU_B = 0.044715


def expert_fwd_kernel(devices, *refs):
    parts, (first_ref, second_ref) = refs[:devices], refs[devices : devices + 2]
    rows_ref, inner_ref, hidden_ref, *outs = refs[devices + 2 :]
    rows = jnp.concatenate([part[0] for part in parts], axis=0)
    rows_ref[0] = rows
    inner = fdot(rows, first_ref[0, 0])
    inner_ref[0] = inner.astype(inner_ref.dtype)
    wave = jnp.tanh(GELU_A * (inner + GELU_B * (inner * inner * inner)))
    hidden = (0.5 * inner * (1.0 + wave)).astype(BF)
    hidden_ref[0] = hidden
    result = fdot(hidden, second_ref[0, 0]).astype(BF)
    size = parts[0].shape[1]
    for part, out in enumerate(outs):
        out[0] = result[part * size : (part + 1) * size]


def expert_forward(parts, first, second, layer):
    devices = len(parts)
    _, size, width = parts[0].shape
    hid = first.shape[3]
    part_spec = pl.BlockSpec((1, size, width), lambda l: (l, 0, 0))
    outs = pl.pallas_call(
        partial(expert_fwd_kernel, devices),
        grid=(2,),
        out_shape=[
            jax.ShapeDtypeStruct((2, devices * size, width), BF),
            jax.ShapeDtypeStruct((2, devices * size, hid), F32),
            jax.ShapeDtypeStruct((2, devices * size, hid), BF),
        ]
        + [jax.ShapeDtypeStruct((2, size, width), BF)] * devices,
        in_specs=[part_spec] * devices
        + [
            pl.BlockSpec((1, 1, width, hid), lambda l: (layer, l, 0, 0)),
            pl.BlockSpec((1, 1, hid, width), lambda l: (layer, l, 0, 0)),
        ],
        out_specs=[
            pl.BlockSpec((1, devices * size, width), lambda l: (l, 0, 0)),
            pl.BlockSpec((1, devices * size, hid), lambda l: (l, 0, 0)),
            pl.BlockSpec((1, devices * size, hid), lambda l: (l, 0, 0)),
        ]
        + [part_spec] * devices,
        cost_estimate=pl.CostEstimate(
            flops=int(8 * devices * size * width * hid), bytes_accessed=int(20e6), transcendentals=0
        ),
        name="expert_fwd",
    )(*parts, first, second)
    return outs[0], outs[1], outs[2], list(outs[3:])


def expert_bwd_kernel(devices, *refs):
    parts = refs[:devices]
    inner_ref, first_ref, second_ref = refs[devices : devices + 3]
    rows_ref, dinner_ref, *outs = refs[devices + 3 :]
    rows = jnp.concatenate([part[0] for part in parts], axis=0)
    rows_ref[0] = rows
    d_hidden = fdot(rows, second_ref[0, 0], ((1,), (1,)))
    inner = inner_ref[0]
    square = inner * inner
    wave = jnp.tanh(GELU_A * inner * (1.0 + GELU_B * square))
    slope = 0.5 * (1.0 + wave) + (0.5 * GELU_A) * inner * (1.0 - wave * wave) * (
        1.0 + (3.0 * GELU_B) * square
    )
    d_inner = (d_hidden * slope).astype(BF)
    dinner_ref[0] = d_inner
    d_rows = fdot(d_inner, first_ref[0, 0], ((1,), (1,))).astype(BF)
    size = parts[0].shape[1]
    for part, out in enumerate(outs):
        out[0] = d_rows[part * size : (part + 1) * size]


def expert_backward(parts, inner, first, second, layer):
    devices = len(parts)
    _, size, width = parts[0].shape
    hid = first.shape[3]
    part_spec = pl.BlockSpec((1, size, width), lambda l: (l, 0, 0))
    outs = pl.pallas_call(
        partial(expert_bwd_kernel, devices),
        grid=(2,),
        out_shape=[
            jax.ShapeDtypeStruct((2, devices * size, width), BF),
            jax.ShapeDtypeStruct((2, devices * size, hid), BF),
        ]
        + [jax.ShapeDtypeStruct((2, size, width), BF)] * devices,
        in_specs=[part_spec] * devices
        + [
            pl.BlockSpec((1, devices * size, hid), lambda l: (l, 0, 0)),
            pl.BlockSpec((1, 1, width, hid), lambda l: (layer, l, 0, 0)),
            pl.BlockSpec((1, 1, hid, width), lambda l: (layer, l, 0, 0)),
        ],
        out_specs=[
            pl.BlockSpec((1, devices * size, width), lambda l: (l, 0, 0)),
            pl.BlockSpec((1, devices * size, hid), lambda l: (l, 0, 0)),
        ]
        + [part_spec] * devices,
        cost_estimate=pl.CostEstimate(
            flops=int(8 * devices * size * width * hid), bytes_accessed=int(20e6), transcendentals=0
        ),
        name="expert_bwd",
    )(*parts, inner, first, second)
    return outs[0], outs[1], list(outs[2:])


def expert_grad_kernel(chunks, aliased, *refs):
    groups = [refs[4 * c : 4 * c + 4] for c in range(chunks)]
    first_out, second_out = refs[-2:]

    first = second = None
    for rows, d_inner, hidden, d_res in groups:
        one = fdot(rows[0], d_inner[0], ((0,), (0,)))
        two = fdot(hidden[0], d_res[0], ((0,), (0,)))
        first = one if first is None else first + one
        second = two if second is None else second + two
    first_out[0, 0] = first
    second_out[0, 0] = second


def expert_grads(groups, layer, layers, previous):
    _, size, width = groups[0][0].shape
    hid = groups[0][1].shape[2]
    row_spec = pl.BlockSpec((1, size, width), lambda l: (l, 0, 0))
    hid_spec = pl.BlockSpec((1, size, hid), lambda l: (l, 0, 0))
    args, specs = [], []
    for group in groups:
        args += list(group)
        specs += [row_spec, hid_spec, hid_spec, row_spec]
    aliases = {}
    if previous is not None:
        aliases = {len(args): 0, len(args) + 1: 1}
        args += list(previous)
        specs += [pl.BlockSpec(memory_space=pl.ANY)] * 2
    return pl.pallas_call(
        partial(expert_grad_kernel, len(groups), previous is not None),
        grid=(2,),
        out_shape=[
            jax.ShapeDtypeStruct((layers, 2, width, hid), F32),
            jax.ShapeDtypeStruct((layers, 2, hid, width), F32),
        ],
        in_specs=specs,
        out_specs=[
            pl.BlockSpec((1, 1, width, hid), lambda l: (layer, l, 0, 0)),
            pl.BlockSpec((1, 1, hid, width), lambda l: (layer, l, 0, 0)),
        ],
        input_output_aliases=aliases,
        cost_estimate=pl.CostEstimate(
            flops=int(8 * len(groups) * size * width * hid),
            bytes_accessed=int(30e6),
            transcendentals=0,
        ),
        name="expert_grad",
    )(*args)


def spread(x, axis_name):
    return lax.all_to_all(x, axis_name, split_axis=0, concat_axis=0, tiled=True)


def swap(x, axis_name, step):
    size = lax.axis_size(axis_name)
    return lax.ppermute(x, axis_name, [(i, i ^ step) for i in range(size)])


def swap_parts(parts, axis_name):
    return [part if step == 0 else swap(part, axis_name, step) for step, part in enumerate(parts)]


def spread_gather(x, axis_name):
    size = lax.axis_size(axis_name)
    return spread(jnp.broadcast_to(x[None], (size,) + x.shape), axis_name)


def reduce_rows(x):
    zs, z_id = lax.axis_size("seq"), lax.axis_index("seq")
    pieces = x.reshape(zs, -1, x.shape[1])
    total = lax.dynamic_index_in_dim(pieces, z_id, 0, keepdims=False).astype(F32)
    for step in range(1, zs):
        piece = lax.dynamic_index_in_dim(pieces, z_id ^ step, 0, keepdims=False)
        total = total + swap(piece, "seq", step).astype(F32)
    return total


def sum_rows(x):
    zs, z_id = lax.axis_size("seq"), lax.axis_index("seq")
    steps = [1 << bit for bit in range(zs.bit_length() - 1)]
    total = x
    for step in steps:
        half = total.shape[0] // 2
        upper = (z_id & step) != 0
        low, high = total[:half], total[half:]
        got = swap(jnp.where(upper, low, high), "seq", step)
        total = (jnp.where(upper, high, low).astype(F32) + got.astype(F32)).astype(BF)
    for step in reversed(steps):
        upper = (z_id & step) != 0
        got = swap(total, "seq", step)
        total = jnp.concatenate(
            [jnp.where(upper, got, total), jnp.where(upper, total, got)], axis=0
        )
    return total


def split_dense_kernel(zs, es, rows, in_ref, out_ref, in_send, out_send):
    for dest in range(es):
        pieces = [
            in_ref[(plane * es + dest) * rows : (plane * es + dest + 1) * rows] for plane in range(zs)
        ]
        in_send[dest] = jnp.concatenate(pieces, axis=0).astype(BF)
        out_send[dest] = out_ref[dest * rows : (dest + 1) * rows].astype(BF)


def split_dense(total_in, total_out, zs, es, rows):
    wide, width = total_in.shape[1], total_out.shape[1]
    if rows % 8 != 0:
        in_send = jnp.transpose(total_in.reshape(zs, es, rows, wide), (1, 0, 2, 3))
        return (
            in_send.reshape(es, zs * rows, wide).astype(BF),
            total_out.reshape(es, rows, width).astype(BF),
        )
    return pl.pallas_call(
        partial(split_dense_kernel, zs, es, rows),
        out_shape=[
            jax.ShapeDtypeStruct((es, zs * rows, wide), BF),
            jax.ShapeDtypeStruct((es, rows, width), BF),
        ],
        in_specs=[VM] * 2,
        out_specs=[VM] * 2,
        cost_estimate=pl.CostEstimate(flops=int(1e6), bytes_accessed=int(4e6), transcendentals=0),
        name="split_dense",
    )(total_in, total_out)


def norm_forward(stream, gain):
    inverse = lax.rsqrt(jnp.mean(stream * stream, axis=-1, keepdims=True) + NORM_EPS)
    return (stream * inverse * gain).astype(BF), inverse


def norm_backward(stream, inverse, gain, upstream):
    scaled = upstream * gain
    inner_mean = jnp.mean(scaled * stream, axis=-1, keepdims=True)
    d_stream = inverse * scaled - stream * (inverse * inverse * inverse) * inner_mean
    return d_stream, jnp.sum(upstream * stream * inverse, axis=0)


def slot_codes(routes, experts, experts_dev, cap, flip):
    blocks = routes.shape[0] // BLK
    flat = routes.reshape(blocks, BLK * 2)
    onehot = (flat[:, :, None] == jnp.arange(experts, dtype=jnp.int32)).astype(F32)
    steps = jnp.arange(BLK * 2, dtype=jnp.int32)
    before = (steps[:, None] > steps[None, :]).astype(F32)
    count = jnp.einsum("ij,bje->bie", before, onehot, preferred_element_type=F32)
    place = jnp.sum(count * onehot, axis=2).astype(jnp.int32)
    code = (flat % 2) * (experts_dev * cap) + ((flat // 2) ^ flip) * cap + place
    return code.reshape(blocks * BLK, 2)


def body(
    tokens,
    cotangent,
    segments,
    buckets,
    routes,
    attend_in,
    attend_out,
    router_weight,
    gain_attend,
    gain_expert,
    bias_table,
    expert_in,
    expert_out,
):
    zs = lax.axis_size("seq")
    es = lax.axis_size("expert")
    z_id = lax.axis_index("seq")
    own_rows, width = tokens.shape[1:]
    length = segments.shape[1]
    layers, shard_rows = attend_in.shape[:2]
    experts = router_weight.shape[2]
    cap = 3 * own_rows // experts
    heads_all = width // HD
    heads = heads_all // zs
    hw = heads * HD
    bucket_count = bias_table.shape[1] * zs * es // heads_all
    chunks = CHUNKS
    rows_c = length // chunks

    def split(x):
        return [x[c * rows_c : (c + 1) * rows_c] for c in range(chunks)]

    route_rows = routes[0].astype(BF).reshape(-1, width) if (own_rows * 2) % width == 0 else None
    if route_rows is None:
        flat_routes = routes[0].astype(BF).reshape(-1)
        pad = -flat_routes.shape[0] % (16 * width)
        route_rows = jnp.pad(flat_routes, (0, pad)).reshape(-1, width)
    packed = lax.all_gather(jnp.concatenate([tokens[0], route_rows], axis=0), "seq", axis=0)
    stream_full = packed[:, :own_rows].reshape(length, width)
    routes_full = (
        packed[:, own_rows:].reshape(zs, -1)[:, : own_rows * 2].reshape(length, 2).astype(jnp.int32)
    )

    small = jnp.concatenate(
        [
            gain_attend.reshape(-1),
            gain_expert.reshape(-1),
            bias_table.reshape(-1),
            router_weight.reshape(-1),
        ]
    )
    small = spread_gather(spread_gather(small, "expert"), "seq").reshape(zs * es, -1)
    sizes = [layers * shard_rows, layers * shard_rows, layers * bias_table.shape[1]]
    at = 0
    parts = []
    for size in sizes:
        parts.append(small[:, at : at + size])
        at += size
    gains_a = jnp.transpose(parts[0].reshape(-1, layers, shard_rows), (1, 0, 2)).reshape(layers, width)
    gains_e = jnp.transpose(parts[1].reshape(-1, layers, shard_rows), (1, 0, 2)).reshape(layers, width)
    bias_all = jnp.transpose(
        parts[2].reshape(-1, layers, bias_table.shape[1]), (1, 0, 2)
    ).reshape(layers, heads_all, bucket_count)
    routers = jnp.transpose(
        small[:, at:].reshape(-1, layers, shard_rows, experts), (1, 0, 2, 3)
    ).reshape(layers, width, experts)
    gains_a = gains_a.astype(F32)
    gains_e = gains_e.astype(F32)

    piece = attend_in.reshape(layers, shard_rows, 3, zs, hw)
    piece = jnp.transpose(piece, (3, 0, 1, 2, 4)).reshape(zs, layers, shard_rows, 3 * hw)
    piece = spread(piece, "seq")
    piece = lax.all_gather(piece, "expert", axis=0)
    piece = jnp.transpose(piece, (2, 1, 0, 3, 4)).reshape(layers, width, 3 * hw)
    w_in_list = [piece[layer] for layer in range(layers)]
    w_out_list = [
        lax.all_gather(attend_out[layer], ("seq", "expert"), axis=0, tiled=True)
        for layer in range(layers)
    ]

    steps = length - jnp.arange(length + BLK, dtype=jnp.int32)
    rev_buckets = jnp.concatenate(
        [buckets[length - 1 :], buckets[::-1], jnp.broadcast_to(buckets[:1], (BLK - 1,))]
    )
    rev_hot = (rev_buckets[:, None] == jnp.arange(bucket_count, dtype=jnp.int32)).astype(F32)
    segrow = segments
    segcol = segments.reshape(length, 1)

    fast = cap % 16 == 0
    flip = lax.axis_index("expert") if fast else 0
    code_full = slot_codes(routes_full, experts, es, cap, flip)
    code_col = split(code_full)
    code_row_full = jnp.transpose(code_full.reshape(-1, BLK, 2), (0, 2, 1))
    blocks_c = rows_c // BLK
    code_row = [code_row_full[c * blocks_c : (c + 1) * blocks_c] for c in range(chunks)]
    route_hot = split(routes_full[..., None] == jnp.arange(experts, dtype=jnp.int32))
    routes_c = split(routes_full)
    expert_outs = None

    def exchange(pair):
        return [
            spread(r.reshape(es, -1, width), "expert").reshape(-1, width) for r in pair
        ]

    def exchange_back(pair):
        return [
            spread(r.reshape(es, -1, width), "expert").reshape(es, blocks_c, cap, width) for r in pair
        ]

    stream = split(stream_full.astype(F32))
    saved = []
    block_out = None
    for layer in range(layers):
        w_in, w_out = w_in_list[layer], w_out_list[layer]
        local_bias = lax.dynamic_slice_in_dim(bias_all[layer], z_id * heads, heads, 0)
        rev_bias = fdot(local_bias, rev_hot.astype(BF), ((1,), (1,)))
        keep = dict(stream=stream, rev_bias=rev_bias, chunks=[])
        qkv = []
        mids, partials = [], []
        for c in range(chunks):
            normed, inv_a = norm_forward(stream[c], gains_a[layer])
            qkv.append(fdot(normed, w_in).astype(BF))
            mixed = attend_forward(c, rev_bias, segcol, segrow, qkv)
            if layer == 0 and c == 0:
                held = lax.optimization_barrier((cotangent, mixed[:8, :128]))[0]
                upstream_full = lax.all_gather(held[0], "seq", axis=0, tiled=True)
            mixed_list = [mixed] + [swap(mixed, "seq", step) for step in range(1, zs)]
            mid, normed_mid, gates = mix_forward(
                z_id, routes_c[c], stream[c], gains_e[layer], routers[layer], w_out, mixed_list
            )
            if fast:
                got = swap_parts(dispatch_parts(normed_mid, code_row[c], None, es, cap), "expert")
                rows, inner, hidden, result = expert_forward(got, expert_in, expert_out, layer)
                back = swap_parts(result, "expert")
                partials.append(combine_parts(back, code_col[c], gates, es, cap, BF))
            else:
                rows = exchange(dispatch(normed_mid, code_row[c], None, es, cap))
                inner, hidden, result = [], [], []
                for loc in range(2):
                    pre = fdot(rows[loc], expert_in[layer, loc])
                    hid = jax.nn.gelu(pre).astype(BF)
                    inner.append(pre)
                    hidden.append(hid)
                    result.append(fdot(hid, expert_out[layer, loc]).astype(BF))
                back = exchange_back(result)
                partials.append(combine(back, code_col[c], gates, es, cap, BF))
            mids.append(mid)
            keep["chunks"].append(
                dict(normed=normed, inv_a=inv_a, mixed=mixed, mid=mid, normed_mid=normed_mid,
                     gates=gates, rows=rows, inner=inner, hidden=hidden, back=back)
            )
        keep["qkv"] = qkv
        saved.append(keep)
        if layer + 1 < layers:
            stream = [mids[c] + sum_rows(partials[c]).astype(F32) for c in range(chunks)]
        else:
            delta = reduce_rows(jnp.concatenate(partials, axis=0))
            mid_own = lax.dynamic_slice_in_dim(
                jnp.concatenate(mids, axis=0), z_id * own_rows, own_rows, 0
            )
            block_out = (mid_own + delta.astype(F32)).astype(BF)

    upstream = split(upstream_full.astype(F32))
    in_grads, out_grads = [None] * layers, [None] * layers
    first_grads, second_grads = [None] * layers, [None] * layers
    small_grads = [None] * layers
    tokens_grad = None
    for layer in reversed(range(layers)):
        keep = saved[layer]
        w_in, w_out = w_in_list[layer], w_out_list[layer]
        d_mids, d_parts = [None] * chunks, [None] * chunks
        total_in = total_out = total_router = total_ga = total_ge = total_fold = None
        g_first = [None, None]
        g_second = [None, None]
        acc = None
        grad_groups = []

        def plus(left, right):
            return right if left is None else left + right

        for c in reversed(range(chunks)):
            k = keep["chunks"][c]
            g2 = upstream[c]
            gates = k["gates"]
            gate_row = jnp.transpose(gates.reshape(blocks_c, BLK, 2), (0, 2, 1))
            if fast:
                got = swap_parts(dispatch_parts(g2, code_row[c], gate_row, es, cap), "expert")
                d_res, d_inner, d_rows = expert_backward(
                    got, k["inner"], expert_in, expert_out, layer
                )
                d_back = swap_parts(d_rows, "expert")
                grad_groups.append((k["rows"], d_inner, k["hidden"], d_res))
                d_logits = logit_grad_parts(
                    g2, k["back"], code_col[c], routes_c[c], gates, experts, es, cap
                )
                partial_d = return_grad(d_back, code_col[c], d_logits, routers[layer], es, cap)
            else:
                d_res = exchange(dispatch(g2, code_row[c], gate_row, es, cap))
                d_rows = []
                for loc in range(2):
                    d_hid = fdot(d_res[loc], expert_out[layer, loc], ((1,), (1,)))
                    _, pull = jax.vjp(jax.nn.gelu, k["inner"][loc])
                    d_inner = pull(d_hid)[0].astype(BF)
                    d_rows.append(fdot(d_inner, expert_in[layer, loc], ((1,), (1,))).astype(BF))
                    g_second[loc] = plus(
                        g_second[loc], fdot(k["hidden"][loc], d_res[loc], ((0,), (0,)))
                    )
                    g_first[loc] = plus(g_first[loc], fdot(k["rows"][loc], d_inner, ((0,), (0,))))
                d_back = exchange_back(d_rows)
                d_gates = gate_grad(g2, k["back"], code_col[c], es, cap)
                d_moved = combine(d_back, code_col[c], None, es, cap, F32)
                d_chosen = gates * (d_gates - jnp.sum(gates * d_gates, axis=-1, keepdims=True))
                d_logits = jnp.sum(jnp.where(route_hot[c], d_chosen[..., None], 0.0), axis=1)
                partial_d = d_moved + exact_dot(d_logits, routers[layer].astype(F32).T)
            total_router = plus(
                total_router, exact_dot(k["normed_mid"].astype(F32).T, d_logits)
            )
            d_normed_mid = sum_rows(partial_d.astype(BF))
            d_mid, d_proj, d_mixed, ge = mix_backward(
                z_id, g2, k["mid"], d_normed_mid, gains_e[layer], w_out, hw
            )
            total_ge = plus(total_ge, ge)
            total_out = plus(total_out, fdot(k["mixed"], d_proj, ((0,), (0,))))
            d_qkv, fold, acc = attend_backward(
                c, keep["rev_bias"], segcol, segrow, d_mixed, keep["qkv"], acc
            )
            total_fold = plus(total_fold, fold)
            total_in = plus(total_in, fdot(k["normed"], d_qkv, ((0,), (0,))))
            d_parts[c] = fdot(d_qkv, w_in, ((1,), (1,))).astype(BF)
            d_mids[c] = d_mid
            if layer > 0:
                d_normed = sum_rows(d_parts[c]).astype(F32)
                d_in, ga = norm_backward(keep["stream"][c], k["inv_a"], gains_a[layer], d_normed)
                total_ga = plus(total_ga, ga)
                upstream[c] = d_in + d_mid
        own = (jnp.arange(zs) == z_id).astype(F32)[:, None]
        if layer == 0:
            d_normed = reduce_rows(jnp.concatenate(d_parts, axis=0))

            def mine(items):
                return lax.dynamic_slice_in_dim(
                    jnp.concatenate(items, axis=0), z_id * own_rows, own_rows, 0
                )

            stream_own = mine(keep["stream"])
            inv_own = mine([keep["chunks"][c]["inv_a"] for c in range(chunks)])
            d_in, ga = norm_backward(stream_own, inv_own, gains_a[layer], d_normed)
            tokens_grad = (d_in + mine(d_mids)).astype(BF)
            gain_a_part = ga.reshape(zs, -1)
        else:
            gain_a_part = total_ga.reshape(zs, -1) * own
        gain_e_part = total_ge.reshape(zs, -1) * own
        fold = total_fold.reshape(heads, BACK, 2 * BLK)
        hot = jnp.stack(
            [
                jnp.concatenate(
                    [
                        rev_hot[length - BLK * back : length - BLK * (back - 1)],
                        rev_hot[length - BLK * (back + 1) : length - BLK * back],
                    ],
                    axis=0,
                )
                for back in range(BACK)
            ]
        )
        table = exact_dot(fold.reshape(heads, -1), hot.reshape(-1, bucket_count))
        table_part = table.reshape(1, -1) * own
        router_part = total_router.reshape(zs, es, shard_rows * experts)
        small_grads[layer] = jnp.concatenate(
            [
                router_part,
                gain_a_part.reshape(zs, es, -1),
                gain_e_part.reshape(zs, es, -1),
                table_part.reshape(zs, es, -1),
            ],
            axis=-1,
        )
        in_send, out_send = split_dense(total_in, total_out, zs, es, shard_rows)
        piece = jnp.sum(spread(in_send, "expert").astype(F32), axis=0)
        out_grads[layer] = jnp.sum(spread(out_send, "expert").astype(F32), axis=0)
        piece = spread(piece.reshape(zs, shard_rows, 3 * hw).astype(BF), "seq").astype(F32)
        piece = jnp.transpose(piece.reshape(zs, shard_rows, 3, hw), (1, 2, 0, 3))
        in_grads[layer] = piece.reshape(shard_rows, 3 * width)
        if fast:
            expert_outs = expert_grads(grad_groups, layer, layers, expert_outs)
        else:
            first_grads[layer] = jnp.stack(g_first)
            second_grads[layer] = jnp.stack(g_second)

    if not fast:
        expert_outs = (jnp.stack(first_grads), jnp.stack(second_grads))
    packed_small = jnp.stack(small_grads, axis=2)
    packed_small = jnp.transpose(packed_small, (1, 0, 2, 3))
    packed_small = jnp.sum(spread(packed_small, "expert"), axis=0)
    packed_small = jnp.sum(spread(packed_small, "seq"), axis=0)
    r_size = shard_rows * experts
    router_grad = packed_small[:, :r_size].reshape(layers, shard_rows, experts)
    ga_grad = packed_small[:, r_size : r_size + shard_rows]
    ge_grad = packed_small[:, r_size + shard_rows : r_size + 2 * shard_rows]
    table_grad = packed_small[:, r_size + 2 * shard_rows :]
    return (
        block_out[None],
        tokens_grad[None],
        jnp.stack(in_grads),
        jnp.stack(out_grads),
        router_grad,
        ga_grad,
        ge_grad,
        table_grad,
        expert_outs[0],
        expert_outs[1],
    )


def solution(mesh):
    both = ("seq", "expert")
    return jax.shard_map(
        body,
        mesh=mesh,
        in_specs=(
            P("expert", "seq", None),
            P("expert", "seq", None),
            P("expert", None),
            P(),
            P("expert", "seq", None),
            P(None, both, None),
            P(None, both, None),
            P(None, both, None),
            P(None, both),
            P(None, both),
            P(None, both),
            P(None, "expert", None, "seq"),
            P(None, "expert", "seq", None),
        ),
        out_specs=(
            P("expert", "seq", None),
            P("expert", "seq", None),
            P(None, both, None),
            P(None, both, None),
            P(None, both, None),
            P(None, both),
            P(None, both),
            P(None, both),
            P(None, "expert", None, "seq"),
            P(None, "expert", "seq", None),
        ),
        check_vma=False,
    )
```

```python
from functools import partial
import math

import jax
import jax.numpy as jnp
from jax import lax
from jax.experimental import pallas as pl
from jax.experimental.pallas import tpu as pltpu
from jax.sharding import PartitionSpec as P

HD = 64
BLK = 256
BACK = 3
CHUNKS = 2
NORM_EPS = 1e-06
MASKED = -1000000000.0
BF = jnp.bfloat16
F32 = jnp.float32


def fdot(left, right, dims=((1,), (0,))):
    return lax.dot_general(left, right, (dims, ((), ())), preferred_element_type=F32)


def exact_dot(left, right):
    return jnp.dot(left, right, precision=lax.Precision.HIGHEST, preferred_element_type=F32)


def toeplitz_rows(rev_ref, head, back, length):
    start = length - BLK * back
    line = jnp.concatenate(
        [rev_ref[head : head + 1, start : start + BLK], rev_ref[head : head + 1, start - BLK : start]],
        axis=1,
    )
    rows = jnp.broadcast_to(line, (8, 2 * BLK))
    row_id = lax.broadcasted_iota(jnp.int32, rows.shape, 0)
    for bit in (1, 2, 4):
        rows = jnp.where((row_id & bit) != 0, pltpu.roll(rows, bit, 1), rows)
    size = 8
    while size < BLK:
        rows = jnp.concatenate([rows, pltpu.roll(rows, size, 1)], axis=0)
        size *= 2
    return rows[:, :BLK]


def toeplitz_fold(grid):
    rows = jnp.concatenate([grid, jnp.zeros_like(grid)], axis=1)
    width = 2 * BLK
    size = BLK // 2
    while size >= 8:
        rows = rows[:size] + pltpu.roll(rows[size:], width - size, 1)
        size //= 2
    row_id = lax.broadcasted_iota(jnp.int32, rows.shape, 0)
    for bit in (1, 2, 4):
        rows = jnp.where((row_id & bit) != 0, pltpu.roll(rows, width - bit, 1), rows)
    return jnp.sum(rows, axis=0, keepdims=True)


def key_span(query_block):
    return list(range(max(0, query_block - BACK + 1), query_block + 1))


def allowed_mask(segcol_ref, segrow_ref, query_block):
    span = key_span(query_block)
    first = span[0] * BLK
    own = segcol_ref[query_block * BLK : (query_block + 1) * BLK, :]
    theirs = segrow_ref[:, first : (query_block + 1) * BLK]
    same = own == theirs
    shape = (BLK, len(span) * BLK)
    rows = lax.broadcasted_iota(jnp.int32, shape, 0) + query_block * BLK
    cols = lax.broadcasted_iota(jnp.int32, shape, 1) + first
    return same & (cols <= rows)


def head_cols(part, head, width):
    return slice(part * width + head * HD, part * width + (head + 1) * HD)


def block_of(refs, per_chunk, block, cols):
    inner = block % per_chunk
    return refs[block // per_chunk][inner * BLK : (inner + 1) * BLK, cols]


def attend_fwd_kernel(chunk, per_chunk, heads, length, rev_ref, segcol_ref, segrow_ref, *rest):
    qkv_refs, out_ref, grid_ref = rest[: chunk + 1], rest[chunk + 1], rest[chunk + 2]
    width = heads * HD
    backs = min(BACK, (chunk + 1) * per_chunk)
    for head in range(heads):
        for back in range(backs):
            grid_ref[head * BACK + back] = toeplitz_rows(rev_ref, head, back, length)
    for inner in range(per_chunk):
        query_block = chunk * per_chunk + inner
        span = key_span(query_block)
        allowed = allowed_mask(segcol_ref, segrow_ref, query_block)
        for head in range(heads):
            query = block_of(qkv_refs, per_chunk, query_block, head_cols(0, head, width))
            scores = jnp.concatenate(
                [
                    fdot(query, block_of(qkv_refs, per_chunk, kb, head_cols(1, head, width)), ((1,), (1,)))
                    * (1.0 / math.sqrt(HD))
                    + grid_ref[head * BACK + query_block - kb]
                    for kb in span
                ],
                axis=1,
            )
            scores = jnp.where(allowed, scores, MASKED)
            top = jnp.max(scores, axis=1, keepdims=True)
            weights = jnp.exp(scores - top)
            weights = weights * (1.0 / jnp.sum(weights, axis=1, keepdims=True))
            probs = weights.astype(BF)
            mixed = sum(
                fdot(
                    probs[:, pos * BLK : (pos + 1) * BLK],
                    block_of(qkv_refs, per_chunk, kb, head_cols(2, head, width)),
                )
                for pos, kb in enumerate(span)
            )
            out_ref[inner * BLK : (inner + 1) * BLK, head * HD : (head + 1) * HD] = mixed.astype(BF)


def attend_bwd_kernel(
    chunk, per_chunk, heads, length, has_acc, rev_ref, segcol_ref, segrow_ref, dmix_ref, *rest
):
    rest = list(rest)
    qkv_refs = [rest.pop(0) for _ in range(chunk + 1)]
    acc_in = [rest.pop(0) for _ in range(chunk + 1)] if has_acc else None
    dqkv_ref = rest.pop(0)
    fold_ref = rest.pop(0)
    acc_out = [rest.pop(0) for _ in range(chunk)]
    grid_ref, dgrid_ref, own_acc = rest
    width = heads * HD
    backs = min(BACK, (chunk + 1) * per_chunk)
    accs = acc_out + [own_acc]
    for pos, acc in enumerate(accs):
        acc[...] = acc_in[pos][...] if has_acc else jnp.zeros_like(acc)
    dgrid_ref[...] = jnp.zeros_like(dgrid_ref)
    for head in range(heads):
        for back in range(backs):
            grid_ref[head * BACK + back] = toeplitz_rows(rev_ref, head, back, length)
    scale = 1.0 / math.sqrt(HD)
    for inner in range(per_chunk):
        query_block = chunk * per_chunk + inner
        own_rows = slice(inner * BLK, (inner + 1) * BLK)
        span = key_span(query_block)
        allowed = allowed_mask(segcol_ref, segrow_ref, query_block)
        for head in range(heads):
            query = block_of(qkv_refs, per_chunk, query_block, head_cols(0, head, width))
            keys = [block_of(qkv_refs, per_chunk, kb, head_cols(1, head, width)) for kb in span]
            values = [block_of(qkv_refs, per_chunk, kb, head_cols(2, head, width)) for kb in span]
            d_mixed = dmix_ref[own_rows, head * HD : (head + 1) * HD]
            scores = jnp.concatenate(
                [
                    fdot(query, key, ((1,), (1,))) * scale + grid_ref[head * BACK + query_block - kb]
                    for key, kb in zip(keys, span)
                ],
                axis=1,
            )
            scores = jnp.where(allowed, scores, MASKED)
            top = jnp.max(scores, axis=1, keepdims=True)
            weights = jnp.exp(scores - top)
            weights = weights * (1.0 / jnp.sum(weights, axis=1, keepdims=True))
            d_soft = jnp.concatenate([fdot(d_mixed, value, ((1,), (1,))) for value in values], axis=1)
            inner_sum = jnp.sum(d_soft * weights, axis=1, keepdims=True)
            d_scores = (weights * (d_soft - inner_sum)).astype(BF)
            probs = weights.astype(BF)
            d_query = jnp.zeros((BLK, HD), F32)
            for pos, kb in enumerate(span):
                cols = slice(pos * BLK, (pos + 1) * BLK)
                piece = d_scores[:, cols]
                d_query = d_query + fdot(piece, keys[pos])
                dgrid_ref[head * BACK + query_block - kb] += piece.astype(F32)
                acc = accs[kb // per_chunk]
                rows = slice((kb % per_chunk) * BLK, (kb % per_chunk + 1) * BLK)
                acc[rows, head_cols(0, head, width)] += fdot(piece, query, ((0,), (0,))) * scale
                acc[rows, head_cols(1, head, width)] += fdot(probs[:, cols], d_mixed, ((0,), (0,)))
            dqkv_ref[own_rows, head_cols(0, head, width)] = (d_query * scale).astype(BF)
    dqkv_ref[:, width : 3 * width] = own_acc[...].astype(BF)
    for slot in range(heads * BACK):
        fold_ref[slot : slot + 1, :] = toeplitz_fold(dgrid_ref[slot])


VM = pl.BlockSpec(memory_space=pltpu.VMEM)


def attend_forward(chunk, rev_bias, segcol, segrow, qkv_list):
    rows, width3 = qkv_list[0].shape
    heads = width3 // (3 * HD)
    length = segrow.shape[1]
    return pl.pallas_call(
        partial(attend_fwd_kernel, chunk, rows // BLK, heads, length),
        out_shape=jax.ShapeDtypeStruct((rows, heads * HD), BF),
        in_specs=[VM] * (3 + chunk + 1),
        out_specs=VM,
        scratch_shapes=[pltpu.VMEM((heads * BACK, BLK, BLK), F32)],
        cost_estimate=pl.CostEstimate(flops=int(2e9), bytes_accessed=int(4e6), transcendentals=int(2e6)),
        name="attend_fwd",
    )(rev_bias, segcol, segrow, *qkv_list[: chunk + 1])


def attend_backward(chunk, rev_bias, segcol, segrow, d_mixed, qkv_list, acc_list):
    rows, width3 = qkv_list[0].shape
    heads = width3 // (3 * HD)
    length = segrow.shape[1]
    acc_shape = (rows, 2 * heads * HD)
    has_acc = acc_list is not None
    args = [rev_bias, segcol, segrow, d_mixed, *qkv_list[: chunk + 1]]
    if has_acc:
        args += list(acc_list)
    outs = pl.pallas_call(
        partial(attend_bwd_kernel, chunk, rows // BLK, heads, length, has_acc),
        out_shape=[
            jax.ShapeDtypeStruct((rows, width3), BF),
            jax.ShapeDtypeStruct((heads * BACK, 2 * BLK), F32),
        ]
        + [jax.ShapeDtypeStruct(acc_shape, F32)] * chunk,
        in_specs=[VM] * len(args),
        out_specs=[VM] * (2 + chunk),
        scratch_shapes=[
            pltpu.VMEM((heads * BACK, BLK, BLK), F32),
            pltpu.VMEM((heads * BACK, BLK, BLK), F32),
            pltpu.VMEM(acc_shape, F32),
        ],
        cost_estimate=pl.CostEstimate(flops=int(5e9), bytes_accessed=int(8e6), transcendentals=int(2e6)),
        name="attend_bwd",
    )(*args)
    return outs[0], outs[1], list(outs[2:])


def dispatch_kernel(experts_dev, cap, weighted, code_ref, *rest):
    if weighted:
        gate_ref, x_ref, *outs = rest
    else:
        x_ref, *outs = rest
    slots = experts_dev * cap * 2
    slot_id = lax.broadcasted_iota(jnp.int32, (slots, BLK), 0)
    first = slot_id == code_ref[0, 0:1, :]
    second = slot_id == code_ref[0, 1:2, :]
    pick = jnp.where(first | second, 1.0, 0.0).astype(BF)
    rows = fdot(pick, x_ref[...].astype(BF))
    if weighted:
        gate = jnp.sum(
            jnp.where(first, gate_ref[0, 0:1, :], 0.0) + jnp.where(second, gate_ref[0, 1:2, :], 0.0),
            axis=1,
            keepdims=True,
        )
        rows = rows * gate
    rows = rows.astype(BF)
    half = slots // 2
    for local, out in enumerate(outs):
        for dest in range(experts_dev):
            out[dest, 0] = rows[local * half + dest * cap : local * half + (dest + 1) * cap]


def dispatch(x, code_row, gate_row, experts_dev, cap):
    tokens, width = x.shape
    blocks = tokens // BLK
    if cap % 16 != 0:
        slots = jnp.arange(2 * experts_dev * cap, dtype=jnp.int32)
        match = code_row[:, :, None, :] == slots[None, None, :, None]
        if gate_row is None:
            pick = jnp.sum(match.astype(F32), axis=1)
        else:
            pick = jnp.sum(jnp.where(match, gate_row[:, :, None, :], 0.0), axis=1)
        rows = jnp.einsum("bst,btd->bsd", pick, x.reshape(blocks, BLK, width).astype(F32),
                          precision=lax.Precision.HIGHEST).astype(BF)
        rows = rows.reshape(blocks, 2, experts_dev, cap, width)
        return tuple(jnp.transpose(rows[:, loc], (1, 0, 2, 3)) for loc in range(2))
    code_spec = pl.BlockSpec((1, 2, BLK), lambda b: (b, 0, 0))
    args, specs = [code_row], [code_spec]
    if gate_row is not None:
        args.append(gate_row)
        specs.append(code_spec)
    args.append(x)
    specs.append(pl.BlockSpec((BLK, width), lambda b: (b, 0)))
    shape = (experts_dev, blocks, cap, width)
    return tuple(
        pl.pallas_call(
            partial(dispatch_kernel, experts_dev, cap, gate_row is not None),
            grid=(blocks,),
            out_shape=[jax.ShapeDtypeStruct(shape, BF)] * 2,
            in_specs=specs,
            out_specs=[pl.BlockSpec((experts_dev, 1, cap, width), lambda b: (0, b, 0, 0))] * 2,
            cost_estimate=pl.CostEstimate(
                flops=int(2 * blocks * 768 * BLK * width), bytes_accessed=int(4e6), transcendentals=0
            ),
            name="dispatch",
        )(*args)
    )


def gather_rows(ref, experts_dev, cap):
    return jnp.concatenate([ref[dest, 0] for dest in range(experts_dev)], axis=0)


def combine_kernel(experts_dev, cap, weighted, code_ref, *rest):
    if weighted:
        gate_ref, r0_ref, r1_ref, out_ref = rest
    else:
        r0_ref, r1_ref, out_ref = rest
    half = experts_dev * cap
    slot_id = lax.broadcasted_iota(jnp.int32, (BLK, 2 * half), 1)
    g0 = gate_ref[:, 0:1] if weighted else 1.0
    g1 = gate_ref[:, 1:2] if weighted else 1.0
    pick = jnp.where(slot_id == code_ref[:, 0:1], g0, 0.0) + jnp.where(
        slot_id == code_ref[:, 1:2], g1, 0.0
    )
    pick = pick.astype(BF)
    total = fdot(pick[:, :half], gather_rows(r0_ref, experts_dev, cap)) + fdot(
        pick[:, half:], gather_rows(r1_ref, experts_dev, cap)
    )
    out_ref[...] = total.astype(out_ref.dtype)


def combine(rows_pair, code_col, gates, experts_dev, cap, out_dtype):
    tokens = code_col.shape[0]
    blocks = tokens // BLK
    width = rows_pair[0].shape[-1]
    if cap % 16 != 0:
        slots = jnp.arange(2 * experts_dev * cap, dtype=jnp.int32)
        match = code_col[:, :, None] == slots
        weight = jnp.where(match, 1.0 if gates is None else gates[:, :, None], 0.0).sum(axis=1)
        rows = jnp.concatenate(
            [jnp.transpose(r, (1, 0, 2, 3)).reshape(blocks, -1, width) for r in rows_pair], axis=1
        )
        out = jnp.einsum("bts,bsd->btd", weight.reshape(blocks, BLK, -1), rows.astype(F32),
                         precision=lax.Precision.HIGHEST)
        return out.reshape(tokens, width).astype(out_dtype)
    row_spec = pl.BlockSpec((experts_dev, 1, cap, width), lambda b: (0, b, 0, 0))
    col_spec = pl.BlockSpec((BLK, 2), lambda b: (b, 0))
    args, specs = [code_col], [col_spec]
    if gates is not None:
        args.append(gates)
        specs.append(col_spec)
    return pl.pallas_call(
        partial(combine_kernel, experts_dev, cap, gates is not None),
        grid=(blocks,),
        out_shape=jax.ShapeDtypeStruct((tokens, width), out_dtype),
        in_specs=specs + [row_spec] * 2,
        out_specs=pl.BlockSpec((BLK, width), lambda b: (b, 0)),
        cost_estimate=pl.CostEstimate(
            flops=int(2 * blocks * 768 * BLK * width), bytes_accessed=int(4e6), transcendentals=0
        ),
        name="combine",
    )(*args, *rows_pair)


def gate_grad_kernel(experts_dev, cap, code_ref, g_ref, r0_ref, r1_ref, out_ref):
    half = experts_dev * cap
    upstream = g_ref[...].astype(BF)
    dots = jnp.concatenate(
        [fdot(upstream, gather_rows(r, experts_dev, cap), ((1,), (1,))) for r in (r0_ref, r1_ref)],
        axis=1,
    )
    slot_id = lax.broadcasted_iota(jnp.int32, (BLK, 2 * half), 1)
    for k in range(2):
        out_ref[:, k : k + 1] = jnp.sum(
            jnp.where(slot_id == code_ref[:, k : k + 1], dots, 0.0), axis=1, keepdims=True
        )


def gate_grad(g2, rows_pair, code_col, experts_dev, cap):
    tokens, width = g2.shape
    blocks = tokens // BLK
    if cap % 16 != 0:
        slots = jnp.arange(2 * experts_dev * cap, dtype=jnp.int32)
        match = code_col[:, :, None] == slots
        rows = jnp.concatenate(
            [jnp.transpose(r, (1, 0, 2, 3)).reshape(blocks, -1, width) for r in rows_pair], axis=1
        )
        dots = jnp.einsum("btd,bsd->bts", g2.reshape(blocks, BLK, width), rows.astype(F32),
                          precision=lax.Precision.HIGHEST)
        return jnp.sum(jnp.where(match, dots.reshape(tokens, 1, -1), 0.0), axis=2)
    row_spec = pl.BlockSpec((experts_dev, 1, cap, width), lambda b: (0, b, 0, 0))
    col_spec = pl.BlockSpec((BLK, 2), lambda b: (b, 0))
    return pl.pallas_call(
        partial(gate_grad_kernel, experts_dev, cap),
        grid=(blocks,),
        out_shape=jax.ShapeDtypeStruct((tokens, 2), F32),
        in_specs=[col_spec, pl.BlockSpec((BLK, width), lambda b: (b, 0)), row_spec, row_spec],
        out_specs=col_spec,
        cost_estimate=pl.CostEstimate(
            flops=int(2 * blocks * 768 * BLK * width), bytes_accessed=int(4e6), transcendentals=0
        ),
        name="gate_grad",
    )(code_col, g2, *rows_pair)


def dispatch_parts_kernel(devices, cap, weighted, code_ref, *rest):
    if weighted:
        gate_ref, x_ref, *outs = rest
    else:
        x_ref, *outs = rest
    slots = devices * cap * 2
    slot_id = lax.broadcasted_iota(jnp.int32, (slots, BLK), 0)
    first = slot_id == code_ref[0, 0:1, :]
    second = slot_id == code_ref[0, 1:2, :]
    pick = jnp.where(first | second, 1.0, 0.0).astype(BF)
    rows = fdot(pick, x_ref[...].astype(BF))
    if weighted:
        gate = jnp.sum(
            jnp.where(first, gate_ref[0, 0:1, :], 0.0) + jnp.where(second, gate_ref[0, 1:2, :], 0.0),
            axis=1,
            keepdims=True,
        )
        rows = rows * gate
    rows = rows.astype(BF)
    for part, out in enumerate(outs):
        for local in range(2):
            at = (local * devices + part) * cap
            out[local] = rows[at : at + cap]


def dispatch_parts(x, code_row, gate_row, devices, cap):
    tokens, width = x.shape
    blocks = tokens // BLK
    code_spec = pl.BlockSpec((1, 2, BLK), lambda b: (b, 0, 0))
    args, specs = [code_row], [code_spec]
    if gate_row is not None:
        args.append(gate_row)
        specs.append(code_spec)
    args.append(x)
    specs.append(pl.BlockSpec((BLK, width), lambda b: (b, 0)))
    return pl.pallas_call(
        partial(dispatch_parts_kernel, devices, cap, gate_row is not None),
        grid=(blocks,),
        out_shape=[jax.ShapeDtypeStruct((2, blocks * cap, width), BF)] * devices,
        in_specs=specs,
        out_specs=[pl.BlockSpec((2, cap, width), lambda b: (0, b, 0))] * devices,
        cost_estimate=pl.CostEstimate(
            flops=int(2 * blocks * 768 * BLK * width), bytes_accessed=int(4e6), transcendentals=0
        ),
        name="dispatch",
    )(*args)


def slot_rows(refs):
    return jnp.concatenate([ref[local] for local in range(2) for ref in refs], axis=0)


def combine_parts_kernel(devices, cap, weighted, code_ref, *rest):
    if weighted:
        gate_ref, *rest = rest
    parts, out_ref = rest[:devices], rest[devices]
    slot_id = lax.broadcasted_iota(jnp.int32, (BLK, 2 * devices * cap), 1)
    g0 = gate_ref[:, 0:1] if weighted else 1.0
    g1 = gate_ref[:, 1:2] if weighted else 1.0
    pick = jnp.where(slot_id == code_ref[:, 0:1], g0, 0.0) + jnp.where(
        slot_id == code_ref[:, 1:2], g1, 0.0
    )
    out_ref[...] = fdot(pick.astype(BF), slot_rows(parts)).astype(out_ref.dtype)


def combine_parts(parts, code_col, gates, devices, cap, out_dtype):
    tokens = code_col.shape[0]
    width = parts[0].shape[-1]
    blocks = tokens // BLK
    row_spec = pl.BlockSpec((2, cap, width), lambda b: (0, b, 0))
    col_spec = pl.BlockSpec((BLK, 2), lambda b: (b, 0))
    args, specs = [code_col], [col_spec]
    if gates is not None:
        args.append(gates)
        specs.append(col_spec)
    return pl.pallas_call(
        partial(combine_parts_kernel, devices, cap, gates is not None),
        grid=(blocks,),
        out_shape=jax.ShapeDtypeStruct((tokens, width), out_dtype),
        in_specs=specs + [row_spec] * devices,
        out_specs=pl.BlockSpec((BLK, width), lambda b: (b, 0)),
        cost_estimate=pl.CostEstimate(
            flops=int(2 * blocks * 768 * BLK * width), bytes_accessed=int(4e6), transcendentals=0
        ),
        name="combine",
    )(*args, *parts)


def gate_grad_parts_kernel(devices, cap, code_ref, route_ref, gate_ref, g_ref, *rest):
    parts, out_ref = rest[:devices], rest[devices]
    dots = fdot(g_ref[...].astype(BF), slot_rows(parts), ((1,), (1,)))
    slot_id = lax.broadcasted_iota(jnp.int32, (BLK, 2 * devices * cap), 1)
    d_gates = [
        jnp.sum(jnp.where(slot_id == code_ref[:, k : k + 1], dots, 0.0), axis=1, keepdims=True)
        for k in range(2)
    ]
    gates = [gate_ref[:, k : k + 1] for k in range(2)]
    centre = gates[0] * d_gates[0] + gates[1] * d_gates[1]
    expert_id = lax.broadcasted_iota(jnp.int32, out_ref.shape, 1)
    total = jnp.zeros(out_ref.shape, F32)
    for k in range(2):
        d_chosen = gates[k] * (d_gates[k] - centre)
        total = total + jnp.where(expert_id == route_ref[:, k : k + 1], d_chosen, 0.0)
    out_ref[...] = total


def logit_grad_parts(g2, parts, code_col, routes, gates, experts, devices, cap):
    tokens, width = g2.shape
    blocks = tokens // BLK
    row_spec = pl.BlockSpec((2, cap, width), lambda b: (0, b, 0))
    col_spec = pl.BlockSpec((BLK, 2), lambda b: (b, 0))
    return pl.pallas_call(
        partial(gate_grad_parts_kernel, devices, cap),
        grid=(blocks,),
        out_shape=jax.ShapeDtypeStruct((tokens, experts), F32),
        in_specs=[col_spec] * 3 + [pl.BlockSpec((BLK, width), lambda b: (b, 0))]
        + [row_spec] * devices,
        out_specs=pl.BlockSpec((BLK, experts), lambda b: (b, 0)),
        cost_estimate=pl.CostEstimate(
            flops=int(2 * blocks * 768 * BLK * width), bytes_accessed=int(4e6), transcendentals=0
        ),
        name="logit_grad",
    )(code_col, routes, gates, g2, *parts)


def return_grad_kernel(devices, cap, code_ref, dlog_ref, router_ref, *rest):
    parts, out_ref = rest[:devices], rest[devices]
    slot_id = lax.broadcasted_iota(jnp.int32, (BLK, 2 * devices * cap), 1)
    chosen = (slot_id == code_ref[:, 0:1]) | (slot_id == code_ref[:, 1:2])
    total = fdot(jnp.where(chosen, 1.0, 0.0).astype(BF), slot_rows(parts))
    router_term = lax.dot_general(
        dlog_ref[...],
        router_ref[...].astype(F32),
        (((1,), (1,)), ((), ())),
        precision=lax.Precision.HIGHEST,
        preferred_element_type=F32,
    )
    out_ref[...] = (total + router_term).astype(out_ref.dtype)


def return_grad(parts, code_col, d_logits, router, devices, cap):
    tokens = code_col.shape[0]
    width = parts[0].shape[-1]
    experts = router.shape[1]
    blocks = tokens // BLK
    return pl.pallas_call(
        partial(return_grad_kernel, devices, cap),
        grid=(blocks,),
        out_shape=jax.ShapeDtypeStruct((tokens, width), BF),
        in_specs=[
            pl.BlockSpec((BLK, 2), lambda b: (b, 0)),
            pl.BlockSpec((BLK, experts), lambda b: (b, 0)),
            pl.BlockSpec((width, experts), lambda b: (0, 0)),
        ]
        + [pl.BlockSpec((2, cap, width), lambda b: (0, b, 0))] * devices,
        out_specs=pl.BlockSpec((BLK, width), lambda b: (b, 0)),
        cost_estimate=pl.CostEstimate(
            flops=int(2 * blocks * 768 * BLK * width), bytes_accessed=int(4e6), transcendentals=0
        ),
        name="return_grad",
    )(code_col, d_logits, router, *parts)


def mix_kernel(zs, z_ref, route_ref, stream_ref, gain_ref, router_ref, w_ref, *rest):
    mixed = rest[:zs]
    mid_ref, normed_ref, gate_ref = rest[zs:]
    z_id = z_ref[0]
    hw = mixed[0].shape[1]
    mid = stream_ref[...]
    for step in range(zs):
        rows = pl.ds(pl.multiple_of((z_id ^ step) * hw, 64), hw)
        mid = mid + fdot(mixed[step][...], w_ref[rows, :])
    mid_ref[...] = mid
    inverse = lax.rsqrt(jnp.mean(mid * mid, axis=1, keepdims=True) + NORM_EPS)
    normed = (mid * inverse * gain_ref[...]).astype(BF)
    normed_ref[...] = normed
    logits = fdot(normed, router_ref[...])
    expert_id = lax.broadcasted_iota(jnp.int32, logits.shape, 1)
    first, second = [
        jnp.sum(jnp.where(expert_id == route_ref[:, k : k + 1], logits, 0.0), axis=1, keepdims=True)
        for k in range(2)
    ]
    top = jnp.maximum(first, second)
    first, second = jnp.exp(first - top), jnp.exp(second - top)
    total = first + second
    gate_ref[:, 0:1] = first / total
    gate_ref[:, 1:2] = second / total


def mix_forward(z_id, routes, stream, gain, router, w_out, mixed_list):
    tokens, width = stream.shape
    zs = len(mixed_list)
    hw = mixed_list[0].shape[1]
    experts = router.shape[1]
    row = lambda cols: pl.BlockSpec((BLK, cols), lambda b: (b, 0))
    full = lambda shape: pl.BlockSpec(shape, lambda b: (0, 0))
    return pl.pallas_call(
        partial(mix_kernel, zs),
        grid=(tokens // BLK,),
        out_shape=[
            jax.ShapeDtypeStruct((tokens, width), F32),
            jax.ShapeDtypeStruct((tokens, width), BF),
            jax.ShapeDtypeStruct((tokens, 2), F32),
        ],
        in_specs=[
            pl.BlockSpec(memory_space=pltpu.SMEM),
            row(2),
            row(width),
            full((1, width)),
            full((width, experts)),
            full((width, width)),
        ]
        + [row(hw)] * zs,
        out_specs=[row(width), row(width), row(2)],
        cost_estimate=pl.CostEstimate(
            flops=int(2 * tokens * width * width), bytes_accessed=int(6e6), transcendentals=0
        ),
        name="mix_fwd",
    )(z_id.reshape(1), routes, stream, gain.reshape(1, -1), router, w_out, *mixed_list)


def mix_bwd_kernel(z_ref, g_ref, mid_ref, dn_ref, gain_ref, w_ref, dmid_ref, dproj_ref, dmix_ref, gain_out):
    hw = dmix_ref.shape[1]
    mid = mid_ref[...]
    upstream = dn_ref[...].astype(F32)
    inverse = lax.rsqrt(jnp.mean(mid * mid, axis=1, keepdims=True) + NORM_EPS)
    scaled = upstream * gain_ref[...]
    inner_mean = jnp.mean(scaled * mid, axis=1, keepdims=True)
    d_mid = g_ref[...] + inverse * scaled - mid * (inverse * inverse * inverse) * inner_mean
    dmid_ref[...] = d_mid
    d_proj = d_mid.astype(BF)
    dproj_ref[...] = d_proj
    rows = pl.ds(pl.multiple_of(z_ref[0] * hw, 64), hw)
    dmix_ref[...] = fdot(d_proj, w_ref[rows, :], ((1,), (1,))).astype(BF)
    part = jnp.sum(upstream * mid * inverse, axis=0, keepdims=True)

    @pl.when(pl.program_id(0) == 0)
    def _():
        gain_out[...] = jnp.zeros_like(gain_out)

    gain_out[...] += part


def mix_backward(z_id, g2, mid, d_normed, gain, w_out, hw):
    tokens, width = mid.shape
    row = lambda cols: pl.BlockSpec((BLK, cols), lambda b: (b, 0))
    full = lambda shape: pl.BlockSpec(shape, lambda b: (0, 0))
    return pl.pallas_call(
        mix_bwd_kernel,
        grid=(tokens // BLK,),
        out_shape=[
            jax.ShapeDtypeStruct((tokens, width), F32),
            jax.ShapeDtypeStruct((tokens, width), BF),
            jax.ShapeDtypeStruct((tokens, hw), BF),
            jax.ShapeDtypeStruct((1, width), F32),
        ],
        in_specs=[
            pl.BlockSpec(memory_space=pltpu.SMEM),
            row(width),
            row(width),
            row(width),
            full((1, width)),
            full((width, width)),
        ],
        out_specs=[row(width), row(width), row(hw), full((1, width))],
        cost_estimate=pl.CostEstimate(
            flops=int(2 * tokens * width * hw), bytes_accessed=int(8e6), transcendentals=0
        ),
        name="mix_bwd",
    )(z_id.reshape(1), g2, mid, d_normed, gain.reshape(1, -1), w_out)


GELU_A = 0.7978845608028654
GELU_B = 0.044715


def expert_fwd_kernel(devices, *refs):
    parts, (first_ref, second_ref) = refs[:devices], refs[devices : devices + 2]
    rows_ref, inner_ref, hidden_ref, *outs = refs[devices + 2 :]
    rows = jnp.concatenate([part[0] for part in parts], axis=0)
    rows_ref[0] = rows
    inner = fdot(rows, first_ref[0, 0])
    inner_ref[0] = inner.astype(inner_ref.dtype)
    wave = jnp.tanh(GELU_A * (inner + GELU_B * (inner * inner * inner)))
    hidden = (0.5 * inner * (1.0 + wave)).astype(BF)
    hidden_ref[0] = hidden
    result = fdot(hidden, second_ref[0, 0]).astype(BF)
    size = parts[0].shape[1]
    for part, out in enumerate(outs):
        out[0] = result[part * size : (part + 1) * size]


def expert_forward(parts, first, second, layer):
    devices = len(parts)
    _, size, width = parts[0].shape
    hid = first.shape[3]
    part_spec = pl.BlockSpec((1, size, width), lambda l: (l, 0, 0))
    outs = pl.pallas_call(
        partial(expert_fwd_kernel, devices),
        grid=(2,),
        out_shape=[
            jax.ShapeDtypeStruct((2, devices * size, width), BF),
            jax.ShapeDtypeStruct((2, devices * size, hid), F32),
            jax.ShapeDtypeStruct((2, devices * size, hid), BF),
        ]
        + [jax.ShapeDtypeStruct((2, size, width), BF)] * devices,
        in_specs=[part_spec] * devices
        + [
            pl.BlockSpec((1, 1, width, hid), lambda l: (layer, l, 0, 0)),
            pl.BlockSpec((1, 1, hid, width), lambda l: (layer, l, 0, 0)),
        ],
        out_specs=[
            pl.BlockSpec((1, devices * size, width), lambda l: (l, 0, 0)),
            pl.BlockSpec((1, devices * size, hid), lambda l: (l, 0, 0)),
            pl.BlockSpec((1, devices * size, hid), lambda l: (l, 0, 0)),
        ]
        + [part_spec] * devices,
        cost_estimate=pl.CostEstimate(
            flops=int(8 * devices * size * width * hid), bytes_accessed=int(20e6), transcendentals=0
        ),
        name="expert_fwd",
    )(*parts, first, second)
    return outs[0], outs[1], outs[2], list(outs[3:])


def expert_bwd_kernel(devices, *refs):
    parts = refs[:devices]
    inner_ref, first_ref, second_ref = refs[devices : devices + 3]
    rows_ref, dinner_ref, *outs = refs[devices + 3 :]
    rows = jnp.concatenate([part[0] for part in parts], axis=0)
    rows_ref[0] = rows
    d_hidden = fdot(rows, second_ref[0, 0], ((1,), (1,)))
    inner = inner_ref[0]
    square = inner * inner
    wave = jnp.tanh(GELU_A * inner * (1.0 + GELU_B * square))
    slope = 0.5 * (1.0 + wave) + (0.5 * GELU_A) * inner * (1.0 - wave * wave) * (
        1.0 + (3.0 * GELU_B) * square
    )
    d_inner = (d_hidden * slope).astype(BF)
    dinner_ref[0] = d_inner
    d_rows = fdot(d_inner, first_ref[0, 0], ((1,), (1,))).astype(BF)
    size = parts[0].shape[1]
    for part, out in enumerate(outs):
        out[0] = d_rows[part * size : (part + 1) * size]


def expert_backward(parts, inner, first, second, layer):
    devices = len(parts)
    _, size, width = parts[0].shape
    hid = first.shape[3]
    part_spec = pl.BlockSpec((1, size, width), lambda l: (l, 0, 0))
    outs = pl.pallas_call(
        partial(expert_bwd_kernel, devices),
        grid=(2,),
        out_shape=[
            jax.ShapeDtypeStruct((2, devices * size, width), BF),
            jax.ShapeDtypeStruct((2, devices * size, hid), BF),
        ]
        + [jax.ShapeDtypeStruct((2, size, width), BF)] * devices,
        in_specs=[part_spec] * devices
        + [
            pl.BlockSpec((1, devices * size, hid), lambda l: (l, 0, 0)),
            pl.BlockSpec((1, 1, width, hid), lambda l: (layer, l, 0, 0)),
            pl.BlockSpec((1, 1, hid, width), lambda l: (layer, l, 0, 0)),
        ],
        out_specs=[
            pl.BlockSpec((1, devices * size, width), lambda l: (l, 0, 0)),
            pl.BlockSpec((1, devices * size, hid), lambda l: (l, 0, 0)),
        ]
        + [part_spec] * devices,
        cost_estimate=pl.CostEstimate(
            flops=int(8 * devices * size * width * hid), bytes_accessed=int(20e6), transcendentals=0
        ),
        name="expert_bwd",
    )(*parts, inner, first, second)
    return outs[0], outs[1], list(outs[2:])


def expert_grad_kernel(chunks, aliased, *refs):
    groups = [refs[4 * c : 4 * c + 4] for c in range(chunks)]
    first_out, second_out = refs[-2:]

    first = second = None
    for rows, d_inner, hidden, d_res in groups:
        one = fdot(rows[0], d_inner[0], ((0,), (0,)))
        two = fdot(hidden[0], d_res[0], ((0,), (0,)))
        first = one if first is None else first + one
        second = two if second is None else second + two
    first_out[0, 0] = first
    second_out[0, 0] = second


def expert_grads(groups, layer, layers, previous):
    _, size, width = groups[0][0].shape
    hid = groups[0][1].shape[2]
    row_spec = pl.BlockSpec((1, size, width), lambda l: (l, 0, 0))
    hid_spec = pl.BlockSpec((1, size, hid), lambda l: (l, 0, 0))
    args, specs = [], []
    for group in groups:
        args += list(group)
        specs += [row_spec, hid_spec, hid_spec, row_spec]
    aliases = {}
    if previous is not None:
        aliases = {len(args): 0, len(args) + 1: 1}
        args += list(previous)
        specs += [pl.BlockSpec(memory_space=pl.ANY)] * 2
    return pl.pallas_call(
        partial(expert_grad_kernel, len(groups), previous is not None),
        grid=(2,),
        out_shape=[
            jax.ShapeDtypeStruct((layers, 2, width, hid), F32),
            jax.ShapeDtypeStruct((layers, 2, hid, width), F32),
        ],
        in_specs=specs,
        out_specs=[
            pl.BlockSpec((1, 1, width, hid), lambda l: (layer, l, 0, 0)),
            pl.BlockSpec((1, 1, hid, width), lambda l: (layer, l, 0, 0)),
        ],
        input_output_aliases=aliases,
        cost_estimate=pl.CostEstimate(
            flops=int(8 * len(groups) * size * width * hid),
            bytes_accessed=int(30e6),
            transcendentals=0,
        ),
        name="expert_grad",
    )(*args)


def spread(x, axis_name):
    return lax.all_to_all(x, axis_name, split_axis=0, concat_axis=0, tiled=True)


def swap(x, axis_name, step):
    size = lax.axis_size(axis_name)
    return lax.ppermute(x, axis_name, [(i, i ^ step) for i in range(size)])


def swap_parts(parts, axis_name):
    return [part if step == 0 else swap(part, axis_name, step) for step, part in enumerate(parts)]


def spread_gather(x, axis_name):
    size = lax.axis_size(axis_name)
    return spread(jnp.broadcast_to(x[None], (size,) + x.shape), axis_name)


def reduce_rows(x):
    zs, z_id = lax.axis_size("seq"), lax.axis_index("seq")
    pieces = x.reshape(zs, -1, x.shape[1])
    total = lax.dynamic_index_in_dim(pieces, z_id, 0, keepdims=False).astype(F32)
    for step in range(1, zs):
        piece = lax.dynamic_index_in_dim(pieces, z_id ^ step, 0, keepdims=False)
        total = total + swap(piece, "seq", step).astype(F32)
    return total


def sum_rows(x):
    zs, z_id = lax.axis_size("seq"), lax.axis_index("seq")
    steps = [1 << bit for bit in range(zs.bit_length() - 1)]
    total = x
    for step in steps:
        half = total.shape[0] // 2
        upper = (z_id & step) != 0
        low, high = total[:half], total[half:]
        got = swap(jnp.where(upper, low, high), "seq", step)
        total = (jnp.where(upper, high, low).astype(F32) + got.astype(F32)).astype(BF)
    for step in reversed(steps):
        upper = (z_id & step) != 0
        got = swap(total, "seq", step)
        total = jnp.concatenate(
            [jnp.where(upper, got, total), jnp.where(upper, total, got)], axis=0
        )
    return total


def split_dense_kernel(zs, es, rows, in_ref, out_ref, in_send, out_send):
    for dest in range(es):
        pieces = [
            in_ref[(plane * es + dest) * rows : (plane * es + dest + 1) * rows] for plane in range(zs)
        ]
        in_send[dest] = jnp.concatenate(pieces, axis=0).astype(BF)
        out_send[dest] = out_ref[dest * rows : (dest + 1) * rows].astype(BF)


def split_dense(total_in, total_out, zs, es, rows):
    wide, width = total_in.shape[1], total_out.shape[1]
    if rows % 8 != 0:
        in_send = jnp.transpose(total_in.reshape(zs, es, rows, wide), (1, 0, 2, 3))
        return (
            in_send.reshape(es, zs * rows, wide).astype(BF),
            total_out.reshape(es, rows, width).astype(BF),
        )
    return pl.pallas_call(
        partial(split_dense_kernel, zs, es, rows),
        out_shape=[
            jax.ShapeDtypeStruct((es, zs * rows, wide), BF),
            jax.ShapeDtypeStruct((es, rows, width), BF),
        ],
        in_specs=[VM] * 2,
        out_specs=[VM] * 2,
        cost_estimate=pl.CostEstimate(flops=int(1e6), bytes_accessed=int(4e6), transcendentals=0),
        name="split_dense",
    )(total_in, total_out)


def norm_forward(stream, gain):
    inverse = lax.rsqrt(jnp.mean(stream * stream, axis=-1, keepdims=True) + NORM_EPS)
    return (stream * inverse * gain).astype(BF), inverse


def norm_backward(stream, inverse, gain, upstream):
    scaled = upstream * gain
    inner_mean = jnp.mean(scaled * stream, axis=-1, keepdims=True)
    d_stream = inverse * scaled - stream * (inverse * inverse * inverse) * inner_mean
    return d_stream, jnp.sum(upstream * stream * inverse, axis=0)


def slot_codes(routes, experts, experts_dev, cap, flip):
    blocks = routes.shape[0] // BLK
    flat = routes.reshape(blocks, BLK * 2)
    onehot = (flat[:, :, None] == jnp.arange(experts, dtype=jnp.int32)).astype(F32)
    steps = jnp.arange(BLK * 2, dtype=jnp.int32)
    before = (steps[:, None] > steps[None, :]).astype(F32)
    count = jnp.einsum("ij,bje->bie", before, onehot, preferred_element_type=F32)
    place = jnp.sum(count * onehot, axis=2).astype(jnp.int32)
    code = (flat % 2) * (experts_dev * cap) + ((flat // 2) ^ flip) * cap + place
    return code.reshape(blocks * BLK, 2)


def body(
    tokens,
    cotangent,
    segments,
    buckets,
    routes,
    attend_in,
    attend_out,
    router_weight,
    gain_attend,
    gain_expert,
    bias_table,
    expert_in,
    expert_out,
):
    zs = lax.axis_size("seq")
    es = lax.axis_size("expert")
    z_id = lax.axis_index("seq")
    own_rows, width = tokens.shape[1:]
    length = segments.shape[1]
    layers, shard_rows = attend_in.shape[:2]
    experts = router_weight.shape[2]
    cap = 3 * own_rows // experts
    heads_all = width // HD
    heads = heads_all // zs
    hw = heads * HD
    bucket_count = bias_table.shape[1] * zs * es // heads_all
    chunks = CHUNKS
    rows_c = length // chunks

    def split(x):
        return [x[c * rows_c : (c + 1) * rows_c] for c in range(chunks)]

    route_rows = routes[0].astype(BF).reshape(-1, width) if (own_rows * 2) % width == 0 else None
    if route_rows is None:
        flat_routes = routes[0].astype(BF).reshape(-1)
        pad = -flat_routes.shape[0] % (16 * width)
        route_rows = jnp.pad(flat_routes, (0, pad)).reshape(-1, width)
    packed = lax.all_gather(jnp.concatenate([tokens[0], route_rows], axis=0), "seq", axis=0)
    stream_full = packed[:, :own_rows].reshape(length, width)
    routes_full = (
        packed[:, own_rows:].reshape(zs, -1)[:, : own_rows * 2].reshape(length, 2).astype(jnp.int32)
    )

    small = jnp.concatenate(
        [
            gain_attend.reshape(-1),
            gain_expert.reshape(-1),
            bias_table.reshape(-1),
            router_weight.reshape(-1),
        ]
    )
    small = spread_gather(spread_gather(small, "expert"), "seq").reshape(zs * es, -1)
    sizes = [layers * shard_rows, layers * shard_rows, layers * bias_table.shape[1]]
    at = 0
    parts = []
    for size in sizes:
        parts.append(small[:, at : at + size])
        at += size
    gains_a = jnp.transpose(parts[0].reshape(-1, layers, shard_rows), (1, 0, 2)).reshape(layers, width)
    gains_e = jnp.transpose(parts[1].reshape(-1, layers, shard_rows), (1, 0, 2)).reshape(layers, width)
    bias_all = jnp.transpose(
        parts[2].reshape(-1, layers, bias_table.shape[1]), (1, 0, 2)
    ).reshape(layers, heads_all, bucket_count)
    routers = jnp.transpose(
        small[:, at:].reshape(-1, layers, shard_rows, experts), (1, 0, 2, 3)
    ).reshape(layers, width, experts)
    gains_a = gains_a.astype(F32)
    gains_e = gains_e.astype(F32)

    piece = attend_in.reshape(layers, shard_rows, 3, zs, hw)
    piece = jnp.transpose(piece, (3, 0, 1, 2, 4)).reshape(zs, layers, shard_rows, 3 * hw)
    piece = spread(piece, "seq")
    piece = lax.all_gather(piece, "expert", axis=0)
    piece = jnp.transpose(piece, (2, 1, 0, 3, 4)).reshape(layers, width, 3 * hw)
    w_in_list = [piece[layer] for layer in range(layers)]
    w_out_list = [
        lax.all_gather(attend_out[layer], ("seq", "expert"), axis=0, tiled=True)
        for layer in range(layers)
    ]

    steps = length - jnp.arange(length + BLK, dtype=jnp.int32)
    rev_buckets = jnp.concatenate(
        [buckets[length - 1 :], buckets[::-1], jnp.broadcast_to(buckets[:1], (BLK - 1,))]
    )
    rev_hot = (rev_buckets[:, None] == jnp.arange(bucket_count, dtype=jnp.int32)).astype(F32)
    segrow = segments
    segcol = segments.reshape(length, 1)

    fast = cap % 16 == 0
    flip = lax.axis_index("expert") if fast else 0
    code_full = slot_codes(routes_full, experts, es, cap, flip)
    code_col = split(code_full)
    code_row_full = jnp.transpose(code_full.reshape(-1, BLK, 2), (0, 2, 1))
    blocks_c = rows_c // BLK
    code_row = [code_row_full[c * blocks_c : (c + 1) * blocks_c] for c in range(chunks)]
    route_hot = split(routes_full[..., None] == jnp.arange(experts, dtype=jnp.int32))
    routes_c = split(routes_full)
    expert_outs = None

    def exchange(pair):
        return [
            spread(r.reshape(es, -1, width), "expert").reshape(-1, width) for r in pair
        ]

    def exchange_back(pair):
        return [
            spread(r.reshape(es, -1, width), "expert").reshape(es, blocks_c, cap, width) for r in pair
        ]

    stream = split(stream_full.astype(F32))
    saved = []
    block_out = None
    for layer in range(layers):
        w_in, w_out = w_in_list[layer], w_out_list[layer]
        local_bias = lax.dynamic_slice_in_dim(bias_all[layer], z_id * heads, heads, 0)
        rev_bias = fdot(local_bias, rev_hot.astype(BF), ((1,), (1,)))
        keep = dict(stream=stream, rev_bias=rev_bias, chunks=[])
        qkv = []
        mids, partials = [], []
        for c in range(chunks):
            normed, inv_a = norm_forward(stream[c], gains_a[layer])
            qkv.append(fdot(normed, w_in).astype(BF))
            mixed = attend_forward(c, rev_bias, segcol, segrow, qkv)
            if layer == 0 and c == 0:
                held = lax.optimization_barrier((cotangent, mixed[:8, :128]))[0]
                upstream_full = lax.all_gather(held[0], "seq", axis=0, tiled=True)
            mixed_list = [mixed] + [swap(mixed, "seq", step) for step in range(1, zs)]
            mid, normed_mid, gates = mix_forward(
                z_id, routes_c[c], stream[c], gains_e[layer], routers[layer], w_out, mixed_list
            )
            if fast:
                got = swap_parts(dispatch_parts(normed_mid, code_row[c], None, es, cap), "expert")
                rows, inner, hidden, result = expert_forward(got, expert_in, expert_out, layer)
                back = swap_parts(result, "expert")
                partials.append(combine_parts(back, code_col[c], gates, es, cap, BF))
            else:
                rows = exchange(dispatch(normed_mid, code_row[c], None, es, cap))
                inner, hidden, result = [], [], []
                for loc in range(2):
                    pre = fdot(rows[loc], expert_in[layer, loc])
                    hid = jax.nn.gelu(pre).astype(BF)
                    inner.append(pre)
                    hidden.append(hid)
                    result.append(fdot(hid, expert_out[layer, loc]).astype(BF))
                back = exchange_back(result)
                partials.append(combine(back, code_col[c], gates, es, cap, BF))
            mids.append(mid)
            keep["chunks"].append(
                dict(normed=normed, inv_a=inv_a, mixed=mixed, mid=mid, normed_mid=normed_mid,
                     gates=gates, rows=rows, inner=inner, hidden=hidden, back=back)
            )
        keep["qkv"] = qkv
        saved.append(keep)
        if layer + 1 < layers:
            stream = [mids[c] + sum_rows(partials[c]).astype(F32) for c in range(chunks)]
        else:
            delta = reduce_rows(jnp.concatenate(partials, axis=0))
            mid_own = lax.dynamic_slice_in_dim(
                jnp.concatenate(mids, axis=0), z_id * own_rows, own_rows, 0
            )
            block_out = (mid_own + delta.astype(F32)).astype(BF)

    upstream = split(upstream_full.astype(F32))
    in_grads, out_grads = [None] * layers, [None] * layers
    first_grads, second_grads = [None] * layers, [None] * layers
    small_grads = [None] * layers
    tokens_grad = None
    for layer in reversed(range(layers)):
        keep = saved[layer]
        w_in, w_out = w_in_list[layer], w_out_list[layer]
        d_mids, d_parts = [None] * chunks, [None] * chunks
        total_in = total_out = total_router = total_ga = total_ge = total_fold = None
        g_first = [None, None]
        g_second = [None, None]
        acc = None
        grad_groups = []

        def plus(left, right):
            return right if left is None else left + right

        for c in reversed(range(chunks)):
            k = keep["chunks"][c]
            g2 = upstream[c]
            gates = k["gates"]
            gate_row = jnp.transpose(gates.reshape(blocks_c, BLK, 2), (0, 2, 1))
            if fast:
                got = swap_parts(dispatch_parts(g2, code_row[c], gate_row, es, cap), "expert")
                d_res, d_inner, d_rows = expert_backward(
                    got, k["inner"], expert_in, expert_out, layer
                )
                d_back = swap_parts(d_rows, "expert")
                grad_groups.append((k["rows"], d_inner, k["hidden"], d_res))
                d_logits = logit_grad_parts(
                    g2, k["back"], code_col[c], routes_c[c], gates, experts, es, cap
                )
                partial_d = return_grad(d_back, code_col[c], d_logits, routers[layer], es, cap)
            else:
                d_res = exchange(dispatch(g2, code_row[c], gate_row, es, cap))
                d_rows = []
                for loc in range(2):
                    d_hid = fdot(d_res[loc], expert_out[layer, loc], ((1,), (1,)))
                    _, pull = jax.vjp(jax.nn.gelu, k["inner"][loc])
                    d_inner = pull(d_hid)[0].astype(BF)
                    d_rows.append(fdot(d_inner, expert_in[layer, loc], ((1,), (1,))).astype(BF))
                    g_second[loc] = plus(
                        g_second[loc], fdot(k["hidden"][loc], d_res[loc], ((0,), (0,)))
                    )
                    g_first[loc] = plus(g_first[loc], fdot(k["rows"][loc], d_inner, ((0,), (0,))))
                d_back = exchange_back(d_rows)
                d_gates = gate_grad(g2, k["back"], code_col[c], es, cap)
                d_moved = combine(d_back, code_col[c], None, es, cap, F32)
                d_chosen = gates * (d_gates - jnp.sum(gates * d_gates, axis=-1, keepdims=True))
                d_logits = jnp.sum(jnp.where(route_hot[c], d_chosen[..., None], 0.0), axis=1)
                partial_d = d_moved + exact_dot(d_logits, routers[layer].astype(F32).T)
            total_router = plus(
                total_router, exact_dot(k["normed_mid"].astype(F32).T, d_logits)
            )
            d_normed_mid = sum_rows(partial_d.astype(BF))
            d_mid, d_proj, d_mixed, ge = mix_backward(
                z_id, g2, k["mid"], d_normed_mid, gains_e[layer], w_out, hw
            )
            total_ge = plus(total_ge, ge)
            total_out = plus(total_out, fdot(k["mixed"], d_proj, ((0,), (0,))))
            d_qkv, fold, acc = attend_backward(
                c, keep["rev_bias"], segcol, segrow, d_mixed, keep["qkv"], acc
            )
            total_fold = plus(total_fold, fold)
            total_in = plus(total_in, fdot(k["normed"], d_qkv, ((0,), (0,))))
            d_part = fdot(d_qkv, w_in, ((1,), (1,)))
            d_parts[c] = d_part.astype(BF)
            if layer == 0:
                total_ga = plus(
                    total_ga, jnp.sum(d_part * keep["stream"][c] * k["inv_a"], axis=0)
                )
            d_mids[c] = d_mid
            if layer > 0:
                d_normed = sum_rows(d_parts[c]).astype(F32)
                d_in, ga = norm_backward(keep["stream"][c], k["inv_a"], gains_a[layer], d_normed)
                total_ga = plus(total_ga, ga)
                upstream[c] = d_in + d_mid
        own = (jnp.arange(zs) == z_id).astype(F32)[:, None]
        if layer == 0:
            d_normed = reduce_rows(jnp.concatenate(d_parts, axis=0))

            def mine(items):
                return lax.dynamic_slice_in_dim(
                    jnp.concatenate(items, axis=0), z_id * own_rows, own_rows, 0
                )

            stream_own = mine(keep["stream"])
            inv_own = mine([keep["chunks"][c]["inv_a"] for c in range(chunks)])
            d_in, _ = norm_backward(stream_own, inv_own, gains_a[layer], d_normed)
            tokens_grad = (d_in + mine(d_mids)).astype(BF)
            gain_a_part = total_ga.reshape(zs, -1)
        else:
            gain_a_part = total_ga.reshape(zs, -1) * own
        gain_e_part = total_ge.reshape(zs, -1) * own
        fold = total_fold.reshape(heads, BACK, 2 * BLK)
        hot = jnp.stack(
            [
                jnp.concatenate(
                    [
                        rev_hot[length - BLK * back : length - BLK * (back - 1)],
                        rev_hot[length - BLK * (back + 1) : length - BLK * back],
                    ],
                    axis=0,
                )
                for back in range(BACK)
            ]
        )
        table = exact_dot(fold.reshape(heads, -1), hot.reshape(-1, bucket_count))
        table_part = table.reshape(1, -1) * own
        router_part = total_router.reshape(zs, es, shard_rows * experts)
        small_grads[layer] = jnp.concatenate(
            [
                router_part,
                gain_a_part.reshape(zs, es, -1),
                gain_e_part.reshape(zs, es, -1),
                table_part.reshape(zs, es, -1),
            ],
            axis=-1,
        )
        in_send, out_send = split_dense(total_in, total_out, zs, es, shard_rows)
        piece = jnp.sum(spread(in_send, "expert").astype(F32), axis=0)
        out_grads[layer] = jnp.sum(spread(out_send, "expert").astype(F32), axis=0)
        piece = spread(piece.reshape(zs, shard_rows, 3 * hw).astype(BF), "seq").astype(F32)
        piece = jnp.transpose(piece.reshape(zs, shard_rows, 3, hw), (1, 2, 0, 3))
        in_grads[layer] = piece.reshape(shard_rows, 3 * width)
        if fast:
            expert_outs = expert_grads(grad_groups, layer, layers, expert_outs)
        else:
            first_grads[layer] = jnp.stack(g_first)
            second_grads[layer] = jnp.stack(g_second)

    if not fast:
        expert_outs = (jnp.stack(first_grads), jnp.stack(second_grads))
    packed_small = jnp.stack(small_grads, axis=2)
    packed_small = jnp.transpose(packed_small, (1, 0, 2, 3))
    packed_small = jnp.sum(spread(packed_small, "expert"), axis=0)
    packed_small = jnp.sum(spread(packed_small, "seq"), axis=0)
    r_size = shard_rows * experts
    router_grad = packed_small[:, :r_size].reshape(layers, shard_rows, experts)
    ga_grad = packed_small[:, r_size : r_size + shard_rows]
    ge_grad = packed_small[:, r_size + shard_rows : r_size + 2 * shard_rows]
    table_grad = packed_small[:, r_size + 2 * shard_rows :]
    return (
        block_out[None],
        tokens_grad[None],
        jnp.stack(in_grads),
        jnp.stack(out_grads),
        router_grad,
        ga_grad,
        ge_grad,
        table_grad,
        expert_outs[0],
        expert_outs[1],
    )


def solution(mesh):
    both = ("seq", "expert")
    return jax.shard_map(
        body,
        mesh=mesh,
        in_specs=(
            P("expert", "seq", None),
            P("expert", "seq", None),
            P("expert", None),
            P(),
            P("expert", "seq", None),
            P(None, both, None),
            P(None, both, None),
            P(None, both, None),
            P(None, both),
            P(None, both),
            P(None, both),
            P(None, "expert", None, "seq"),
            P(None, "expert", "seq", None),
        ),
        out_specs=(
            P("expert", "seq", None),
            P("expert", "seq", None),
            P(None, both, None),
            P(None, both, None),
            P(None, both, None),
            P(None, both),
            P(None, both),
            P(None, both),
            P(None, "expert", None, "seq"),
            P(None, "expert", "seq", None),
        ),
        check_vma=False,
    )
```
